32 devices in a mesh: ep: 8 (over z, y), dp: 4 (over x, core).
Axes of the slice: x: 2, y: 2, z: 4, core: 2. Of those that a mesh axis runs over, the one named last changes fastest.
Arguments:
- tokens: bfloat16 [1024, 2048], P(('ep', 'dp')), may hold values from -6 to 6
- cotangent: bfloat16 [1024, 2048], P(('ep', 'dp')), may hold values from -6 to 6
- expert_ids: int32 [1024, 8], P(('ep', 'dp')), may hold values from 0 to 7, as said below
- route_weights: bfloat16 [1024, 8], P(('ep', 'dp')), may hold values from 0.049804688 to 0.5
- w_gate: bfloat16 [8, 2048, 768], P('ep'), may hold values from -0.125 to 0.125
- w_up: bfloat16 [8, 2048, 768], P('ep'), may hold values from -0.125 to 0.125
- w_down: bfloat16 [8, 768, 2048], P('ep'), may hold values from -0.21875 to 0.21875
Outputs:
- grad_tokens: bfloat16 [1024, 2048], P(('ep', 'dp'))
- grad_route: bfloat16 [1024, 8], P(('ep', 'dp'))
- grad_gate: bfloat16 [8, 2048, 768], P('ep', 'dp')
- grad_up: bfloat16 [8, 2048, 768], P('ep', 'dp')
- grad_down: bfloat16 [8, 768, 2048], P('ep', None, 'dp')
The draws below stay inside these ranges and needn't reach their ends.
Inputs may be any that keep to these rules, and one draw needn't show every extreme that they name: `expert_ids`: each token names 8 different experts. The tokens of one device name no expert more than 32 times; 1 expert, drawn from the seed, are named exactly 32 times by every device's tokens.
All inputs are finite; a program needn't handle non-finite values.
Results may differ from the reference program's by a relative error of at most 0.0095.
Values may be sent and summed in bfloat16 or wider, within the bound.
A program may use at most 128 MiB of HBM per device.

```python
import math
import jax
import jax.numpy as jnp
from jax import lax

D = 2048
FF = 768
TOPK = 8
TOK_DEV = 32
EXPERTS = 8
CAP = 32
HOT = 1
TOKENS = 1024
N_EP = 8
N_DP = 4


def draw_expert_ids(key, part):
    blocks = TOKENS // TOK_DEV
    half_count = EXPERTS // 2
    hot_key = jax.random.fold_in(key, 11)
    pair_pick = jax.random.permutation(jax.random.fold_in(hot_key, 1), half_count)[:HOT].astype(jnp.int32)
    side_pick = jax.random.randint(jax.random.fold_in(hot_key, 2), (HOT,), 0, 2).astype(jnp.int32)
    hot_ids = pair_pick + side_pick * half_count
    is_hot = jnp.zeros((EXPERTS,), jnp.int32).at[hot_ids].set(1)
    tickets = EXPERTS * CAP
    ticket_owner = jnp.arange(tickets, dtype=jnp.int32) // CAP
    row_total = TOK_DEV * TOPK

    def one_block(index):
        block_key = jax.random.fold_in(jax.random.fold_in(key, 23), index)
        ranking = jax.random.permutation(jax.random.fold_in(block_key, 1), tickets).astype(jnp.int32)
        score = (1 - is_hot[ticket_owner]) * tickets + ranking
        chosen = jnp.argsort(score, stable=True)[:row_total]
        listed = jnp.sort(ticket_owner[chosen])
        slot_pos = jnp.arange(row_total, dtype=jnp.int32)
        token_pos = slot_pos % TOK_DEV
        column_pos = slot_pos // TOK_DEV
        shuffle = jax.random.permutation(jax.random.fold_in(block_key, 2), TOK_DEV).astype(jnp.int32)
        turned = jax.random.randint(jax.random.fold_in(block_key, 3), (TOK_DEV,), 0, TOPK).astype(jnp.int32)
        new_token = shuffle[token_pos]
        new_column = (column_pos + turned[new_token]) % TOPK
        return jnp.zeros((TOK_DEV, TOPK), jnp.int32).at[new_token, new_column].set(listed)
    drawn = lax.map(one_block, jnp.arange(blocks, dtype=jnp.int32))
    return drawn.reshape(TOKENS, TOPK)


def steps_of(rng, extent, split, low, high):
    level, own = 1.0, jax.random.fold_in(rng, 6)
    for position, blocks in split:
        draws = jnp.exp(jax.random.uniform(jax.random.fold_in(own, position), (blocks,), jnp.float32, low / len(split), high / len(split)))
        level = level * jnp.repeat(draws, extent[position] // blocks).reshape([-1 if axis == position else 1 for axis in range(len(extent))])
    return level


def centred(own_key, dims, scale, reach, shards=(), kind=jnp.bfloat16):
    array = scale * jax.random.normal(own_key, dims, jnp.float32)
    if shards:
        array = array * steps_of(own_key, dims, shards, -0.22, 0.18)
    return jnp.clip(array, -reach, reach).astype(kind)


def setup_inputs(seed: int = 0) -> dict:
    streams_of = jax.random.split(jax.random.key(seed), 8)
    tokens = centred(streams_of[0], (TOKENS, D), 1.0, 6.0, ((0, 32),))
    cotangent = centred(streams_of[1], (TOKENS, D), 1.0, 6.0, ((0, 32),))
    expert_ids = draw_expert_ids(jax.random.fold_in(streams_of[7], 71), 0)
    route_weights = jnp.clip(jnp.exp(math.log(0.5) - 2.306499 * jax.random.uniform(streams_of[3], (TOKENS, TOPK), jnp.float32) ** steps_of(streams_of[3], (TOKENS, TOPK), ((0, 32),), -0.2, 0.2)), 0.049804688, 0.5).astype(jnp.bfloat16)
    w_gate = centred(streams_of[4], (EXPERTS, D, FF), D ** -0.5, 0.125, ((0, 8),))
    w_up = centred(streams_of[5], (EXPERTS, D, FF), D ** -0.5, 0.125, ((0, 8),))
    w_down = centred(streams_of[6], (EXPERTS, FF, D), FF ** -0.5, 0.21875, ((0, 8),))
    return {"tokens": tokens, "cotangent": cotangent, "expert_ids": expert_ids, "route_weights": route_weights, "w_gate": w_gate, "w_up": w_up, "w_down": w_down}


contract_last = (((1,), (1,)), ((), ()))
contract_first = (((0,), (0,)), ((), ()))


def silu_parts(gate_pre):
    sig = jax.nn.sigmoid(gate_pre)
    return gate_pre * sig, sig * (1.0 + gate_pre * (1.0 - sig))


def expert_rows(tok_rows, cot_rows, weight, w_gate_one, w_up_one, w_down_one):
    gate_pre = jnp.dot(tok_rows, w_gate_one, preferred_element_type=jnp.float32)
    up_pre = jnp.dot(tok_rows, w_up_one, preferred_element_type=jnp.float32)
    act, slope = silu_parts(gate_pre)
    hidden = lax.optimization_barrier((act * up_pre).astype(jnp.bfloat16))
    back = lax.dot_general(cot_rows, w_down_one, contract_last, preferred_element_type=jnp.float32)
    route_grad = jnp.sum(hidden.astype(jnp.float32) * back, axis=1)
    scaled = weight * back
    grad_gate_pre = (scaled * up_pre * slope).astype(jnp.bfloat16)
    grad_up_pre = (scaled * act).astype(jnp.bfloat16)
    scaled_cot = (weight * cot_rows.astype(jnp.float32)).astype(jnp.bfloat16)
    slot_grad = lax.dot_general(grad_gate_pre, w_gate_one, contract_last, preferred_element_type=jnp.float32)
    slot_grad = slot_grad + lax.dot_general(grad_up_pre, w_up_one, contract_last, preferred_element_type=jnp.float32)
    part_gate = lax.dot_general(tok_rows, grad_gate_pre, contract_first, preferred_element_type=jnp.float32)
    part_up = lax.dot_general(tok_rows, grad_up_pre, contract_first, preferred_element_type=jnp.float32)
    part_down = lax.dot_general(hidden, scaled_cot, contract_first, preferred_element_type=jnp.float32)
    return slot_grad, route_grad, part_gate, part_up, part_down


def reference(tokens, cotangent, expert_ids, route_weights, w_gate, w_up, w_down):
    slots = TOKENS * TOPK
    rows = N_EP * CAP
    flat_ids = expert_ids.reshape(slots)
    flat_w = route_weights.reshape(slots)
    slot_index = jnp.arange(slots, dtype=jnp.int32)
    group_of = (slot_index // (TOK_DEV * TOPK)) % N_DP

    def one_expert(expert):
        w_gate_one = w_gate[expert]
        w_up_one = w_up[expert]
        w_down_one = w_down[expert]
        total_gate = jnp.zeros((D, FF), jnp.float32)
        total_up = jnp.zeros((D, FF), jnp.float32)
        total_down = jnp.zeros((FF, D), jnp.float32)
        slot_list = []
        route_list = []
        target_list = []
        for group in range(N_DP):
            keyed = jnp.where((flat_ids == expert) & (group_of == group), slot_index, slots)
            order = jnp.argsort(keyed, stable=True)[:rows].astype(jnp.int32)
            valid = keyed[order] < slots
            pick = jnp.where(valid, order, 0).astype(jnp.int32)
            mask = valid.astype(tokens.dtype)[:, None]
            tok_rows = tokens[pick // TOPK] * mask
            cot_rows = cotangent[pick // TOPK] * mask
            weight = (flat_w[pick] * valid.astype(flat_w.dtype)).astype(jnp.float32)[:, None]
            result = expert_rows(tok_rows, cot_rows, weight, w_gate_one, w_up_one, w_down_one)
            slot_list.append(result[0].astype(jnp.bfloat16))
            route_list.append(result[1].astype(jnp.bfloat16))
            target_list.append(jnp.where(valid, order, slots).astype(jnp.int32))
            total_gate = total_gate + lax.optimization_barrier(result[2].astype(jnp.bfloat16)).astype(jnp.float32)
            total_up = total_up + lax.optimization_barrier(result[3].astype(jnp.bfloat16)).astype(jnp.float32)
            total_down = total_down + lax.optimization_barrier(result[4].astype(jnp.bfloat16)).astype(jnp.float32)
        return (jnp.stack(slot_list), jnp.stack(route_list), jnp.stack(target_list),
                total_gate.astype(jnp.bfloat16), total_up.astype(jnp.bfloat16), total_down.astype(jnp.bfloat16))

    outs = lax.map(one_expert, jnp.arange(EXPERTS, dtype=jnp.int32))
    targets = outs[2].reshape(-1)
    placed = jnp.zeros((slots + 1, D), jnp.float32).at[targets].set(outs[0].reshape(-1, D).astype(jnp.float32))[:slots]
    grad_tokens = jnp.sum(placed.reshape(TOKENS, TOPK, D), axis=1).astype(jnp.bfloat16)
    grad_route = jnp.zeros((slots + 1,), jnp.bfloat16).at[targets].set(outs[1].reshape(-1))[:slots].reshape(TOKENS, TOPK)
    return grad_tokens, grad_route, outs[3], outs[4], outs[5]
```

```python
import jax
import jax.numpy as jnp
from jax import lax
from jax.experimental import pallas as pl
from jax.experimental.pallas import tpu as pltpu
from jax.sharding import PartitionSpec as P

block_rows = 128
contract_last = (((1,), (1,)), ((), ()))
contract_first = (((0,), (0,)), ((), ()))


def silu_parts(gate_pre):
    sig = jax.nn.sigmoid(gate_pre)
    return (gate_pre * sig, sig * (1.0 + gate_pre * (1.0 - sig)))


def expert_pass(rows_x, rows_cot, rows_w, live_count, w_gate_one, w_up_one, w_down_one):
    total, model = rows_x.shape
    width = w_gate_one.shape[1]

    def step(index, carry):
        acc_gate, acc_up, acc_down, slot_grad, route_grad = carry
        start = index * block_rows
        tok = lax.dynamic_slice_in_dim(rows_x, start, block_rows, 0)
        cot = lax.dynamic_slice_in_dim(rows_cot, start, block_rows, 0)
        weight = lax.dynamic_slice_in_dim(rows_w, start, block_rows, 0).astype(jnp.float32)[:, None]
        gate_pre = jnp.dot(tok, w_gate_one, preferred_element_type=jnp.float32)
        up_pre = jnp.dot(tok, w_up_one, preferred_element_type=jnp.float32)
        act, slope = silu_parts(gate_pre)
        hidden = lax.optimization_barrier((act * up_pre).astype(jnp.bfloat16))
        back = lax.dot_general(cot, w_down_one, contract_last, preferred_element_type=jnp.float32)
        route_part = jnp.sum(hidden.astype(jnp.float32) * back, axis=1)
        scaled = weight * back
        grad_gate_pre = (scaled * up_pre * slope).astype(jnp.bfloat16)
        grad_up_pre = (scaled * act).astype(jnp.bfloat16)
        scaled_cot = (weight * cot.astype(jnp.float32)).astype(jnp.bfloat16)
        part = lax.dot_general(
            grad_gate_pre, w_gate_one, contract_last, preferred_element_type=jnp.float32
        )
        part = part + lax.dot_general(
            grad_up_pre, w_up_one, contract_last, preferred_element_type=jnp.float32
        )
        acc_gate = acc_gate + lax.dot_general(
            tok, grad_gate_pre, contract_first, preferred_element_type=jnp.float32
        )
        acc_up = acc_up + lax.dot_general(
            tok, grad_up_pre, contract_first, preferred_element_type=jnp.float32
        )
        acc_down = acc_down + lax.dot_general(
            hidden, scaled_cot, contract_first, preferred_element_type=jnp.float32
        )
        slot_grad = lax.dynamic_update_slice_in_dim(slot_grad, part, start, 0)
        route_grad = lax.dynamic_update_slice_in_dim(route_grad, route_part, start, 0)
        return (acc_gate, acc_up, acc_down, slot_grad, route_grad)

    init = (
        jnp.zeros((model, width), jnp.float32),
        jnp.zeros((model, width), jnp.float32),
        jnp.zeros((width, model), jnp.float32),
        jnp.zeros((total, model), jnp.float32),
        jnp.zeros((total,), jnp.float32),
    )
    block_count = (live_count + block_rows - 1) // block_rows
    return lax.fori_loop(0, block_count, step, init)


def routed_body(tokens, cotangent, expert_ids, route_weights, w_gate, w_up, w_down):
    tok_count, topk = expert_ids.shape
    model = tokens.shape[1]
    experts = lax.axis_size("ep")
    capacity = min(tok_count, 2 * tok_count * topk // experts)
    slots = tok_count * topk
    row_total = experts * capacity
    flat_ids = expert_ids.reshape(slots)
    onehot = (flat_ids[:, None] == jnp.arange(experts, dtype=jnp.int32)[None, :]).astype(jnp.int32)
    position = jnp.sum((jnp.cumsum(onehot, axis=0) - 1) * onehot, axis=1)
    slot_ids = jnp.arange(slots, dtype=jnp.int32)
    source = (
        jnp.full((row_total,), slots, jnp.int32).at[flat_ids * capacity + position].set(slot_ids)
    )
    filled = source < slots
    source_token = jnp.where(filled, source // topk, tok_count)
    joined = jnp.concatenate([tokens, cotangent], axis=1)
    picked = jnp.take(joined, source_token, axis=0, mode="fill", fill_value=0)
    send_x = picked[:, :model].reshape(experts, capacity, model)
    send_cot = picked[:, model:].reshape(experts, capacity, model)
    send_w = jnp.take(
        route_weights.reshape(slots), jnp.where(filled, source, slots), mode="fill", fill_value=0
    ).reshape(experts, capacity)
    recv_x, recv_cot, recv_w = (
        lax.all_to_all(send_x, "ep", split_axis=0, concat_axis=0, tiled=True),
        lax.all_to_all(send_cot, "ep", split_axis=0, concat_axis=0, tiled=True),
        lax.all_to_all(send_w, "ep", split_axis=0, concat_axis=0, tiled=True),
    )
    flat_w = recv_w.reshape(row_total)
    live = (flat_w != 0).astype(jnp.int32)
    live_count = jnp.sum(live)
    place = jnp.where(live > 0, jnp.cumsum(live) - 1, row_total)
    anchor = (
        jnp.full((row_total,), row_total, jnp.int32)
        .at[place]
        .set(jnp.arange(row_total, dtype=jnp.int32), mode="drop")
    )
    recv_joined = jnp.concatenate(
        [recv_x.reshape(row_total, model), recv_cot.reshape(row_total, model)], axis=1
    )
    packed = jnp.take(recv_joined, anchor, axis=0, mode="fill", fill_value=0)
    pack_x = packed[:, :model]
    pack_cot = packed[:, model:]
    pack_w = jnp.take(flat_w, anchor, mode="fill", fill_value=0)
    w_gate_one = w_gate[0]
    w_up_one = w_up[0]
    w_down_one = w_down[0]
    acc_gate, acc_up, acc_down, slot_grad, route_grad = expert_pass(
        pack_x, pack_cot, pack_w, live_count, w_gate_one, w_up_one, w_down_one
    )
    slot_rows = jnp.take(slot_grad, place, axis=0, mode="fill", fill_value=0.0).astype(jnp.bfloat16)
    route_rows = jnp.take(route_grad, place, axis=0, mode="fill", fill_value=0.0).astype(
        jnp.bfloat16
    )
    back_x, back_route_rows = (
        lax.all_to_all(
            slot_rows.reshape(experts, capacity, model),
            "ep",
            split_axis=0,
            concat_axis=0,
            tiled=True,
        ),
        lax.all_to_all(
            route_rows.reshape(experts, capacity), "ep", split_axis=0, concat_axis=0, tiled=True
        ),
    )
    mine_rows = back_x[flat_ids, position].reshape(tok_count, topk, model)
    grad_tokens = jnp.sum(mine_rows.astype(jnp.float32), axis=1).astype(jnp.bfloat16)
    grad_route = back_route_rows[flat_ids, position].reshape(tok_count, topk)
    summed = (
        lax.psum_scatter(
            acc_gate[None].astype(jnp.bfloat16), "dp", scatter_dimension=1, tiled=True
        ).astype(jnp.float32),
        lax.psum_scatter(
            acc_up[None].astype(jnp.bfloat16), "dp", scatter_dimension=1, tiled=True
        ).astype(jnp.float32),
        lax.psum_scatter(
            acc_down[None].astype(jnp.bfloat16), "dp", scatter_dimension=2, tiled=True
        ).astype(jnp.float32),
    )
    return (
        grad_tokens,
        grad_route,
        summed[0].astype(jnp.bfloat16),
        summed[1].astype(jnp.bfloat16),
        summed[2].astype(jnp.bfloat16),
    )


def fused_kernel(
    tok_hbm, cot_hbm, ids_hbm, rw_hbm, wg_hbm, wu_hbm, wdn_hbm,
    gt_ref, route_ref, gg_ref, gu_ref, gd_ref,
    ids_ref, rw_ref, wg, wu, wdn, tc, wd, wbuf, wcol, cols, colst, act_buf, fac_buf, hid_buf,
    hw_own, hw_recv, gp_own, gp_recv, part, ys, yr, zs, zr, xs, xr, rs, rr,
    l_sem, w_sem, g_send, g_recv, c_send, c_recv, h_send, h_done, y_sem, z_sem, x_sem, r_sem,
):
    ep_size = lax.axis_size("ep")
    groups = lax.axis_size("dp")
    count = tok_hbm.shape[0]
    col = tc.shape[3]
    tiles, rows, ft = hw_own.shape
    half = rows // 2
    ep = lax.axis_index("ep")
    dp = lax.axis_index("dp")
    z, y = ep // 2, ep % 2
    q, i = z // 2, z % 2
    xx, core = dp // 2, dp % 2
    peers_dp = (xx * 2 + 1 - core, (1 - xx) * 2 + core, (1 - xx) * 2 + 1 - core)
    inner = i != q
    outer = i == q
    zp = z + 1 - 2 * i
    ynb = z * 2 + 1 - y
    znb = zp * 2 + y
    diag = zp * 2 + 1 - y
    near = (2 - q) * 2 + y
    far = (3 - 3 * q) * 2 + y
    near_o = (2 - q) * 2 + 1 - y
    far_o = (3 - 3 * q) * 2 + 1 - y
    twin = (ep + 4) % 8
    pairs = (q, 1 - q)
    f32 = jnp.float32
    bf16 = jnp.bfloat16
    first = 1

    def span(index, size):
        return pl.ds(pl.multiple_of(index * size, size), size)

    def remote(src, dst, send, recv, ep_to, dp_to):
        return pltpu.make_async_remote_copy(
            src_ref=src, dst_ref=dst, send_sem=send, recv_sem=recv,
            device_id=(ep_to, dp_to), device_id_type=pl.DeviceIdType.MESH,
        )

    loads = [
        [
            pltpu.make_async_copy(ref.at[:, pl.ds(j * col, col)], tc.at[k, j, span(ep, count)], l_sem.at[k])
            for j in range(groups)
        ]
        for k, ref in enumerate((tok_hbm, cot_hbm))
    ]
    for group in loads:
        for load in group:
            load.start()
    lists = (
        pltpu.make_async_copy(ids_hbm, ids_ref, l_sem.at[2]),
        pltpu.make_async_copy(rw_hbm, rw_ref, l_sem.at[3]),
    )
    for load in lists:
        load.start()
    w_loads = [
        pltpu.make_async_copy(src, dst, l_sem.at[4 + k])
        for k, (src, dst) in enumerate(((wg_hbm, wg), (wu_hbm, wu), (wdn_hbm, wdn)))
    ]

    barrier = pltpu.get_barrier_semaphore()
    for k in range(1, ep_size):
        pl.semaphore_signal(
            barrier, inc=1, device_id=((ep + k) % ep_size, dp), device_id_type=pl.DeviceIdType.MESH
        )
    for peer in peers_dp:
        pl.semaphore_signal(barrier, inc=1, device_id=(ep, peer), device_id_type=pl.DeviceIdType.MESH)
    wd[...] = jnp.zeros(wd.shape, f32)
    rs[...] = jnp.zeros(rs.shape, f32)
    for load in lists:
        load.wait()
    ids = ids_ref[...]
    values = rw_ref[...].astype(f32)
    for e in range(ep_size):
        line = jnp.sum(jnp.where(ids == e, values, 0.0), axis=0, keepdims=True)
        wd[e, :, 0:count] = jnp.broadcast_to(line, (wd.shape[1], count))
    pl.semaphore_wait(barrier, ep_size - 1 + len(peers_dp))

    def view(k, pos, piece):
        if k == 2:
            return cols.at[1, pl.ds((1, 1, 2)[piece], (2, 1, 1)[piece]), span(pos, count)]
        return tc.at[k, pl.ds((0, 0, first)[piece], (groups, first, groups - first)[piece]), span(pos, count)]

    def hop(k, pos, piece, late, ep_to):
        ref = view(k, pos, piece)
        slot = ep_to if piece == 2 else pos
        remote(ref, ref, g_send.at[k, late], g_recv.at[k, slot], ep_to, dp).start()

    def got(k, pos):
        ref = view(k, pos, 0)
        remote(ref, ref, g_send.at[k, 0], g_recv.at[k, pos], ynb, dp).wait_recv()

    def got_diag(k):
        ref = view(k, diag, 1)
        remote(ref, ref, g_send.at[k, 0], g_recv.at[k, diag], ynb, dp).wait_recv()
        ref = view(k, diag, 2)
        remote(ref, ref, g_send.at[k, 0], g_recv.at[k, ep], znb, dp).wait_recv()

    def send_cols(k, pos, reach):
        for r in (1, 2, 0)[3 - reach:] if reach == 3 else (0,):
            peer = peers_dp[r]
            remote(
                tc.at[k, peer, span(pos, count)], cols.at[k, r, span(pos, count)],
                c_send.at[k, r], c_recv.at[k, r], ep, peer,
            ).start()

    def share(k, pos):
        if k < 2:
            send_cols(k, pos, 3 - 2 * k)

    def own_out(k):
        hop(k, ep, 0, 0, ynb)
        hop(k, ep, 0, 0, znb)

        @pl.when(inner)
        def _():
            hop(k, ep, 0, 1, near)

    def pair_out(k):
        got(k, znb)
        hop(k, znb, 1, 0, ynb)

        @pl.when(inner)
        def _():
            hop(k, znb, 0, 1, near)

        share(k, znb)
        got(k, ynb)
        hop(k, ynb, 2, 0, znb)
        share(k, ynb)

    def inner_pass(k, pos):
        @pl.when(inner)
        def _():
            got(k, pos)
            hop(k, pos, 0, 1, znb)
            hop(k, pos, 0, 1, ynb)
            share(k, pos)

    def outer_pass(k, pos):
        @pl.when(outer)
        def _():
            got(k, pos)
            hop(k, pos, 0, 1, ynb)
            share(k, pos)

    def take(k, pos):
        got(k, pos)
        share(k, pos)

    for k in range(2):
        ref = view(k, ep, 0)
        pltpu.make_async_copy(ref, ref, l_sem.at[k]).wait()
        own_out(k)
        send_cols(k, ep, 3)
    for k in range(1, ep_size):
        to = (ep + k) % ep_size
        remote(wd.at[to], wbuf.at[ep], w_sem.at[0], w_sem.at[1], to, dp).start()
    keep_w = pltpu.make_async_copy(wd.at[ep], wbuf.at[ep], w_sem.at[1])
    keep_w.start()
    for load in w_loads:
        load.start()
    pair_out(0)
    pair_out(1)

    def wave_rows(wave):
        return span(pairs[wave], half)

    def gate_step(wave):
        block = wave_rows(wave)

        def step(t, carry):
            lanes = span(t, ft)
            gate_pre = jnp.zeros((half, ft), f32)
            up_pre = jnp.zeros((half, ft), f32)
            for j in range(groups):
                depth = pl.ds(j * col, col)
                gate_pre += jnp.dot(tc[0, j, block], wg[depth, lanes], preferred_element_type=f32)
                up_pre += jnp.dot(tc[0, j, block], wu[depth, lanes], preferred_element_type=f32)
            act, slope = silu_parts(gate_pre)
            product = act * up_pre
            weight = wcol[block, 0:1]
            hw_own[t, block] = (weight * product).astype(bf16)
            act_buf[t, block] = act
            fac_buf[t, block] = up_pre * slope
            hid_buf[t, block] = product.astype(bf16)
            for r in (1, 0):
                done = h_done.at[1 + wave] if r == 1 else h_done.at[0]
                remote(
                    hw_own.at[t, block], hw_recv.at[r, t, block], h_send.at[0, r], done, ep, peers_dp[r]
                ).start()
            return carry

        lax.fori_loop(0, tiles, step, 0)

    def back_step(wave):
        block = wave_rows(wave)
        weight = wcol[block, 0:1]

        def step(t, route):
            back = jnp.zeros((half, ft), f32)
            for j in range(groups):
                back += lax.dot_general(
                    tc[1, j, block], wdn[span(t, ft), pl.ds(j * col, col)], contract_last, preferred_element_type=f32
                )
            scaled = weight * back
            gp_own[t, 0, block] = (scaled * fac_buf[t, block]).astype(bf16)
            gp_own[t, 1, block] = (scaled * act_buf[t, block]).astype(bf16)
            route = route + jnp.sum(hid_buf[t, block].astype(f32) * back, axis=1, keepdims=True)
            for r in (1, 0):
                done = h_done.at[(5 + wave) + wave * t] if r == 1 else h_done.at[4]
                remote(
                    gp_own.at[t, :, block], gp_recv.at[r, t, :, block], h_send.at[1, r], done, ep, peers_dp[r]
                ).start()
            return route

        route = lax.fori_loop(0, tiles, step, jnp.zeros((half, 1), f32))
        lined = jnp.broadcast_to(route, (half, 128)).T
        for p in range(4):
            line = lined[0:1, p * count:(p + 1) * count]
            rs[pairs[wave] * 4 + p, :, 0:count] = jnp.broadcast_to(line, (rs.shape[1], count))

    def y_copy(wave, n):
        done = y_sem.at[1 + wave * (1 + n)]
        return remote(ys.at[wave, n], yr.at[wave, n], y_sem.at[0], done, ynb, dp)

    def slot_step(wave, sending):
        block = wave_rows(wave)

        def step(n, carry):
            total = jnp.zeros((half, col), f32)
            for t in range(tiles):
                lanes = pl.ds(t * ft, ft)
                total += lax.dot_general(
                    gp_own[t, 0, block], wg[span(n, col), lanes], contract_last, preferred_element_type=f32
                )
                total += lax.dot_general(
                    gp_own[t, 1, block], wu[span(n, col), lanes], contract_last, preferred_element_type=f32
                )
            part[wave, n] = total.reshape(2, 2, count, col)
            ys[wave, n] = part[wave, n, :, 1 - y].astype(bf16)
            if sending is None:
                y_copy(wave, n).start()
            else:
                @pl.when(sending)
                def _():
                    y_copy(wave, n).start()
            return carry

        lax.fori_loop(0, groups, step, 0)

    def y_add(wave):
        if wave == 0:
            remote(ys.at[0], yr.at[0], y_sem.at[0], y_sem.at[1], ynb, dp).wait_recv()

        def step(n, carry):
            if wave == 1:
                y_copy(1, n).wait_recv()
            total = part[wave, n, :, y] + yr[wave, n].astype(f32)
            part[wave, n, :, y] = total
            zs[wave, n] = part[wave, n, 1 - i, y].astype(bf16)
            remote(
                zs.at[wave, n], zr.at[wave, n], z_sem.at[0], z_sem.at[1 + wave * (1 + n)], znb, dp
            ).start()
            return carry

        lax.fori_loop(0, groups, step, 0)

    def z_add(wave):
        if wave == 0:
            remote(zs.at[0], zr.at[0], z_sem.at[0], z_sem.at[1], znb, dp).wait_recv()

        def step(n, carry):
            if wave == 1:
                remote(zs.at[1, n], zr.at[1, n], z_sem.at[0], z_sem.at[2 + n], znb, dp).wait_recv()
            total = part[wave, n, i, y] + zr[wave, n].astype(f32)
            if wave == 0:
                part[0, n, i, y] = total
            else:
                xs[n] = total.astype(bf16)
                remote(xs.at[n], xr.at[n], x_sem.at[0], x_sem.at[1 + n], twin, dp).start()
            return carry

        lax.fori_loop(0, groups, step, 0)

    def pass_hidden(wave):
        block = wave_rows(wave)
        ref = hw_recv.at[1, :, block]
        remote(ref, ref, h_send.at[0, 1], h_done.at[1 + wave], ep, peers_dp[1]).wait_recv()
        remote(ref, hw_recv.at[2, :, block], h_send.at[0, 2], h_done.at[3], ep, peers_dp[0]).start()

    def pass_grad_first():
        ref = gp_recv.at[1, :, :, wave_rows(0)]
        remote(ref, ref, h_send.at[1, 1], h_done.at[5], ep, peers_dp[1]).wait_recv()
        remote(ref, gp_recv.at[2, :, :, wave_rows(0)], h_send.at[1, 2], h_done.at[6 + tiles], ep, peers_dp[0]).start()

    def pass_grad(t):
        ref = gp_recv.at[1, t, :, wave_rows(1)]
        remote(ref, ref, h_send.at[1, 1], h_done.at[6 + t], ep, peers_dp[1]).wait_recv()
        remote(
            ref, gp_recv.at[2, t, :, wave_rows(1)], h_send.at[1, 2], h_done.at[7 + tiles + t], ep, peers_dp[0]
        ).start()

    got_diag(0)
    share(0, diag)
    for load in w_loads:
        load.wait()
    remote(wbuf, wbuf, w_sem.at[0], w_sem.at[1], ynb, dp).wait_recv()
    flat = wbuf[...].reshape(ep_size * wbuf.shape[1], wbuf.shape[2])
    turned = jnp.concatenate([flat] * (128 // flat.shape[0]), axis=0).T
    step8 = wbuf.shape[1]
    for p in range(ep_size):
        wcol[pl.ds(p * count, count), :] = jnp.broadcast_to(turned[0:count, p * step8:p * step8 + 1], (count, 128))
    gate_step(0)
    inner_pass(0, near)
    inner_pass(0, far)
    inner_pass(1, near)
    got_diag(1)
    share(1, diag)
    back_step(0)
    inner_pass(1, far)
    for r in (1, 2):
        ref = cols.at[1, r, span(ep, count)]
        remote(ref, ref, c_send.at[1, r], c_recv.at[1, r], ep, peers_dp[r]).wait_recv()
    own_out(2)
    slot_step(0, inner)
    outer_pass(0, near)
    outer_pass(0, far)
    take(0, near_o)
    take(0, far_o)
    outer_pass(1, near)
    gate_step(1)
    outer_pass(1, far)

    @pl.when(outer)
    def _():
        def step(n, carry):
            y_copy(0, n).start()
            return carry

        lax.fori_loop(0, groups, step, 0)

    pass_hidden(0)
    pair_out(2)
    take(1, near_o)
    take(1, far_o)
    back_step(1)
    inner_pass(2, near)
    inner_pass(2, far)
    slot_step(1, None)
    pass_grad_first()
    y_add(0)
    outer_pass(2, near)
    outer_pass(2, far)
    for k in range(1, ep_size):
        to = (ep + k) % ep_size
        remote(rs.at[to], rr.at[ep], r_sem.at[0], r_sem.at[1], to, dp).start()
    pltpu.make_async_copy(rs.at[ep], rr.at[ep], r_sem.at[1]).start()
    pass_hidden(1)
    colst[0] = tc[0, dp].T
    for r in range(3):
        remote(cols.at[0, r], cols.at[0, r], c_send.at[0, r], c_recv.at[0, r], ep, peers_dp[r]).wait_recv()
        colst[1 + r] = cols[0, r].T
    y_add(1)
    z_add(0)
    remote(cols.at[1, 0], cols.at[1, 0], c_send.at[1, 0], c_recv.at[1, 0], ep, peers_dp[0]).wait_recv()
    got_diag(2)
    got(2, near_o)
    got(2, far_o)
    remote(hw_recv.at[0], hw_recv.at[0], h_send.at[0, 0], h_done.at[0], ep, peers_dp[0]).wait_recv()
    remote(hw_recv.at[2], hw_recv.at[2], h_send.at[0, 2], h_done.at[3], ep, peers_dp[0]).wait_recv()

    def down_step(t, carry):
        blocks = [hw_own.at[t]] + [hw_recv.at[r, t] for r in range(3)]
        cots = [tc.at[1, dp]] + [cols.at[1, r] for r in range(3)]
        grad_down = jnp.zeros((ft, col), f32)
        for g in range(4):
            grad_down += lax.dot_general(blocks[g][...], cots[g][...], contract_first, preferred_element_type=f32)
        gd_ref[span(t, ft), :] = grad_down.astype(bf16)
        return carry

    lax.fori_loop(0, tiles, down_step, 0)
    z_add(1)
    remote(gp_recv.at[0], gp_recv.at[0], h_send.at[1, 0], h_done.at[4], ep, peers_dp[0]).wait_recv()
    ref = gp_recv.at[2, :, :, wave_rows(0)]
    remote(ref, ref, h_send.at[1, 2], h_done.at[6 + tiles], ep, peers_dp[0]).wait_recv()
    pass_grad(0)

    def sum_step(n, carry):
        remote(xs.at[n], xr.at[n], x_sem.at[0], x_sem.at[1 + n], twin, dp).wait_recv()
        gt_ref[:, span(n, col)] = (part[0, n, i, y] + xr[n].astype(f32)).astype(bf16)
        return carry

    def weight_step(t, carry):
        @pl.when(t + 1 < tiles)
        def _():
            pass_grad(t + 1)

        @pl.when(t + 1 == tiles)
        def _():
            lax.fori_loop(0, groups, sum_step, 0)

        ref = gp_recv.at[2, t, :, wave_rows(1)]
        remote(ref, ref, h_send.at[1, 2], h_done.at[7 + tiles + t], ep, peers_dp[0]).wait_recv()
        blocks = [gp_own.at[t]] + [gp_recv.at[r, t] for r in range(3)]
        grad_gate = jnp.zeros((col, ft), f32)
        grad_up = jnp.zeros((col, ft), f32)
        for g in range(4):
            grad_gate += jnp.dot(colst[g], blocks[g][0], preferred_element_type=f32)
            grad_up += jnp.dot(colst[g], blocks[g][1], preferred_element_type=f32)
        gg_ref[:, span(t, ft)] = grad_gate.astype(bf16)
        gu_ref[:, span(t, ft)] = grad_up.astype(bf16)
        return carry

    lax.fori_loop(0, tiles, weight_step, 0)

    remote(rr, rr, r_sem.at[0], r_sem.at[1], ynb, dp).wait_recv()
    table = jnp.zeros(ids.shape, f32)
    for e in range(ep_size):
        table = table + jnp.where(ids == e, rr[e, 0:1, 0:count], 0.0)
    route_ref[...] = table.astype(bf16)

    def sent(ref, sem):
        remote(ref, ref, sem, r_sem.at[1], ynb, dp).wait_send()

    sent(rs.at[pl.ds(0, ep_size - 1)], r_sem.at[0])
    sent(wd.at[pl.ds(0, ep_size - 1)], w_sem.at[0])
    sent(ys, y_sem.at[0])
    sent(zs, z_sem.at[0])
    sent(xs, x_sem.at[0])
    for k in range(3):
        def whole(n):
            return cols.at[1, pl.ds(1, 2), pl.ds(0, n * count)] if k == 2 else tc.at[k, :, pl.ds(0, n * count)]

        sent(whole(3), g_send.at[k, 0])

        @pl.when(inner)
        def _():
            sent(whole(6), g_send.at[k, 1])

        @pl.when(outer)
        def _():
            sent(whole(2), g_send.at[k, 1])

    for k in range(2):
        for r in range(3):
            sent(cols.at[1, r, pl.ds(0, count)] if k == 1 and r > 0 else cols.at[k, r], c_send.at[k, r])
            sent((hw_recv, gp_recv)[k].at[r], h_send.at[k, r])


def store_kernel(*refs):
    sems = refs[-1]
    each = (len(refs) - 1) // 2
    copies = [pltpu.make_async_copy(refs[k], refs[each + k], sems.at[k]) for k in range(each)]
    for copy in copies:
        copy.start()
    for copy in copies:
        copy.wait()


def fused_body(tokens, cotangent, expert_ids, route_weights, w_gate, w_up, w_down):
    count, topk = expert_ids.shape
    model = tokens.shape[1]
    experts = lax.axis_size("ep")
    groups = lax.axis_size("dp")
    width = w_gate.shape[2]
    rows = experts * count
    col = model // groups
    ft = 256 if width % 256 == 0 else width
    tiles = width // ft
    lanes = 128
    bf16 = jnp.bfloat16
    f32 = jnp.float32
    any_spec = pl.BlockSpec(memory_space=pl.ANY)
    hbm = pl.BlockSpec(memory_space=pltpu.HBM)
    vmem = pl.BlockSpec(memory_space=pltpu.VMEM)
    dma = pltpu.SemaphoreType.DMA
    small = (experts, 8, lanes)
    shapes = ((count, model), (topk, count), (col, width), (col, width), (width, col))
    outs = pl.pallas_call(
        fused_kernel,
        name="fused_layer",
        out_shape=tuple(pltpu.VMEM(shape, bf16) for shape in shapes),
        in_specs=[hbm] * 7,
        out_specs=(vmem,) * 5,
        scratch_shapes=[
            pltpu.VMEM((topk, count), jnp.int32),
            pltpu.VMEM((topk, count), bf16),
            pltpu.VMEM((model, width), bf16),
            pltpu.VMEM((model, width), bf16),
            pltpu.VMEM((width, model), bf16),
            pltpu.VMEM((2, groups, rows, col), bf16),
            pltpu.VMEM(small, f32),
            pltpu.VMEM(small, f32),
            pltpu.VMEM((rows, lanes), f32),
            pltpu.VMEM((2, 3, rows, col), bf16),
            pltpu.VMEM((4, col, rows), bf16),
            pltpu.VMEM((tiles, rows, ft), f32),
            pltpu.VMEM((tiles, rows, ft), f32),
            pltpu.VMEM((tiles, rows, ft), bf16),
            pltpu.VMEM((tiles, rows, ft), bf16),
            pltpu.VMEM((3, tiles, rows, ft), bf16),
            pltpu.VMEM((tiles, 2, rows, ft), bf16),
            pltpu.VMEM((3, tiles, 2, rows, ft), bf16),
            pltpu.VMEM((2, groups, 2, 2, count, col), f32),
            pltpu.VMEM((2, groups, 2, count, col), bf16),
            pltpu.VMEM((2, groups, 2, count, col), bf16),
            pltpu.VMEM((2, groups, count, col), bf16),
            pltpu.VMEM((2, groups, count, col), bf16),
            pltpu.VMEM((groups, count, col), bf16),
            pltpu.VMEM((groups, count, col), bf16),
            pltpu.VMEM(small, f32),
            pltpu.VMEM(small, f32),
            dma((7,)),
            dma((2,)),
            dma((3, 2)),
            dma((3, experts)),
            dma((2, 3)),
            dma((2, 3)),
            dma((2, 3)),
            dma((7 + 2 * tiles,)),
            dma((2 + groups,)),
            dma((2 + groups,)),
            dma((1 + groups,)),
            dma((2,)),
        ],
        compiler_params=pltpu.CompilerParams(
            collective_id=0, has_side_effects=True, vmem_limit_bytes=64200000
        ),
    )(tokens, cotangent, expert_ids.T, route_weights.T, w_gate[0], w_up[0], w_down[0])
    outs = pl.pallas_call(
        store_kernel,
        name="store_results",
        out_shape=tuple(jax.ShapeDtypeStruct(shape, bf16) for shape in shapes),
        in_specs=[any_spec] * 5,
        out_specs=(any_spec,) * 5,
        scratch_shapes=[dma((5,))],
        compiler_params=pltpu.CompilerParams(vmem_limit_bytes=4 * 1024 * 1024),
    )(*outs)
    grad_tokens, grad_route, grad_gate, grad_up, grad_down = outs
    return grad_tokens, grad_route.T, grad_gate[None], grad_up[None], grad_down[None]


def body(tokens, cotangent, expert_ids, route_weights, w_gate, w_up, w_down):
    tok_count, topk = expert_ids.shape
    experts = lax.axis_size("ep")
    whole = 2 * tok_count * topk // experts >= tok_count
    paired = lax.axis_size("dp") == 4 and experts == 8 and tok_count in (32, 64)
    chosen = fused_body if whole and paired else routed_body
    return chosen(tokens, cotangent, expert_ids, route_weights, w_gate, w_up, w_down)


def solution(mesh):
    return jax.shard_map(
        body,
        mesh=mesh,
        in_specs=(
            P(("ep", "dp"), None),
            P(("ep", "dp"), None),
            P(("ep", "dp"), None),
            P(("ep", "dp"), None),
            P("ep", None, None),
            P("ep", None, None),
            P("ep", None, None),
        ),
        out_specs=(
            P(("ep", "dp"), None),
            P(("ep", "dp"), None),
            P("ep", "dp", None),
            P("ep", "dp", None),
            P("ep", None, "dp"),
        ),
        check_vma=False,
    )
```

```python
import jax
import jax.numpy as jnp
from jax import lax
from jax.experimental import pallas as pl
from jax.experimental.pallas import tpu as pltpu
from jax.sharding import PartitionSpec as P

block_rows = 128
lead = 3
contract_last = (((1,), (1,)), ((), ()))
contract_first = (((0,), (0,)), ((), ()))


def silu_parts(gate_pre):
    sig = jax.nn.sigmoid(gate_pre)
    return (gate_pre * sig, sig * (1.0 + gate_pre * (1.0 - sig)))


def expert_pass(rows_x, rows_cot, rows_w, live_count, w_gate_one, w_up_one, w_down_one):
    total, model = rows_x.shape
    width = w_gate_one.shape[1]

    def step(index, carry):
        acc_gate, acc_up, acc_down, slot_grad, route_grad = carry
        start = index * block_rows
        tok = lax.dynamic_slice_in_dim(rows_x, start, block_rows, 0)
        cot = lax.dynamic_slice_in_dim(rows_cot, start, block_rows, 0)
        weight = lax.dynamic_slice_in_dim(rows_w, start, block_rows, 0).astype(jnp.float32)[:, None]
        gate_pre = jnp.dot(tok, w_gate_one, preferred_element_type=jnp.float32)
        up_pre = jnp.dot(tok, w_up_one, preferred_element_type=jnp.float32)
        act, slope = silu_parts(gate_pre)
        hidden = lax.optimization_barrier((act * up_pre).astype(jnp.bfloat16))
        back = lax.dot_general(cot, w_down_one, contract_last, preferred_element_type=jnp.float32)
        route_part = jnp.sum(hidden.astype(jnp.float32) * back, axis=1)
        scaled = weight * back
        grad_gate_pre = (scaled * up_pre * slope).astype(jnp.bfloat16)
        grad_up_pre = (scaled * act).astype(jnp.bfloat16)
        scaled_cot = (weight * cot.astype(jnp.float32)).astype(jnp.bfloat16)
        part = lax.dot_general(
            grad_gate_pre, w_gate_one, contract_last, preferred_element_type=jnp.float32
        )
        part = part + lax.dot_general(
            grad_up_pre, w_up_one, contract_last, preferred_element_type=jnp.float32
        )
        acc_gate = acc_gate + lax.dot_general(
            tok, grad_gate_pre, contract_first, preferred_element_type=jnp.float32
        )
        acc_up = acc_up + lax.dot_general(
            tok, grad_up_pre, contract_first, preferred_element_type=jnp.float32
        )
        acc_down = acc_down + lax.dot_general(
            hidden, scaled_cot, contract_first, preferred_element_type=jnp.float32
        )
        slot_grad = lax.dynamic_update_slice_in_dim(slot_grad, part, start, 0)
        route_grad = lax.dynamic_update_slice_in_dim(route_grad, route_part, start, 0)
        return (acc_gate, acc_up, acc_down, slot_grad, route_grad)

    init = (
        jnp.zeros((model, width), jnp.float32),
        jnp.zeros((model, width), jnp.float32),
        jnp.zeros((width, model), jnp.float32),
        jnp.zeros((total, model), jnp.float32),
        jnp.zeros((total,), jnp.float32),
    )
    block_count = (live_count + block_rows - 1) // block_rows
    return lax.fori_loop(0, block_count, step, init)


def routed_body(tokens, cotangent, expert_ids, route_weights, w_gate, w_up, w_down):
    tok_count, topk = expert_ids.shape
    model = tokens.shape[1]
    experts = lax.axis_size("ep")
    capacity = min(tok_count, 2 * tok_count * topk // experts)
    slots = tok_count * topk
    row_total = experts * capacity
    flat_ids = expert_ids.reshape(slots)
    onehot = (flat_ids[:, None] == jnp.arange(experts, dtype=jnp.int32)[None, :]).astype(jnp.int32)
    position = jnp.sum((jnp.cumsum(onehot, axis=0) - 1) * onehot, axis=1)
    slot_ids = jnp.arange(slots, dtype=jnp.int32)
    source = (
        jnp.full((row_total,), slots, jnp.int32).at[flat_ids * capacity + position].set(slot_ids)
    )
    filled = source < slots
    source_token = jnp.where(filled, source // topk, tok_count)
    joined = jnp.concatenate([tokens, cotangent], axis=1)
    picked = jnp.take(joined, source_token, axis=0, mode="fill", fill_value=0)
    send_x = picked[:, :model].reshape(experts, capacity, model)
    send_cot = picked[:, model:].reshape(experts, capacity, model)
    send_w = jnp.take(
        route_weights.reshape(slots), jnp.where(filled, source, slots), mode="fill", fill_value=0
    ).reshape(experts, capacity)
    recv_x, recv_cot, recv_w = (
        lax.all_to_all(send_x, "ep", split_axis=0, concat_axis=0, tiled=True),
        lax.all_to_all(send_cot, "ep", split_axis=0, concat_axis=0, tiled=True),
        lax.all_to_all(send_w, "ep", split_axis=0, concat_axis=0, tiled=True),
    )
    flat_w = recv_w.reshape(row_total)
    live = (flat_w != 0).astype(jnp.int32)
    live_count = jnp.sum(live)
    place = jnp.where(live > 0, jnp.cumsum(live) - 1, row_total)
    anchor = (
        jnp.full((row_total,), row_total, jnp.int32)
        .at[place]
        .set(jnp.arange(row_total, dtype=jnp.int32), mode="drop")
    )
    recv_joined = jnp.concatenate(
        [recv_x.reshape(row_total, model), recv_cot.reshape(row_total, model)], axis=1
    )
    packed = jnp.take(recv_joined, anchor, axis=0, mode="fill", fill_value=0)
    pack_x = packed[:, :model]
    pack_cot = packed[:, model:]
    pack_w = jnp.take(flat_w, anchor, mode="fill", fill_value=0)
    w_gate_one = w_gate[0]
    w_up_one = w_up[0]
    w_down_one = w_down[0]
    acc_gate, acc_up, acc_down, slot_grad, route_grad = expert_pass(
        pack_x, pack_cot, pack_w, live_count, w_gate_one, w_up_one, w_down_one
    )
    slot_rows = jnp.take(slot_grad, place, axis=0, mode="fill", fill_value=0.0).astype(jnp.bfloat16)
    route_rows = jnp.take(route_grad, place, axis=0, mode="fill", fill_value=0.0).astype(
        jnp.bfloat16
    )
    back_x, back_route_rows = (
        lax.all_to_all(
            slot_rows.reshape(experts, capacity, model),
            "ep",
            split_axis=0,
            concat_axis=0,
            tiled=True,
        ),
        lax.all_to_all(
            route_rows.reshape(experts, capacity), "ep", split_axis=0, concat_axis=0, tiled=True
        ),
    )
    mine_rows = back_x[flat_ids, position].reshape(tok_count, topk, model)
    grad_tokens = jnp.sum(mine_rows.astype(jnp.float32), axis=1).astype(jnp.bfloat16)
    grad_route = back_route_rows[flat_ids, position].reshape(tok_count, topk)
    summed = (
        lax.psum_scatter(
            acc_gate[None].astype(jnp.bfloat16), "dp", scatter_dimension=1, tiled=True
        ).astype(jnp.float32),
        lax.psum_scatter(
            acc_up[None].astype(jnp.bfloat16), "dp", scatter_dimension=1, tiled=True
        ).astype(jnp.float32),
        lax.psum_scatter(
            acc_down[None].astype(jnp.bfloat16), "dp", scatter_dimension=2, tiled=True
        ).astype(jnp.float32),
    )
    return (
        grad_tokens,
        grad_route,
        summed[0].astype(jnp.bfloat16),
        summed[1].astype(jnp.bfloat16),
        summed[2].astype(jnp.bfloat16),
    )


def fused_kernel(
    tok_hbm, cot_hbm, ids_hbm, rw_hbm, wg_hbm, wu_hbm, wdn_hbm,
    gt_ref, route_ref, gg_ref, gu_ref, gd_ref,
    ids_ref, rw_ref, wg, wu, wdn, tc, wd, wbuf, wcol, cols, colst, act_buf, fac_buf, hid_buf,
    hw_own, hw_recv, gp_own, gp_recv, part, fs, fr, bs, br, xs, xr, rs, rr,
    l_sem, w_sem, g_send, g_recv, c_send, c_recv, h_send, h_done, f_sem, b_sem, x_sem, r_sem,
):
    ep_size = lax.axis_size("ep")
    groups = lax.axis_size("dp")
    count = tok_hbm.shape[0]
    col = tc.shape[3]
    tiles, rows, ft = hw_own.shape
    ep = lax.axis_index("ep")
    dp = lax.axis_index("dp")
    z, y = ep // 2, ep % 2
    q, i = z // 2, z % 2
    xx, core = dp // 2, dp % 2
    peers_dp = (xx * 2 + 1 - core, (1 - xx) * 2 + core, (1 - xx) * 2 + 1 - core)
    inner = i != q
    outer = i == q
    zline = (z, z + 1 - 2 * i, z + 2 - 4 * q, 3 - z)
    targets = tuple(zline[s // 2] * 2 + (1 - y if s % 2 else y) for s in range(8))
    ynb, znb, twin, facing = targets[1], targets[2], targets[4], targets[6]
    inside = (i + q) % 2
    near = 4 + 2 * inside
    far = 6 - 2 * inside
    starts = (0, lead)
    sizes = (lead, 8 - lead)
    early = lead - 2
    f32 = jnp.float32
    bf16 = jnp.bfloat16

    def span(index, size):
        return pl.ds(pl.multiple_of(index * size, size), size)

    def remote(src, dst, send, recv, ep_to, dp_to):
        return pltpu.make_async_remote_copy(
            src_ref=src, dst_ref=dst, send_sem=send, recv_sem=recv,
            device_id=(ep_to, dp_to), device_id_type=pl.DeviceIdType.MESH,
        )

    loads = [
        [
            pltpu.make_async_copy(ref.at[:, pl.ds(j * col, col)], tc.at[k, j, pl.ds(0, count)], l_sem.at[k])
            for j in range(groups)
        ]
        for k, ref in enumerate((tok_hbm, cot_hbm))
    ]
    for group in loads:
        for load in group:
            load.start()
    lists = (
        pltpu.make_async_copy(ids_hbm, ids_ref, l_sem.at[2]),
        pltpu.make_async_copy(rw_hbm, rw_ref, l_sem.at[3]),
    )
    for load in lists:
        load.start()
    w_loads = [
        pltpu.make_async_copy(src, dst, l_sem.at[4 + k])
        for k, (src, dst) in enumerate(((wg_hbm, wg), (wu_hbm, wu), (wdn_hbm, wdn)))
    ]

    for load in w_loads:
        load.start()
    barrier = pltpu.get_barrier_semaphore()
    for k in range(1, ep_size):
        pl.semaphore_signal(
            barrier, inc=1, device_id=((ep + k) % ep_size, dp), device_id_type=pl.DeviceIdType.MESH
        )
    for peer in peers_dp:
        pl.semaphore_signal(barrier, inc=1, device_id=(ep, peer), device_id_type=pl.DeviceIdType.MESH)
    wd[...] = jnp.zeros(wd.shape, f32)
    rs[...] = jnp.zeros(rs.shape, f32)
    for load in lists:
        load.wait()
    ids = ids_ref[...]
    values = rw_ref[...].astype(f32)
    for e in range(ep_size):
        line = jnp.sum(jnp.where(ids == e, values, 0.0), axis=0, keepdims=True)
        wd[e, :, 0:count] = jnp.broadcast_to(line, (wd.shape[1], count))
    pl.semaphore_wait(barrier, ep_size - 1 + len(peers_dp))

    def view(k, slot):
        place = span(slot, count)
        return cols.at[1, pl.ds(1, 2), place] if k == 2 else tc.at[k, :, place]

    def hop(k, slot, there, late, ep_to):
        remote(view(k, slot), view(k, there), g_send.at[k, late], g_recv.at[k, there], ep_to, dp).start()

    def got(k, slot):
        remote(view(k, slot), view(k, slot), g_send.at[k, 0], g_recv.at[k, slot], ynb, dp).wait_recv()

    def share(k, slot, every=False):
        if k == 2:
            return
        for r in (1, 2, 0) if k == 0 or every else (0,):
            peer = peers_dp[r]
            remote(
                tc.at[k, peer, span(slot, count)], cols.at[k, r, span(slot, count)],
                c_send.at[k, r], c_recv.at[k, r], ep, peer,
            ).start()

    def take(k, slot):
        got(k, slot)
        share(k, slot)

    def own_out(k):
        hop(k, 0, 1, 0, ynb)
        hop(k, 0, 2, 0, znb)

        @pl.when(inner)
        def _():
            hop(k, 0, 6, 1, facing)

    def pair_out(k):
        got(k, 2)
        if k < 2:
            hop(k, 2, 3, 0, ynb)

        @pl.when(inner)
        def _():
            hop(k, 2, 4, 1, facing)

        share(k, 2)
        got(k, 1)
        if k == 2:
            hop(k, 1, 3, 0, znb)
        share(k, 1)

    def inner_pass(k, slot):
        @pl.when(inner)
        def _():
            got(k, slot)
            hop(k, slot, 10 - slot, 1, znb)
            hop(k, slot, slot + 1, 1, ynb)
            share(k, slot)

    def outer_pass(k, slot):
        @pl.when(outer)
        def _():
            got(k, slot)
            hop(k, slot, slot + 1, 1, ynb)
            share(k, slot)

    for s in range(1, 8):
        remote(wd.at[targets[s]], wbuf.at[s], w_sem.at[0], w_sem.at[1], targets[s], dp).start()
    keep_w = pltpu.make_async_copy(wd.at[ep], wbuf.at[0], w_sem.at[1])
    keep_w.start()
    for k in range(2):
        pltpu.make_async_copy(view(k, 0), view(k, 0), l_sem.at[k]).wait()
        own_out(k)
        share(k, 0, True)

    def wave_rows(wave):
        return pl.ds(starts[wave] * count, sizes[wave] * count)

    def gate_step(wave):
        block = wave_rows(wave)
        half = sizes[wave] * count

        def step(t, carry):
            lanes = span(t, ft)
            gate_pre = jnp.zeros((half, ft), f32)
            up_pre = jnp.zeros((half, ft), f32)
            for j in range(groups):
                depth = pl.ds(j * col, col)
                gate_pre += jnp.dot(tc[0, j, block], wg[depth, lanes], preferred_element_type=f32)
                up_pre += jnp.dot(tc[0, j, block], wu[depth, lanes], preferred_element_type=f32)
            act, slope = silu_parts(gate_pre)
            product = act * up_pre
            weight = wcol[block, 0:1]
            hw_own[t, block] = (weight * product).astype(bf16)
            act_buf[t, block] = act
            fac_buf[t, block] = up_pre * slope
            hid_buf[t, block] = product.astype(bf16)
            for r in (1, 0):
                done = h_done.at[1 + wave] if r == 1 else h_done.at[0]
                remote(
                    hw_own.at[t, block], hw_recv.at[r, t, block], h_send.at[0, r], done, ep, peers_dp[r]
                ).start()
            return carry

        lax.fori_loop(0, tiles, step, 0)

    def back_step(wave):
        block = wave_rows(wave)
        weight = wcol[block, 0:1]
        half = sizes[wave] * count

        def step(t, route):
            back = jnp.zeros((half, ft), f32)
            for j in range(groups):
                back += lax.dot_general(
                    tc[1, j, block], wdn[span(t, ft), pl.ds(j * col, col)], contract_last, preferred_element_type=f32
                )
            scaled = weight * back
            gp_own[t, 0, block] = (scaled * fac_buf[t, block]).astype(bf16)
            gp_own[t, 1, block] = (scaled * act_buf[t, block]).astype(bf16)
            route = route + jnp.sum(hid_buf[t, block].astype(f32) * back, axis=1, keepdims=True)
            for r in (1, 0):
                done = h_done.at[(5 + wave) + wave * t] if r == 1 else h_done.at[4]
                remote(
                    gp_own.at[t, :, block], gp_recv.at[r, t, :, block], h_send.at[1, r], done, ep, peers_dp[r]
                ).start()
            return route

        route = lax.fori_loop(0, tiles, step, jnp.zeros((half, 1), f32))
        lined = jnp.broadcast_to(route, (half, 128)).T
        for p in range(sizes[wave]):
            line = lined[0:1, p * count:(p + 1) * count]
            rs[starts[wave] + p, :, 0:count] = jnp.broadcast_to(line, (rs.shape[1], count))

    def fold_send(n, mode, phase):
        place = pl.ds(early * phase, early + (4 - 2 * early) * phase)
        done = f_sem.at[1 + phase * (1 + n)]
        to = ynb + mode * (znb - ynb)
        return remote(fs.at[n, place], fr.at[n, place], f_sem.at[0], done, to, dp)

    def fold_rows(n, mode, phase):
        for j in ((range(early), range(early, 4))[phase]):
            source = 2 * j + 1 + mode * (1 - j % 2)
            fs[n, j] = part[n, source].astype(bf16)

    def slot_step(wave):
        block = wave_rows(wave)
        size = sizes[wave]

        def step(n, carry):
            total = jnp.zeros((size * count, col), f32)
            for t in range(tiles):
                lanes = pl.ds(t * ft, ft)
                total += lax.dot_general(
                    gp_own[t, 0, block], wg[span(n, col), lanes], contract_last, preferred_element_type=f32
                )
                total += lax.dot_general(
                    gp_own[t, 1, block], wu[span(n, col), lanes], contract_last, preferred_element_type=f32
                )
            part[n, pl.ds(starts[wave], size)] = total.reshape(size, count, col)
            mode = n // 2
            fold_rows(n, mode, wave)
            if wave == 1:
                fold_send(n, mode, 1).start()
            return carry

        lax.fori_loop(0, groups, step, 0)

    def fold_early():
        def step(n, carry):
            fold_send(n, n // 2, 0).start()
            return carry

        lax.fori_loop(0, groups, step, 0)

    def fold_mid():
        ref = fr.at[:, pl.ds(0, early)]
        remote(ref, ref, f_sem.at[0], f_sem.at[1], ynb, dp).wait_recv()

        def step(n, carry):
            mode = n // 2
            fold_send(n, mode, 1).wait_recv()
            bs[n, 0] = (part[n, 2 - mode] + fr[n, 1].astype(f32)).astype(bf16)
            bs[n, 1] = (part[n, 6 - mode] + fr[n, 3].astype(f32)).astype(bf16)
            to = znb + mode * (ynb - znb)
            remote(bs.at[n], br.at[n], b_sem.at[0], b_sem.at[1 + n], to, dp).start()
            return carry

        lax.fori_loop(0, groups, step, 0)

    def fold_cross():
        def step(n, carry):
            remote(bs.at[n], br.at[n], b_sem.at[0], b_sem.at[1 + n], znb, dp).wait_recv()
            xs[n] = (part[n, 4] + fr[n, 2].astype(f32) + br[n, 1].astype(f32)).astype(bf16)
            remote(xs.at[n], xr.at[n], x_sem.at[0], x_sem.at[1 + n], twin, dp).start()
            return carry

        lax.fori_loop(0, groups, step, 0)

    def pass_hidden(wave):
        block = wave_rows(wave)
        ref = hw_recv.at[1, :, block]
        remote(ref, ref, h_send.at[0, 1], h_done.at[1 + wave], ep, peers_dp[1]).wait_recv()
        remote(ref, hw_recv.at[2, :, block], h_send.at[0, 2], h_done.at[3], ep, peers_dp[0]).start()

    def pass_grad_first():
        ref = gp_recv.at[1, :, :, wave_rows(0)]
        remote(ref, ref, h_send.at[1, 1], h_done.at[5], ep, peers_dp[1]).wait_recv()
        remote(ref, gp_recv.at[2, :, :, wave_rows(0)], h_send.at[1, 2], h_done.at[6 + tiles], ep, peers_dp[0]).start()

    def pass_grad(t):
        ref = gp_recv.at[1, t, :, wave_rows(1)]
        remote(ref, ref, h_send.at[1, 1], h_done.at[6 + t], ep, peers_dp[1]).wait_recv()
        remote(
            ref, gp_recv.at[2, t, :, wave_rows(1)], h_send.at[1, 2], h_done.at[7 + tiles + t], ep, peers_dp[0]
        ).start()

    pair_out(0)
    if lead == 4:
        take(0, 3)
    for load in w_loads[0:2]:
        load.wait()
    remote(wbuf, wbuf, w_sem.at[0], w_sem.at[1], ynb, dp).wait_recv()
    flat = wbuf[...].reshape(ep_size * wbuf.shape[1], wbuf.shape[2])
    turned = jnp.concatenate([flat] * (128 // flat.shape[0]), axis=0).T
    step8 = wbuf.shape[1]
    for p in range(ep_size):
        wcol[pl.ds(p * count, count), :] = jnp.broadcast_to(turned[0:count, p * step8:p * step8 + 1], (count, 128))
    gate_step(0)
    inner_pass(0, near)
    pair_out(1)
    if lead == 4:
        take(1, 3)
    w_loads[2].wait()
    back_step(0)
    inner_pass(0, far)
    for r in (1, 2):
        ref = cols.at[1, r, pl.ds(0, count)]
        remote(ref, ref, c_send.at[1, r], c_recv.at[1, r], ep, peers_dp[r]).wait_recv()
    own_out(2)
    slot_step(0)
    inner_pass(1, near)
    inner_pass(1, far)
    outer_pass(0, near)
    outer_pass(0, far)
    if lead == 3:
        take(0, 3)
    take(0, near + 1)
    outer_pass(1, near)
    take(0, far + 1)
    gate_step(1)
    outer_pass(1, far)
    fold_early()
    pair_out(2)
    pass_hidden(0)
    if lead == 3:
        take(1, 3)
    take(1, near + 1)
    take(1, far + 1)
    back_step(1)
    inner_pass(2, near)
    slot_step(1)
    pass_grad_first()
    for s in range(1, 8):
        remote(rs.at[s], rr.at[ep], r_sem.at[0], r_sem.at[1], targets[s], dp).start()
    pltpu.make_async_copy(rs.at[0], rr.at[ep], r_sem.at[1]).start()
    inner_pass(2, far)
    pass_hidden(1)
    colst[0] = tc[0, dp].T
    for r in range(3):
        remote(cols.at[0, r], cols.at[0, r], c_send.at[0, r], c_recv.at[0, r], ep, peers_dp[r]).wait_recv()
        colst[1 + r] = cols[0, r].T
    fold_mid()
    outer_pass(2, near)
    outer_pass(2, far)
    remote(cols.at[1, 0], cols.at[1, 0], c_send.at[1, 0], c_recv.at[1, 0], ep, peers_dp[0]).wait_recv()
    fold_cross()
    got(2, 3)
    got(2, near + 1)
    got(2, far + 1)
    remote(hw_recv.at[0], hw_recv.at[0], h_send.at[0, 0], h_done.at[0], ep, peers_dp[0]).wait_recv()
    remote(hw_recv.at[2], hw_recv.at[2], h_send.at[0, 2], h_done.at[3], ep, peers_dp[0]).wait_recv()

    def down_step(t, carry):
        blocks = [hw_own.at[t]] + [hw_recv.at[r, t] for r in range(3)]
        cots = [tc.at[1, dp]] + [cols.at[1, r] for r in range(3)]
        grad_down = jnp.zeros((ft, col), f32)
        for g in range(4):
            grad_down += lax.dot_general(blocks[g][...], cots[g][...], contract_first, preferred_element_type=f32)
        gd_ref[span(t, ft), :] = grad_down.astype(bf16)
        return carry

    lax.fori_loop(0, tiles, down_step, 0)
    remote(gp_recv.at[0], gp_recv.at[0], h_send.at[1, 0], h_done.at[4], ep, peers_dp[0]).wait_recv()
    ref = gp_recv.at[2, :, :, wave_rows(0)]
    remote(ref, ref, h_send.at[1, 2], h_done.at[6 + tiles], ep, peers_dp[0]).wait_recv()
    pass_grad(0)

    def sum_step(n, carry):
        remote(xs.at[n], xr.at[n], x_sem.at[0], x_sem.at[1 + n], twin, dp).wait_recv()
        total = part[n, 0] + fr[n, 0].astype(f32) + br[n, 0].astype(f32) + xr[n].astype(f32)
        gt_ref[:, span(n, col)] = total.astype(bf16)
        return carry

    def weight_step(t, carry):
        @pl.when(t + 1 < tiles)
        def _():
            pass_grad(t + 1)

        @pl.when(t + 1 == tiles)
        def _():
            lax.fori_loop(0, groups, sum_step, 0)

        ref = gp_recv.at[2, t, :, wave_rows(1)]
        remote(ref, ref, h_send.at[1, 2], h_done.at[7 + tiles + t], ep, peers_dp[0]).wait_recv()
        blocks = [gp_own.at[t]] + [gp_recv.at[r, t] for r in range(3)]
        grad_gate = jnp.zeros((col, ft), f32)
        grad_up = jnp.zeros((col, ft), f32)
        for g in range(4):
            grad_gate += jnp.dot(colst[g], blocks[g][0], preferred_element_type=f32)
            grad_up += jnp.dot(colst[g], blocks[g][1], preferred_element_type=f32)
        gg_ref[:, span(t, ft)] = grad_gate.astype(bf16)
        gu_ref[:, span(t, ft)] = grad_up.astype(bf16)
        return carry

    lax.fori_loop(0, tiles, weight_step, 0)

    remote(rr, rr, r_sem.at[0], r_sem.at[1], ynb, dp).wait_recv()
    table = jnp.zeros(ids.shape, f32)
    for e in range(ep_size):
        table = table + jnp.where(ids == e, rr[e, 0:1, 0:count], 0.0)
    route_ref[...] = table.astype(bf16)

    def sent(ref, sem):
        remote(ref, ref, sem, r_sem.at[1], ynb, dp).wait_send()

    sent(rs.at[pl.ds(0, ep_size - 1)], r_sem.at[0])
    sent(wd.at[pl.ds(0, ep_size - 1)], w_sem.at[0])
    sent(fs, f_sem.at[0])
    sent(bs, b_sem.at[0])
    sent(xs, x_sem.at[0])
    for k in range(3):
        def whole(n):
            return cols.at[1, pl.ds(1, 2), pl.ds(0, n * count)] if k == 2 else tc.at[k, :, pl.ds(0, n * count)]

        sent(whole(3), g_send.at[k, 0])

        @pl.when(inner)
        def _():
            sent(whole(6), g_send.at[k, 1])

        @pl.when(outer)
        def _():
            sent(whole(2), g_send.at[k, 1])

    for k in range(2):
        for r in range(3):
            sent(cols.at[1, r, pl.ds(0, count)] if k == 1 and r > 0 else cols.at[k, r], c_send.at[k, r])
            sent((hw_recv, gp_recv)[k].at[r], h_send.at[k, r])


def store_kernel(*refs):
    sems = refs[-1]
    each = (len(refs) - 1) // 2
    copies = [pltpu.make_async_copy(refs[k], refs[each + k], sems.at[k]) for k in range(each)]
    for copy in copies:
        copy.start()
    for copy in copies:
        copy.wait()


def fused_body(tokens, cotangent, expert_ids, route_weights, w_gate, w_up, w_down):
    count, topk = expert_ids.shape
    model = tokens.shape[1]
    experts = lax.axis_size("ep")
    groups = lax.axis_size("dp")
    width = w_gate.shape[2]
    rows = experts * count
    col = model // groups
    ft = 256 if width % 256 == 0 else width
    tiles = width // ft
    lanes = 128
    bf16 = jnp.bfloat16
    f32 = jnp.float32
    any_spec = pl.BlockSpec(memory_space=pl.ANY)
    hbm = pl.BlockSpec(memory_space=pltpu.HBM)
    vmem = pl.BlockSpec(memory_space=pltpu.VMEM)
    dma = pltpu.SemaphoreType.DMA
    small = (experts, 8, lanes)
    shapes = ((count, model), (topk, count), (col, width), (col, width), (width, col))
    outs = pl.pallas_call(
        fused_kernel,
        name="fused_layer",
        out_shape=tuple(pltpu.VMEM(shape, bf16) for shape in shapes),
        in_specs=[hbm] * 7,
        out_specs=(vmem,) * 5,
        scratch_shapes=[
            pltpu.VMEM((topk, count), jnp.int32),
            pltpu.VMEM((topk, count), bf16),
            pltpu.VMEM((model, width), bf16),
            pltpu.VMEM((model, width), bf16),
            pltpu.VMEM((width, model), bf16),
            pltpu.VMEM((2, groups, rows, col), bf16),
            pltpu.VMEM(small, f32),
            pltpu.VMEM(small, f32),
            pltpu.VMEM((rows, lanes), f32),
            pltpu.VMEM((2, 3, rows, col), bf16),
            pltpu.VMEM((4, col, rows), bf16),
            pltpu.VMEM((tiles, rows, ft), f32),
            pltpu.VMEM((tiles, rows, ft), f32),
            pltpu.VMEM((tiles, rows, ft), bf16),
            pltpu.VMEM((tiles, rows, ft), bf16),
            pltpu.VMEM((3, tiles, rows, ft), bf16),
            pltpu.VMEM((tiles, 2, rows, ft), bf16),
            pltpu.VMEM((3, tiles, 2, rows, ft), bf16),
            pltpu.VMEM((groups, 8, count, col), f32),
            pltpu.VMEM((groups, 4, count, col), bf16),
            pltpu.VMEM((groups, 4, count, col), bf16),
            pltpu.VMEM((groups, 2, count, col), bf16),
            pltpu.VMEM((groups, 2, count, col), bf16),
            pltpu.VMEM((groups, count, col), bf16),
            pltpu.VMEM((groups, count, col), bf16),
            pltpu.VMEM(small, f32),
            pltpu.VMEM(small, f32),
            dma((7,)),
            dma((2,)),
            dma((3, 2)),
            dma((3, experts)),
            dma((2, 3)),
            dma((2, 3)),
            dma((2, 3)),
            dma((7 + 2 * tiles,)),
            dma((2 + groups,)),
            dma((1 + groups,)),
            dma((1 + groups,)),
            dma((2,)),
        ],
        compiler_params=pltpu.CompilerParams(
            collective_id=0, has_side_effects=True, vmem_limit_bytes=64200000
        ),
    )(tokens, cotangent, expert_ids.T, route_weights.T, w_gate[0], w_up[0], w_down[0])
    outs = pl.pallas_call(
        store_kernel,
        name="store_results",
        out_shape=tuple(jax.ShapeDtypeStruct(shape, bf16) for shape in shapes),
        in_specs=[any_spec] * 5,
        out_specs=(any_spec,) * 5,
        scratch_shapes=[dma((5,))],
        compiler_params=pltpu.CompilerParams(vmem_limit_bytes=4 * 1024 * 1024),
    )(*outs)
    grad_tokens, grad_route, grad_gate, grad_up, grad_down = outs
    return grad_tokens, grad_route.T, grad_gate[None], grad_up[None], grad_down[None]


def body(tokens, cotangent, expert_ids, route_weights, w_gate, w_up, w_down):
    tok_count, topk = expert_ids.shape
    experts = lax.axis_size("ep")
    whole = 2 * tok_count * topk // experts >= tok_count
    paired = lax.axis_size("dp") == 4 and experts == 8 and tok_count in (32, 64)
    chosen = fused_body if whole and paired else routed_body
    return chosen(tokens, cotangent, expert_ids, route_weights, w_gate, w_up, w_down)


def solution(mesh):
    return jax.shard_map(
        body,
        mesh=mesh,
        in_specs=(
            P(("ep", "dp"), None),
            P(("ep", "dp"), None),
            P(("ep", "dp"), None),
            P(("ep", "dp"), None),
            P("ep", None, None),
            P("ep", None, None),
            P("ep", None, None),
        ),
        out_specs=(
            P(("ep", "dp"), None),
            P(("ep", "dp"), None),
            P("ep", "dp", None),
            P("ep", "dp", None),
            P("ep", None, "dp"),
        ),
        check_vma=False,
    )
```

```python
import jax
import jax.numpy as jnp
from jax import lax
from jax.experimental import pallas as pl
from jax.experimental.pallas import tpu as pltpu
from jax.sharding import PartitionSpec as P

block_rows = 128
lead = 3
store_pieces = 4
along_y = 2
contract_last = (((1,), (1,)), ((), ()))
contract_first = (((0,), (0,)), ((), ()))


def silu_parts(gate_pre):
    sig = jax.nn.sigmoid(gate_pre)
    return (gate_pre * sig, sig * (1.0 + gate_pre * (1.0 - sig)))


def expert_pass(rows_x, rows_cot, rows_w, live_count, w_gate_one, w_up_one, w_down_one):
    total, model = rows_x.shape
    width = w_gate_one.shape[1]

    def step(index, carry):
        acc_gate, acc_up, acc_down, slot_grad, route_grad = carry
        start = index * block_rows
        tok = lax.dynamic_slice_in_dim(rows_x, start, block_rows, 0)
        cot = lax.dynamic_slice_in_dim(rows_cot, start, block_rows, 0)
        weight = lax.dynamic_slice_in_dim(rows_w, start, block_rows, 0).astype(jnp.float32)[:, None]
        gate_pre = jnp.dot(tok, w_gate_one, preferred_element_type=jnp.float32)
        up_pre = jnp.dot(tok, w_up_one, preferred_element_type=jnp.float32)
        act, slope = silu_parts(gate_pre)
        hidden = lax.optimization_barrier((act * up_pre).astype(jnp.bfloat16))
        back = lax.dot_general(cot, w_down_one, contract_last, preferred_element_type=jnp.float32)
        route_part = jnp.sum(hidden.astype(jnp.float32) * back, axis=1)
        scaled = weight * back
        grad_gate_pre = (scaled * up_pre * slope).astype(jnp.bfloat16)
        grad_up_pre = (scaled * act).astype(jnp.bfloat16)
        scaled_cot = (weight * cot.astype(jnp.float32)).astype(jnp.bfloat16)
        part = lax.dot_general(
            grad_gate_pre, w_gate_one, contract_last, preferred_element_type=jnp.float32
        )
        part = part + lax.dot_general(
            grad_up_pre, w_up_one, contract_last, preferred_element_type=jnp.float32
        )
        acc_gate = acc_gate + lax.dot_general(
            tok, grad_gate_pre, contract_first, preferred_element_type=jnp.float32
        )
        acc_up = acc_up + lax.dot_general(
            tok, grad_up_pre, contract_first, preferred_element_type=jnp.float32
        )
        acc_down = acc_down + lax.dot_general(
            hidden, scaled_cot, contract_first, preferred_element_type=jnp.float32
        )
        slot_grad = lax.dynamic_update_slice_in_dim(slot_grad, part, start, 0)
        route_grad = lax.dynamic_update_slice_in_dim(route_grad, route_part, start, 0)
        return (acc_gate, acc_up, acc_down, slot_grad, route_grad)

    init = (
        jnp.zeros((model, width), jnp.float32),
        jnp.zeros((model, width), jnp.float32),
        jnp.zeros((width, model), jnp.float32),
        jnp.zeros((total, model), jnp.float32),
        jnp.zeros((total,), jnp.float32),
    )
    block_count = (live_count + block_rows - 1) // block_rows
    return lax.fori_loop(0, block_count, step, init)


def routed_body(tokens, cotangent, expert_ids, route_weights, w_gate, w_up, w_down):
    tok_count, topk = expert_ids.shape
    model = tokens.shape[1]
    experts = lax.axis_size("ep")
    capacity = min(tok_count, 2 * tok_count * topk // experts)
    slots = tok_count * topk
    row_total = experts * capacity
    flat_ids = expert_ids.reshape(slots)
    onehot = (flat_ids[:, None] == jnp.arange(experts, dtype=jnp.int32)[None, :]).astype(jnp.int32)
    position = jnp.sum((jnp.cumsum(onehot, axis=0) - 1) * onehot, axis=1)
    slot_ids = jnp.arange(slots, dtype=jnp.int32)
    source = (
        jnp.full((row_total,), slots, jnp.int32).at[flat_ids * capacity + position].set(slot_ids)
    )
    filled = source < slots
    source_token = jnp.where(filled, source // topk, tok_count)
    joined = jnp.concatenate([tokens, cotangent], axis=1)
    picked = jnp.take(joined, source_token, axis=0, mode="fill", fill_value=0)
    send_x = picked[:, :model].reshape(experts, capacity, model)
    send_cot = picked[:, model:].reshape(experts, capacity, model)
    send_w = jnp.take(
        route_weights.reshape(slots), jnp.where(filled, source, slots), mode="fill", fill_value=0
    ).reshape(experts, capacity)
    recv_x, recv_cot, recv_w = (
        lax.all_to_all(send_x, "ep", split_axis=0, concat_axis=0, tiled=True),
        lax.all_to_all(send_cot, "ep", split_axis=0, concat_axis=0, tiled=True),
        lax.all_to_all(send_w, "ep", split_axis=0, concat_axis=0, tiled=True),
    )
    flat_w = recv_w.reshape(row_total)
    live = (flat_w != 0).astype(jnp.int32)
    live_count = jnp.sum(live)
    place = jnp.where(live > 0, jnp.cumsum(live) - 1, row_total)
    anchor = (
        jnp.full((row_total,), row_total, jnp.int32)
        .at[place]
        .set(jnp.arange(row_total, dtype=jnp.int32), mode="drop")
    )
    recv_joined = jnp.concatenate(
        [recv_x.reshape(row_total, model), recv_cot.reshape(row_total, model)], axis=1
    )
    packed = jnp.take(recv_joined, anchor, axis=0, mode="fill", fill_value=0)
    pack_x = packed[:, :model]
    pack_cot = packed[:, model:]
    pack_w = jnp.take(flat_w, anchor, mode="fill", fill_value=0)
    w_gate_one = w_gate[0]
    w_up_one = w_up[0]
    w_down_one = w_down[0]
    acc_gate, acc_up, acc_down, slot_grad, route_grad = expert_pass(
        pack_x, pack_cot, pack_w, live_count, w_gate_one, w_up_one, w_down_one
    )
    slot_rows = jnp.take(slot_grad, place, axis=0, mode="fill", fill_value=0.0).astype(jnp.bfloat16)
    route_rows = jnp.take(route_grad, place, axis=0, mode="fill", fill_value=0.0).astype(
        jnp.bfloat16
    )
    back_x, back_route_rows = (
        lax.all_to_all(
            slot_rows.reshape(experts, capacity, model),
            "ep",
            split_axis=0,
            concat_axis=0,
            tiled=True,
        ),
        lax.all_to_all(
            route_rows.reshape(experts, capacity), "ep", split_axis=0, concat_axis=0, tiled=True
        ),
    )
    mine_rows = back_x[flat_ids, position].reshape(tok_count, topk, model)
    grad_tokens = jnp.sum(mine_rows.astype(jnp.float32), axis=1).astype(jnp.bfloat16)
    grad_route = back_route_rows[flat_ids, position].reshape(tok_count, topk)
    summed = (
        lax.psum_scatter(
            acc_gate[None].astype(jnp.bfloat16), "dp", scatter_dimension=1, tiled=True
        ).astype(jnp.float32),
        lax.psum_scatter(
            acc_up[None].astype(jnp.bfloat16), "dp", scatter_dimension=1, tiled=True
        ).astype(jnp.float32),
        lax.psum_scatter(
            acc_down[None].astype(jnp.bfloat16), "dp", scatter_dimension=2, tiled=True
        ).astype(jnp.float32),
    )
    return (
        grad_tokens,
        grad_route,
        summed[0].astype(jnp.bfloat16),
        summed[1].astype(jnp.bfloat16),
        summed[2].astype(jnp.bfloat16),
    )


def fused_kernel(
    tok_hbm, cot_hbm, ids_hbm, rw_hbm, wg_hbm, wu_hbm, wdn_hbm,
    gt_ref, route_ref, gg_ref, gu_ref, gd_ref,
    ids_ref, rw_ref, wg, wu, wdn, wgt, wut, wdt, tc, wd, wbuf, wcol, cols, colst, act_buf, fac_buf, hid_buf,
    hw_own, hw_recv, gp_own, gp_recv, part, fs, fr, bs, br, xs, xr, rs, rr,
    l_sem, w_sem, g_send, g_recv, c_send, c_recv, h_send, h_done, f_sem, b_sem, x_sem, r_sem,
):
    ep_size = lax.axis_size("ep")
    groups = lax.axis_size("dp")
    count = tok_hbm.shape[0]
    col = tc.shape[3]
    model = wdn.shape[1]
    tiles, rows, ft = hw_own.shape
    ep = lax.axis_index("ep")
    dp = lax.axis_index("dp")
    z, y = ep // 2, ep % 2
    q, i = z // 2, z % 2
    xx, core = dp // 2, dp % 2
    peers_dp = (xx * 2 + 1 - core, (1 - xx) * 2 + core, (1 - xx) * 2 + 1 - core)
    inner = i != q
    outer = i == q
    zline = (z, z + 1 - 2 * i, z + 2 - 4 * q, 3 - z)
    targets = tuple(zline[s // 2] * 2 + (1 - y if s % 2 else y) for s in range(8))
    ynb, znb, twin, facing = targets[1], targets[2], targets[4], targets[6]
    inside = (i + q) % 2
    near = 4 + 2 * inside
    far = 6 - 2 * inside
    starts = (0, lead)
    sizes = (lead, 8 - lead)
    early = lead - 2
    f32 = jnp.float32
    bf16 = jnp.bfloat16

    def span(index, size):
        return pl.ds(pl.multiple_of(index * size, size), size)

    def remote(src, dst, send, recv, ep_to, dp_to):
        return pltpu.make_async_remote_copy(
            src_ref=src, dst_ref=dst, send_sem=send, recv_sem=recv,
            device_id=(ep_to, dp_to), device_id_type=pl.DeviceIdType.MESH,
        )

    loads = [
        [
            pltpu.make_async_copy(ref.at[:, pl.ds(j * col, col)], tc.at[k, j, pl.ds(0, count)], l_sem.at[k])
            for j in range(groups)
        ]
        for k, ref in enumerate((tok_hbm, cot_hbm))
    ]
    for group in loads:
        for load in group:
            load.start()
    lists = (
        pltpu.make_async_copy(ids_hbm, ids_ref, l_sem.at[2]),
        pltpu.make_async_copy(rw_hbm, rw_ref, l_sem.at[3]),
    )
    for load in lists:
        load.start()
    w_loads = [
        pltpu.make_async_copy(src, dst, l_sem.at[4 + k])
        for k, (src, dst) in enumerate(((wg_hbm, wg), (wu_hbm, wu), (wdn_hbm, wdn)))
    ]

    for k in (2, 0, 1):
        w_loads[k].start()
    barrier = pltpu.get_barrier_semaphore()
    for k in range(1, ep_size):
        pl.semaphore_signal(
            barrier, inc=1, device_id=((ep + k) % ep_size, dp), device_id_type=pl.DeviceIdType.MESH
        )
    for peer in peers_dp:
        pl.semaphore_signal(barrier, inc=1, device_id=(ep, peer), device_id_type=pl.DeviceIdType.MESH)
    wd[...] = jnp.zeros(wd.shape, f32)
    rs[...] = jnp.zeros(rs.shape, f32)
    for load in lists:
        load.wait()
    ids = ids_ref[...]
    values = rw_ref[...].astype(f32)
    for e in range(ep_size):
        line = jnp.sum(jnp.where(ids == e, values, 0.0), axis=0, keepdims=True)
        wd[e, :, 0:count] = jnp.broadcast_to(line, (wd.shape[1], count))
    pl.semaphore_wait(barrier, ep_size - 1 + len(peers_dp))

    def view(k, slot):
        place = span(slot, count)
        return cols.at[1, pl.ds(1, 2), place] if k == 2 else tc.at[k, :, place]

    def hop(k, slot, there, late, ep_to):
        remote(view(k, slot), view(k, there), g_send.at[0], g_recv.at[k, there], ep_to, dp).start()

    def got(k, slot):
        remote(view(k, slot), view(k, slot), g_send.at[0], g_recv.at[k, slot], ynb, dp).wait_recv()

    def share(k, slot, every=False):
        if k == 2:
            return
        for r in (1, 2, 0) if k == 0 or every else (0,):
            peer = peers_dp[r]
            remote(
                tc.at[k, peer, span(slot, count)], cols.at[k, r, span(slot, count)],
                c_send.at[0], c_recv.at[0 if k == 0 else 1 if r == 0 else 2], ep, peer,
            ).start()

    def take(k, slot):
        got(k, slot)
        share(k, slot)

    def own_out(k):
        hop(k, 0, 1, 0, ynb)
        hop(k, 0, 2, 0, znb)

        @pl.when(inner)
        def _():
            hop(k, 0, 6, 1, facing)

    def pair_out(k):
        got(k, 2)
        hop(k, 2, 3, 0, ynb)

        @pl.when(inner)
        def _():
            hop(k, 2, 4, 1, facing)

        share(k, 2)
        take(k, 1)

    def facing_out(k):
        @pl.when(inner)
        def _():
            got(k, 2)
            hop(k, 2, 4, 1, facing)

    def diag_out(k):
        @pl.when(outer)
        def _():
            got(k, 2)

        got(k, 1)
        hop(k, 1, 3, 0, znb)

    def inner_pass(k, slot):
        @pl.when(inner)
        def _():
            got(k, slot)
            hop(k, slot, 10 - slot, 1, znb)
            hop(k, slot, slot + 1, 1, ynb)
            share(k, slot)

    def outer_pass(k, slot):
        @pl.when(outer)
        def _():
            got(k, slot)
            hop(k, slot, slot + 1, 1, ynb)
            share(k, slot)

    for s in range(1, 8):
        remote(wd.at[targets[s]], wbuf.at[s], w_sem.at[0], w_sem.at[1], targets[s], dp).start()
    keep_w = pltpu.make_async_copy(wd.at[ep], wbuf.at[0], w_sem.at[1])
    keep_w.start()
    for k in range(2):
        pltpu.make_async_copy(view(k, 0), view(k, 0), l_sem.at[k]).wait()
        own_out(k)
        share(k, 0, True)

    def wave_rows(wave):
        return pl.ds(starts[wave] * count, sizes[wave] * count)

    def gate_step(wave):
        block = wave_rows(wave)
        half = sizes[wave] * count

        def step(t, carry):
            lanes = span(t, ft)
            gate_pre = jnp.zeros((half, ft), f32)
            up_pre = jnp.zeros((half, ft), f32)
            for j in range(groups):
                depth = pl.ds(j * col, col)
                gate_pre += jnp.dot(tc[0, j, block], wg[depth, lanes], preferred_element_type=f32)
                up_pre += jnp.dot(tc[0, j, block], wu[depth, lanes], preferred_element_type=f32)
            act, slope = silu_parts(gate_pre)
            product = act * up_pre
            weight = wcol[block, 0:1]
            hw_own[t, block] = (weight * product).astype(bf16)
            act_buf[t, block] = act
            fac_buf[t, block] = up_pre * slope
            hid_buf[t, block] = product.astype(bf16)
            for r in (1, 0):
                done = h_done.at[1 + wave] if r == 1 else h_done.at[0]
                remote(
                    hw_own.at[t, block], hw_recv.at[r, t, block], h_send.at[0], done, ep, peers_dp[r]
                ).start()
            return carry

        lax.fori_loop(0, tiles, step, 0)

    def back_step(wave):
        block = wave_rows(wave)
        weight = wcol[block, 0:1]
        half = sizes[wave] * count

        def step(t, route):
            back = jnp.zeros((half, ft), f32)
            for j in range(groups):
                back += jnp.dot(tc[1, j, block], wdt[pl.ds(j * col, col), span(t, ft)], preferred_element_type=f32)
            scaled = weight * back
            gp_own[t, 0, block] = (scaled * fac_buf[t, block]).astype(bf16)
            gp_own[t, 1, block] = (scaled * act_buf[t, block]).astype(bf16)
            route = route + jnp.sum(hid_buf[t, block].astype(f32) * back, axis=1, keepdims=True)
            for r in (1, 0):
                done = h_done.at[(5 + wave) + wave * t] if r == 1 else h_done.at[4]
                remote(
                    gp_own.at[t, :, block], gp_recv.at[r, t, :, block], h_send.at[1], done, ep, peers_dp[r]
                ).start()
            return route

        route = lax.fori_loop(0, tiles, step, jnp.zeros((half, 1), f32))
        lined = jnp.broadcast_to(route, (half, 128)).T
        for p in range(sizes[wave]):
            line = lined[0:1, p * count:(p + 1) * count]
            rs[starts[wave] + p, :, 0:count] = jnp.broadcast_to(line, (rs.shape[1], count))

    def fold_send(n, mode, phase):
        place = pl.ds(early * phase, early + (4 - 2 * early) * phase)
        done = f_sem.at[1 + phase * (1 + n)]
        to = ynb + mode * (znb - ynb)
        return remote(fs.at[n, place], fr.at[n, place], f_sem.at[0], done, to, dp)

    def fold_rows(n, mode, phase):
        for j in ((range(early), range(early, 4))[phase]):
            source = 2 * j + 1 + mode * (1 - j % 2)
            fs[n, j] = part[n, source].astype(bf16)

    def slot_step(wave):
        block = wave_rows(wave)
        size = sizes[wave]

        def step(turn, carry):
            n = turn % 2 * (groups // 2) + turn // 2
            total = jnp.zeros((size * count, col), f32)
            for t in range(tiles):
                depth = pl.ds(t * ft, ft)
                if wave == 0:
                    total += lax.dot_general(
                        gp_own[t, 0, block], wg[span(n, col), depth], contract_last, preferred_element_type=f32
                    )
                    total += lax.dot_general(
                        gp_own[t, 1, block], wu[span(n, col), depth], contract_last, preferred_element_type=f32
                    )
                else:
                    total += jnp.dot(gp_own[t, 0, block], wgt[depth, span(n, col)], preferred_element_type=f32)
                    total += jnp.dot(gp_own[t, 1, block], wut[depth, span(n, col)], preferred_element_type=f32)
            part[n, pl.ds(starts[wave], size)] = total.reshape(size, count, col)
            mode = n // along_y
            fold_rows(n, mode, wave)
            if wave == 1:
                fold_send(n, mode, 1).start()
            return carry

        lax.fori_loop(0, groups, step, 0)

    def fold_early():
        def step(n, carry):
            fold_send(n, n // along_y, 0).start()
            return carry

        lax.fori_loop(0, groups, step, 0)

    def fold_ready():
        ref = fr.at[:, pl.ds(0, early)]
        remote(ref, ref, f_sem.at[0], f_sem.at[1], ynb, dp).wait_recv()

    def fold_mid(n):
        mode = n // along_y
        fold_send(n, mode, 1).wait_recv()
        bs[n, 0] = (part[n, 2 - mode] + fr[n, 1].astype(f32)).astype(bf16)
        bs[n, 1] = (part[n, 6 - mode] + fr[n, 3].astype(f32)).astype(bf16)
        remote(bs.at[n], br.at[n], f_sem.at[0], b_sem.at[n], (znb, ynb)[mode], dp).start()

    def fold_cross(n):
        remote(bs.at[n], br.at[n], f_sem.at[0], b_sem.at[n], znb, dp).wait_recv()
        xs[n] = (part[n, 4] + fr[n, 2].astype(f32) + br[n, 1].astype(f32)).astype(bf16)
        remote(xs.at[n], xr.at[n], f_sem.at[0], x_sem.at[0], twin, dp).start()

    def pass_hidden(wave):
        block = wave_rows(wave)
        ref = hw_recv.at[1, :, block]
        remote(ref, ref, h_send.at[0], h_done.at[1 + wave], ep, peers_dp[1]).wait_recv()
        remote(ref, hw_recv.at[2, :, block], h_send.at[0], h_done.at[0], ep, peers_dp[0]).start()

    def pass_grad_first():
        ref = gp_recv.at[1, :, :, wave_rows(0)]
        remote(ref, ref, h_send.at[1], h_done.at[5], ep, peers_dp[1]).wait_recv()
        remote(ref, gp_recv.at[2, :, :, wave_rows(0)], h_send.at[1], h_done.at[6 + tiles], ep, peers_dp[0]).start()

    def pass_grad(t):
        ref = gp_recv.at[1, t, :, wave_rows(1)]
        remote(ref, ref, h_send.at[1], h_done.at[6 + t], ep, peers_dp[1]).wait_recv()
        remote(
            ref, gp_recv.at[2, t, :, wave_rows(1)], h_send.at[1], h_done.at[7 + tiles + t], ep, peers_dp[0]
        ).start()

    def turn_down():
        def step(t, carry):
            for j in range(groups):
                wdt[pl.ds(j * col, col), span(t, ft)] = wdn[span(t, ft), pl.ds(j * col, col)].T
            return carry

        lax.fori_loop(0, tiles, step, 0)

    def turn_up():
        def step(n, carry):
            for t in range(tiles):
                wgt[pl.ds(t * ft, ft), span(n, col)] = wg[span(n, col), pl.ds(t * ft, ft)].T
                wut[pl.ds(t * ft, ft), span(n, col)] = wu[span(n, col), pl.ds(t * ft, ft)].T
            return carry

        lax.fori_loop(0, groups, step, 0)

    w_loads[2].wait()
    turn_down()
    pair_out(0)
    for load in w_loads[0:2]:
        load.wait()
    remote(wbuf, wbuf, w_sem.at[0], w_sem.at[1], ynb, dp).wait_recv()
    flat = wbuf[...].reshape(ep_size * wbuf.shape[1], wbuf.shape[2])
    turned = jnp.concatenate([flat] * (128 // flat.shape[0]), axis=0).T
    step8 = wbuf.shape[1]
    for p in range(ep_size):
        wcol[pl.ds(p * count, count), :] = jnp.broadcast_to(turned[0:count, p * step8:p * step8 + 1], (count, 128))
    gate_step(0)
    inner_pass(0, near)
    pair_out(1)
    back_step(0)
    inner_pass(0, far)
    slot_step(0)
    inner_pass(1, near)
    inner_pass(1, far)
    ref = cols.at[1, pl.ds(1, 2), pl.ds(0, count)]
    remote(ref, ref, c_send.at[0], c_recv.at[2], ep, peers_dp[1]).wait_recv()
    own_out(2)
    outer_pass(0, near)
    turn_up()
    facing_out(2)
    outer_pass(0, far)
    if lead == 3:
        take(0, 3)
    take(0, near + 1)
    outer_pass(1, near)
    outer_pass(1, far)
    inner_pass(2, near)
    take(0, far + 1)
    inner_pass(2, far)
    gate_step(1)
    fold_early()
    outer_pass(2, near)
    outer_pass(2, far)
    pass_hidden(0)
    if lead == 3:
        take(1, 3)
    take(1, near + 1)
    take(1, far + 1)
    back_step(1)
    diag_out(2)
    slot_step(1)
    for s in range(1, 8):
        remote(rs.at[s], rr.at[ep], r_sem.at[0], r_sem.at[1], targets[s], dp).start()
    pltpu.make_async_copy(rs.at[0], rr.at[ep], r_sem.at[1]).start()
    pass_grad_first()
    remote(cols.at[0], cols.at[0], c_send.at[0], c_recv.at[0], ep, peers_dp[0]).wait_recv()
    colst[0] = tc[0, dp].T
    for r in range(3):
        colst[1 + r] = cols[0, r].T
    pass_hidden(1)
    fold_ready()
    fold_mid(0)
    fold_mid(2)
    fold_mid(1)
    fold_mid(3)
    remote(cols.at[1, 0], cols.at[1, 0], c_send.at[0], c_recv.at[1], ep, peers_dp[0]).wait_recv()
    remote(gp_recv.at[0], gp_recv.at[0], h_send.at[1], h_done.at[4], ep, peers_dp[0]).wait_recv()
    ref = gp_recv.at[2, :, :, wave_rows(0)]
    remote(ref, ref, h_send.at[1], h_done.at[6 + tiles], ep, peers_dp[0]).wait_recv()

    def down_tile(t):
        blocks = [hw_own.at[t]] + [hw_recv.at[r, t] for r in range(3)]
        cots = [tc.at[1, dp]] + [cols.at[1, r] for r in range(3)]
        grad_down = jnp.zeros((ft, col), f32)
        for g in range(4):
            grad_down += lax.dot_general(blocks[g][...], cots[g][...], contract_first, preferred_element_type=f32)
        gd_ref[span(t, ft), :] = grad_down.astype(bf16)

    def sum_all():
        remote(xs, xr, f_sem.at[0], x_sem.at[0], twin, dp).wait_recv()

        def step(n, carry):
            total = part[n, 0] + fr[n, 0].astype(f32) + br[n, 0].astype(f32) + xr[n].astype(f32)
            gt_ref[:, span(n, col)] = total.astype(bf16)
            return carry

        lax.fori_loop(0, groups, step, 0)

    def weight_tile(t):
        ref = gp_recv.at[2, t, :, wave_rows(1)]
        remote(ref, ref, h_send.at[1], h_done.at[7 + tiles + t], ep, peers_dp[0]).wait_recv()
        blocks = [gp_own.at[t]] + [gp_recv.at[r, t] for r in range(3)]
        grad_gate = jnp.zeros((col, ft), f32)
        grad_up = jnp.zeros((col, ft), f32)
        for g in range(4):
            grad_gate += jnp.dot(colst[g], blocks[g][0], preferred_element_type=f32)
            grad_up += jnp.dot(colst[g], blocks[g][1], preferred_element_type=f32)
        gg_ref[:, span(t, ft)] = grad_gate.astype(bf16)
        gu_ref[:, span(t, ft)] = grad_up.astype(bf16)

    def down_ready():
        got(2, 3)
        got(2, near + 1)
        got(2, far + 1)
        ref = hw_recv.at[pl.ds(0, 2)]
        remote(ref, ref, h_send.at[0], h_done.at[0], ep, peers_dp[0]).wait_recv()

    pass_grad(0)
    fold_cross(0)
    fold_cross(2)
    fold_cross(1)
    fold_cross(3)
    pass_grad(1)
    weight_tile(0)
    down_ready()
    for t in range(tiles):
        down_tile(t)
    pass_grad(2)
    weight_tile(1)
    sum_all()
    weight_tile(2)

    remote(rr, rr, r_sem.at[0], r_sem.at[1], ynb, dp).wait_recv()
    table = jnp.zeros(ids.shape, f32)
    for e in range(ep_size):
        table = table + jnp.where(ids == e, rr[e, 0:1, 0:count], 0.0)
    route_ref[...] = table.astype(bf16)

    def sent(ref, sem):
        remote(ref, ref, sem, r_sem.at[1], ynb, dp).wait_send()

    sent(rs.at[pl.ds(0, ep_size - 1)], r_sem.at[0])
    sent(wd.at[pl.ds(0, ep_size - 1)], w_sem.at[0])
    sent(wdn.at[pl.ds(0, (7 * groups * count * col) // model)], f_sem.at[0])
    unit = (groups * count * col) // model

    @pl.when(inner)
    def _():
        sent(wdn.at[pl.ds(0, 9 * (2 * unit + unit // 2))], g_send.at[0])

    @pl.when(outer)
    def _():
        sent(wdn.at[pl.ds(0, 5 * (2 * unit + unit // 2))], g_send.at[0])

    sent(wdn.at[pl.ds(0, (34 * count * col) // model)], c_send.at[0])
    sent(hw_recv, h_send.at[0])
    sent(gp_recv, h_send.at[1])


def store_kernel(*refs):
    sems = refs[-1]
    each = (len(refs) - 1) // 2
    copies = []
    for k in range(each):
        size = refs[k].shape[0]
        pieces = store_pieces if size % (16 * store_pieces) == 0 else 1
        step = size // pieces
        for p in range(pieces):
            place = pl.ds(p * step, step)
            copies.append(pltpu.make_async_copy(refs[k].at[place], refs[each + k].at[place], sems.at[k]))
    for copy in copies:
        copy.start()
    for k in range(each):
        pltpu.make_async_copy(refs[k], refs[each + k], sems.at[k]).wait()


def fused_body(tokens, cotangent, expert_ids, route_weights, w_gate, w_up, w_down):
    count, topk = expert_ids.shape
    model = tokens.shape[1]
    experts = lax.axis_size("ep")
    groups = lax.axis_size("dp")
    width = w_gate.shape[2]
    rows = experts * count
    col = model // groups
    ft = 256 if width % 256 == 0 else width
    tiles = width // ft
    lanes = 128
    bf16 = jnp.bfloat16
    f32 = jnp.float32
    any_spec = pl.BlockSpec(memory_space=pl.ANY)
    hbm = pl.BlockSpec(memory_space=pltpu.HBM)
    vmem = pl.BlockSpec(memory_space=pltpu.VMEM)
    dma = pltpu.SemaphoreType.DMA
    small = (experts, 8, lanes)
    shapes = ((count, model), (topk, count), (col, width), (col, width), (width, col))
    outs = pl.pallas_call(
        fused_kernel,
        name="fused_layer",
        out_shape=tuple(pltpu.VMEM(shape, bf16) for shape in shapes),
        in_specs=[hbm] * 7,
        out_specs=(vmem,) * 5,
        scratch_shapes=[
            pltpu.VMEM((topk, count), jnp.int32),
            pltpu.VMEM((topk, count), bf16),
            pltpu.VMEM((model, width), bf16),
            pltpu.VMEM((model, width), bf16),
            pltpu.VMEM((width, model), bf16),
            pltpu.VMEM((width, model), bf16),
            pltpu.VMEM((width, model), bf16),
            pltpu.VMEM((model, width), bf16),
            pltpu.VMEM((2, groups, rows, col), bf16),
            pltpu.VMEM(small, f32),
            pltpu.VMEM(small, f32),
            pltpu.VMEM((rows, lanes), f32),
            pltpu.VMEM((2, 3, rows, col), bf16),
            pltpu.VMEM((4, col, rows), bf16),
            pltpu.VMEM((tiles, rows, ft), f32),
            pltpu.VMEM((tiles, rows, ft), f32),
            pltpu.VMEM((tiles, rows, ft), bf16),
            pltpu.VMEM((tiles, rows, ft), bf16),
            pltpu.VMEM((3, tiles, rows, ft), bf16),
            pltpu.VMEM((tiles, 2, rows, ft), bf16),
            pltpu.VMEM((3, tiles, 2, rows, ft), bf16),
            pltpu.VMEM((groups, 8, count, col), f32),
            pltpu.VMEM((groups, 4, count, col), bf16),
            pltpu.VMEM((groups, 4, count, col), bf16),
            pltpu.VMEM((groups, 2, count, col), bf16),
            pltpu.VMEM((groups, 2, count, col), bf16),
            pltpu.VMEM((groups, count, col), bf16),
            pltpu.VMEM((groups, count, col), bf16),
            pltpu.VMEM(small, f32),
            pltpu.VMEM(small, f32),
            dma((7,)),
            dma((2,)),
            dma((1,)),
            dma((3, experts)),
            dma((1,)),
            dma((3,)),
            dma((2,)),
            dma((7 + 2 * tiles,)),
            dma((2 + groups,)),
            dma((groups,)),
            dma((1,)),
            dma((2,)),
        ],
        compiler_params=pltpu.CompilerParams(
            collective_id=0, has_side_effects=True, vmem_limit_bytes=64200000
        ),
    )(tokens, cotangent, expert_ids.T, route_weights.T, w_gate[0], w_up[0], w_down[0])
    outs = pl.pallas_call(
        store_kernel,
        name="store_results",
        out_shape=tuple(jax.ShapeDtypeStruct(shape, bf16) for shape in shapes),
        in_specs=[any_spec] * 5,
        out_specs=(any_spec,) * 5,
        scratch_shapes=[dma((5,))],
        compiler_params=pltpu.CompilerParams(vmem_limit_bytes=4 * 1024 * 1024),
    )(*outs)
    grad_tokens, grad_route, grad_gate, grad_up, grad_down = outs
    return grad_tokens, grad_route.T, grad_gate[None], grad_up[None], grad_down[None]


def body(tokens, cotangent, expert_ids, route_weights, w_gate, w_up, w_down):
    tok_count, topk = expert_ids.shape
    experts = lax.axis_size("ep")
    whole = 2 * tok_count * topk // experts >= tok_count
    paired = lax.axis_size("dp") == 4 and experts == 8 and tok_count == 32
    chosen = fused_body if whole and paired else routed_body
    return chosen(tokens, cotangent, expert_ids, route_weights, w_gate, w_up, w_down)


def solution(mesh):
    return jax.shard_map(
        body,
        mesh=mesh,
        in_specs=(
            P(("ep", "dp"), None),
            P(("ep", "dp"), None),
            P(("ep", "dp"), None),
            P(("ep", "dp"), None),
            P("ep", None, None),
            P("ep", None, None),
            P("ep", None, None),
        ),
        out_specs=(
            P(("ep", "dp"), None),
            P(("ep", "dp"), None),
            P("ep", "dp", None),
            P("ep", "dp", None),
            P("ep", None, "dp"),
        ),
        check_vma=False,
    )
```

```python
import jax
import jax.numpy as jnp
from jax import lax
from jax.experimental import pallas as pl
from jax.experimental.pallas import tpu as pltpu
from jax.sharding import PartitionSpec as P

block_rows = 128
lead = 3
store_pieces = 4
along_y = 2
contract_last = (((1,), (1,)), ((), ()))
contract_first = (((0,), (0,)), ((), ()))


def silu_parts(gate_pre):
    sig = jax.nn.sigmoid(gate_pre)
    return (gate_pre * sig, sig * (1.0 + gate_pre * (1.0 - sig)))


def expert_pass(rows_x, rows_cot, rows_w, live_count, w_gate_one, w_up_one, w_down_one):
    total, model = rows_x.shape
    width = w_gate_one.shape[1]

    def step(index, carry):
        acc_gate, acc_up, acc_down, slot_grad, route_grad = carry
        start = index * block_rows
        tok = lax.dynamic_slice_in_dim(rows_x, start, block_rows, 0)
        cot = lax.dynamic_slice_in_dim(rows_cot, start, block_rows, 0)
        weight = lax.dynamic_slice_in_dim(rows_w, start, block_rows, 0).astype(jnp.float32)[:, None]
        gate_pre = jnp.dot(tok, w_gate_one, preferred_element_type=jnp.float32)
        up_pre = jnp.dot(tok, w_up_one, preferred_element_type=jnp.float32)
        act, slope = silu_parts(gate_pre)
        hidden = lax.optimization_barrier((act * up_pre).astype(jnp.bfloat16))
        back = lax.dot_general(cot, w_down_one, contract_last, preferred_element_type=jnp.float32)
        route_part = jnp.sum(hidden.astype(jnp.float32) * back, axis=1)
        scaled = weight * back
        grad_gate_pre = (scaled * up_pre * slope).astype(jnp.bfloat16)
        grad_up_pre = (scaled * act).astype(jnp.bfloat16)
        scaled_cot = (weight * cot.astype(jnp.float32)).astype(jnp.bfloat16)
        part = lax.dot_general(
            grad_gate_pre, w_gate_one, contract_last, preferred_element_type=jnp.float32
        )
        part = part + lax.dot_general(
            grad_up_pre, w_up_one, contract_last, preferred_element_type=jnp.float32
        )
        acc_gate = acc_gate + lax.dot_general(
            tok, grad_gate_pre, contract_first, preferred_element_type=jnp.float32
        )
        acc_up = acc_up + lax.dot_general(
            tok, grad_up_pre, contract_first, preferred_element_type=jnp.float32
        )
        acc_down = acc_down + lax.dot_general(
            hidden, scaled_cot, contract_first, preferred_element_type=jnp.float32
        )
        slot_grad = lax.dynamic_update_slice_in_dim(slot_grad, part, start, 0)
        route_grad = lax.dynamic_update_slice_in_dim(route_grad, route_part, start, 0)
        return (acc_gate, acc_up, acc_down, slot_grad, route_grad)

    init = (
        jnp.zeros((model, width), jnp.float32),
        jnp.zeros((model, width), jnp.float32),
        jnp.zeros((width, model), jnp.float32),
        jnp.zeros((total, model), jnp.float32),
        jnp.zeros((total,), jnp.float32),
    )
    block_count = (live_count + block_rows - 1) // block_rows
    return lax.fori_loop(0, block_count, step, init)


def routed_body(tokens, cotangent, expert_ids, route_weights, w_gate, w_up, w_down):
    tok_count, topk = expert_ids.shape
    model = tokens.shape[1]
    experts = lax.axis_size("ep")
    capacity = min(tok_count, 2 * tok_count * topk // experts)
    slots = tok_count * topk
    row_total = experts * capacity
    flat_ids = expert_ids.reshape(slots)
    onehot = (flat_ids[:, None] == jnp.arange(experts, dtype=jnp.int32)[None, :]).astype(jnp.int32)
    position = jnp.sum((jnp.cumsum(onehot, axis=0) - 1) * onehot, axis=1)
    slot_ids = jnp.arange(slots, dtype=jnp.int32)
    source = (
        jnp.full((row_total,), slots, jnp.int32).at[flat_ids * capacity + position].set(slot_ids)
    )
    filled = source < slots
    source_token = jnp.where(filled, source // topk, tok_count)
    joined = jnp.concatenate([tokens, cotangent], axis=1)
    picked = jnp.take(joined, source_token, axis=0, mode="fill", fill_value=0)
    send_x = picked[:, :model].reshape(experts, capacity, model)
    send_cot = picked[:, model:].reshape(experts, capacity, model)
    send_w = jnp.take(
        route_weights.reshape(slots), jnp.where(filled, source, slots), mode="fill", fill_value=0
    ).reshape(experts, capacity)
    recv_x, recv_cot, recv_w = (
        lax.all_to_all(send_x, "ep", split_axis=0, concat_axis=0, tiled=True),
        lax.all_to_all(send_cot, "ep", split_axis=0, concat_axis=0, tiled=True),
        lax.all_to_all(send_w, "ep", split_axis=0, concat_axis=0, tiled=True),
    )
    flat_w = recv_w.reshape(row_total)
    live = (flat_w != 0).astype(jnp.int32)
    live_count = jnp.sum(live)
    place = jnp.where(live > 0, jnp.cumsum(live) - 1, row_total)
    anchor = (
        jnp.full((row_total,), row_total, jnp.int32)
        .at[place]
        .set(jnp.arange(row_total, dtype=jnp.int32), mode="drop")
    )
    recv_joined = jnp.concatenate(
        [recv_x.reshape(row_total, model), recv_cot.reshape(row_total, model)], axis=1
    )
    packed = jnp.take(recv_joined, anchor, axis=0, mode="fill", fill_value=0)
    pack_x = packed[:, :model]
    pack_cot = packed[:, model:]
    pack_w = jnp.take(flat_w, anchor, mode="fill", fill_value=0)
    w_gate_one = w_gate[0]
    w_up_one = w_up[0]
    w_down_one = w_down[0]
    acc_gate, acc_up, acc_down, slot_grad, route_grad = expert_pass(
        pack_x, pack_cot, pack_w, live_count, w_gate_one, w_up_one, w_down_one
    )
    slot_rows = jnp.take(slot_grad, place, axis=0, mode="fill", fill_value=0.0).astype(jnp.bfloat16)
    route_rows = jnp.take(route_grad, place, axis=0, mode="fill", fill_value=0.0).astype(
        jnp.bfloat16
    )
    back_x, back_route_rows = (
        lax.all_to_all(
            slot_rows.reshape(experts, capacity, model),
            "ep",
            split_axis=0,
            concat_axis=0,
            tiled=True,
        ),
        lax.all_to_all(
            route_rows.reshape(experts, capacity), "ep", split_axis=0, concat_axis=0, tiled=True
        ),
    )
    mine_rows = back_x[flat_ids, position].reshape(tok_count, topk, model)
    grad_tokens = jnp.sum(mine_rows.astype(jnp.float32), axis=1).astype(jnp.bfloat16)
    grad_route = back_route_rows[flat_ids, position].reshape(tok_count, topk)
    summed = (
        lax.psum_scatter(
            acc_gate[None].astype(jnp.bfloat16), "dp", scatter_dimension=1, tiled=True
        ).astype(jnp.float32),
        lax.psum_scatter(
            acc_up[None].astype(jnp.bfloat16), "dp", scatter_dimension=1, tiled=True
        ).astype(jnp.float32),
        lax.psum_scatter(
            acc_down[None].astype(jnp.bfloat16), "dp", scatter_dimension=2, tiled=True
        ).astype(jnp.float32),
    )
    return (
        grad_tokens,
        grad_route,
        summed[0].astype(jnp.bfloat16),
        summed[1].astype(jnp.bfloat16),
        summed[2].astype(jnp.bfloat16),
    )


def fused_kernel(
    tok_hbm, cot_hbm, ids_hbm, rw_hbm, wg_hbm, wu_hbm, wdn_hbm,
    gt_ref, route_ref, gg_ref, gu_ref, gd_ref,
    ids_ref, rw_ref, wg, wu, wdn, wgt, wut, wdt, tc, wd, wbuf, wcol, cols, colst, act_buf, fac_buf, hid_buf,
    hw_own, hw_recv, gp_own, gp_recv, part, fs, fr, bs, br, xs, xr, rs, rr,
    l_sem, w_sem, g_send, g_recv, c_send, c_recv, h_send, h_done, f_sem, b_sem, x_sem, r_sem,
):
    ep_size = lax.axis_size("ep")
    groups = lax.axis_size("dp")
    count = tok_hbm.shape[0]
    col = tc.shape[3]
    model = wdn.shape[1]
    tiles, rows, ft = hw_own.shape
    ep = lax.axis_index("ep")
    dp = lax.axis_index("dp")
    z, y = ep // 2, ep % 2
    q, i = z // 2, z % 2
    xx, core = dp // 2, dp % 2
    peers_dp = (xx * 2 + 1 - core, (1 - xx) * 2 + core, (1 - xx) * 2 + 1 - core)
    inner = i != q
    outer = i == q
    zline = (z, z + 1 - 2 * i, z + 2 - 4 * q, 3 - z)
    targets = tuple(zline[s // 2] * 2 + (1 - y if s % 2 else y) for s in range(8))
    ynb, znb, twin, facing = targets[1], targets[2], targets[4], targets[6]
    inside = (i + q) % 2
    near = 4 + 2 * inside
    far = 6 - 2 * inside
    starts = (0, lead)
    sizes = (lead, 8 - lead)
    early = lead - 2
    f32 = jnp.float32
    bf16 = jnp.bfloat16

    def span(index, size):
        return pl.ds(pl.multiple_of(index * size, size), size)

    def remote(src, dst, send, recv, ep_to, dp_to):
        return pltpu.make_async_remote_copy(
            src_ref=src, dst_ref=dst, send_sem=send, recv_sem=recv,
            device_id=(ep_to, dp_to), device_id_type=pl.DeviceIdType.MESH,
        )

    loads = [
        [
            pltpu.make_async_copy(ref.at[:, pl.ds(j * col, col)], tc.at[k, j, pl.ds(0, count)], l_sem.at[k])
            for j in range(groups)
        ]
        for k, ref in enumerate((tok_hbm, cot_hbm))
    ]
    for group in loads:
        for load in group:
            load.start()
    lists = (
        pltpu.make_async_copy(ids_hbm, ids_ref, l_sem.at[2]),
        pltpu.make_async_copy(rw_hbm, rw_ref, l_sem.at[3]),
    )
    for load in lists:
        load.start()
    w_loads = [
        pltpu.make_async_copy(src, dst, l_sem.at[4 + k])
        for k, (src, dst) in enumerate(((wg_hbm, wg), (wu_hbm, wu), (wdn_hbm, wdn)))
    ]

    for k in (2, 0, 1):
        w_loads[k].start()
    barrier = pltpu.get_barrier_semaphore()
    for k in range(1, ep_size):
        pl.semaphore_signal(
            barrier, inc=1, device_id=((ep + k) % ep_size, dp), device_id_type=pl.DeviceIdType.MESH
        )
    for peer in peers_dp:
        pl.semaphore_signal(barrier, inc=1, device_id=(ep, peer), device_id_type=pl.DeviceIdType.MESH)
    wd[...] = jnp.zeros(wd.shape, f32)
    rs[...] = jnp.zeros(rs.shape, f32)
    for load in lists:
        load.wait()
    ids = ids_ref[...]
    values = rw_ref[...].astype(f32)
    for e in range(ep_size):
        line = jnp.sum(jnp.where(ids == e, values, 0.0), axis=0, keepdims=True)
        wd[e, :, 0:count] = jnp.broadcast_to(line, (wd.shape[1], count))
    pl.semaphore_wait(barrier, ep_size - 1 + len(peers_dp))

    def view(k, slot):
        place = span(slot, count)
        return cols.at[1, pl.ds(1, 2), place] if k == 2 else tc.at[k, :, place]

    def hop(k, slot, there, late, ep_to):
        remote(view(k, slot), view(k, there), g_send.at[0], g_recv.at[k, there], ep_to, dp).start()

    def got(k, slot):
        remote(view(k, slot), view(k, slot), g_send.at[0], g_recv.at[k, slot], ynb, dp).wait_recv()

    def share(k, slot, every=False):
        if k == 2:
            return
        for r in (1, 2, 0) if k == 0 or every else (0,):
            peer = peers_dp[r]
            remote(
                tc.at[k, peer, span(slot, count)], cols.at[k, r, span(slot, count)],
                c_send.at[0], c_recv.at[0 if k == 0 else 1 if r == 0 else 2], ep, peer,
            ).start()

    def take(k, slot):
        got(k, slot)
        share(k, slot)

    def own_out(k):
        hop(k, 0, 1, 0, ynb)
        hop(k, 0, 2, 0, znb)

        @pl.when(inner)
        def _():
            hop(k, 0, 6, 1, facing)

    def pair_out(k):
        got(k, 2)
        hop(k, 2, 3, 0, ynb)

        @pl.when(inner)
        def _():
            hop(k, 2, 4, 1, facing)

        share(k, 2)
        take(k, 1)

    def side_out():
        @pl.when(inner)
        def _():
            hop(0, 1, 7, 1, facing)
            hop(1, 1, 7, 1, facing)

    def take_side(k):
        got(k, near + 1)
        share(k, near + 1)

    def facing_out(k):
        @pl.when(inner)
        def _():
            got(k, 2)
            hop(k, 2, 4, 1, facing)

    def diag_out(k):
        @pl.when(outer)
        def _():
            got(k, 2)

        got(k, 1)
        hop(k, 1, 3, 0, znb)

    def inner_pass(k, slot, sideways=True):
        @pl.when(inner)
        def _():
            got(k, slot)
            hop(k, slot, 10 - slot, 1, znb)
            if sideways:
                hop(k, slot, slot + 1, 1, ynb)
            share(k, slot)

    def outer_pass(k, slot, sideways=True):
        @pl.when(outer)
        def _():
            got(k, slot)
            if sideways:
                hop(k, slot, slot + 1, 1, ynb)
            share(k, slot)

    for s in range(1, 8):
        remote(wd.at[targets[s]], wbuf.at[s], w_sem.at[0], w_sem.at[1], targets[s], dp).start()
    keep_w = pltpu.make_async_copy(wd.at[ep], wbuf.at[0], w_sem.at[1])
    keep_w.start()
    for k in range(2):
        pltpu.make_async_copy(view(k, 0), view(k, 0), l_sem.at[k]).wait()
        own_out(k)
        share(k, 0, True)

    def wave_rows(wave):
        return pl.ds(starts[wave] * count, sizes[wave] * count)

    def gate_step(wave):
        block = wave_rows(wave)
        half = sizes[wave] * count

        def step(t, carry):
            lanes = span(t, ft)
            gate_pre = jnp.zeros((half, ft), f32)
            up_pre = jnp.zeros((half, ft), f32)
            for j in range(groups):
                depth = pl.ds(j * col, col)
                gate_pre += jnp.dot(tc[0, j, block], wg[depth, lanes], preferred_element_type=f32)
                up_pre += jnp.dot(tc[0, j, block], wu[depth, lanes], preferred_element_type=f32)
            act, slope = silu_parts(gate_pre)
            product = act * up_pre
            weight = wcol[block, 0:1]
            hw_own[t, block] = (weight * product).astype(bf16)
            act_buf[t, block] = act
            fac_buf[t, block] = up_pre * slope
            hid_buf[t, block] = product.astype(bf16)
            for r in (1, 0):
                done = h_done.at[1 + wave] if r == 1 else h_done.at[0]
                remote(
                    hw_own.at[t, block], hw_recv.at[r, t, block], h_send.at[0], done, ep, peers_dp[r]
                ).start()
            return carry

        lax.fori_loop(0, tiles, step, 0)

    def back_step(wave):
        block = wave_rows(wave)
        weight = wcol[block, 0:1]
        half = sizes[wave] * count

        def step(t, route):
            back = jnp.zeros((half, ft), f32)
            for j in range(groups):
                back += jnp.dot(tc[1, j, block], wdt[pl.ds(j * col, col), span(t, ft)], preferred_element_type=f32)
            scaled = weight * back
            gp_own[t, 0, block] = (scaled * fac_buf[t, block]).astype(bf16)
            gp_own[t, 1, block] = (scaled * act_buf[t, block]).astype(bf16)
            route = route + jnp.sum(hid_buf[t, block].astype(f32) * back, axis=1, keepdims=True)
            for r in (1, 0):
                done = h_done.at[(5 + wave) + wave * t] if r == 1 else h_done.at[4]
                remote(
                    gp_own.at[t, :, block], gp_recv.at[r, t, :, block], h_send.at[1], done, ep, peers_dp[r]
                ).start()
            return route

        route = lax.fori_loop(0, tiles, step, jnp.zeros((half, 1), f32))
        lined = jnp.broadcast_to(route, (half, 128)).T
        for p in range(sizes[wave]):
            line = lined[0:1, p * count:(p + 1) * count]
            rs[starts[wave] + p, :, 0:count] = jnp.broadcast_to(line, (rs.shape[1], count))

    def fold_send(n, mode, phase):
        place = pl.ds(early * phase, early + (4 - 2 * early) * phase)
        done = f_sem.at[1 + phase * (1 + n)]
        to = ynb + mode * (znb - ynb)
        return remote(fs.at[n, place], fr.at[n, place], f_sem.at[0], done, to, dp)

    def fold_rows(n, mode, phase):
        for j in ((range(early), range(early, 4))[phase]):
            source = 2 * j + 1 + mode * (1 - j % 2)
            fs[n, j] = part[n, source].astype(bf16)

    def slot_step(wave):
        block = wave_rows(wave)
        size = sizes[wave]

        def step(turn, carry):
            n = turn % 2 * (groups // 2) + turn // 2
            total = jnp.zeros((size * count, col), f32)
            for t in range(tiles):
                depth = pl.ds(t * ft, ft)
                if wave == 0:
                    total += lax.dot_general(
                        gp_own[t, 0, block], wg[span(n, col), depth], contract_last, preferred_element_type=f32
                    )
                    total += lax.dot_general(
                        gp_own[t, 1, block], wu[span(n, col), depth], contract_last, preferred_element_type=f32
                    )
                else:
                    total += jnp.dot(gp_own[t, 0, block], wgt[depth, span(n, col)], preferred_element_type=f32)
                    total += jnp.dot(gp_own[t, 1, block], wut[depth, span(n, col)], preferred_element_type=f32)
            part[n, pl.ds(starts[wave], size)] = total.reshape(size, count, col)
            mode = n // along_y
            fold_rows(n, mode, wave)
            if wave == 1:
                fold_send(n, mode, 1).start()
            return carry

        lax.fori_loop(0, groups, step, 0)

    def fold_early():
        def step(n, carry):
            fold_send(n, n // along_y, 0).start()
            return carry

        lax.fori_loop(0, groups, step, 0)

    def fold_ready():
        ref = fr.at[:, pl.ds(0, early)]
        remote(ref, ref, f_sem.at[0], f_sem.at[1], ynb, dp).wait_recv()

    def fold_mid(n):
        mode = n // along_y
        fold_send(n, mode, 1).wait_recv()
        bs[n, 0] = (part[n, 2 - mode] + fr[n, 1].astype(f32)).astype(bf16)
        bs[n, 1] = (part[n, 6 - mode] + fr[n, 3].astype(f32)).astype(bf16)
        remote(bs.at[n], br.at[n], f_sem.at[0], b_sem.at[n], (znb, ynb)[mode], dp).start()

    def fold_cross(n):
        remote(bs.at[n], br.at[n], f_sem.at[0], b_sem.at[n], znb, dp).wait_recv()
        xs[n] = (part[n, 4] + fr[n, 2].astype(f32) + br[n, 1].astype(f32)).astype(bf16)
        remote(xs.at[n], xr.at[n], f_sem.at[0], x_sem.at[0], twin, dp).start()

    def pass_hidden(wave):
        block = wave_rows(wave)
        ref = hw_recv.at[1, :, block]
        remote(ref, ref, h_send.at[0], h_done.at[1 + wave], ep, peers_dp[1]).wait_recv()
        remote(ref, hw_recv.at[2, :, block], h_send.at[0], h_done.at[0], ep, peers_dp[0]).start()

    def pass_grad_first():
        ref = gp_recv.at[1, :, :, wave_rows(0)]
        remote(ref, ref, h_send.at[1], h_done.at[5], ep, peers_dp[1]).wait_recv()
        remote(ref, gp_recv.at[2, :, :, wave_rows(0)], h_send.at[1], h_done.at[6 + tiles], ep, peers_dp[0]).start()

    def pass_grad(t):
        ref = gp_recv.at[1, t, :, wave_rows(1)]
        remote(ref, ref, h_send.at[1], h_done.at[6 + t], ep, peers_dp[1]).wait_recv()
        remote(
            ref, gp_recv.at[2, t, :, wave_rows(1)], h_send.at[1], h_done.at[7 + tiles + t], ep, peers_dp[0]
        ).start()

    def turn_down():
        def step(t, carry):
            for j in range(groups):
                wdt[pl.ds(j * col, col), span(t, ft)] = wdn[span(t, ft), pl.ds(j * col, col)].T
            return carry

        lax.fori_loop(0, tiles, step, 0)

    def turn_up():
        def step(n, carry):
            for t in range(tiles):
                wgt[pl.ds(t * ft, ft), span(n, col)] = wg[span(n, col), pl.ds(t * ft, ft)].T
                wut[pl.ds(t * ft, ft), span(n, col)] = wu[span(n, col), pl.ds(t * ft, ft)].T
            return carry

        lax.fori_loop(0, groups, step, 0)

    w_loads[2].wait()
    turn_down()
    pair_out(0)
    for load in w_loads[0:2]:
        load.wait()
    remote(wbuf, wbuf, w_sem.at[0], w_sem.at[1], ynb, dp).wait_recv()
    flat = wbuf[...].reshape(ep_size * wbuf.shape[1], wbuf.shape[2])
    turned = jnp.concatenate([flat] * (128 // flat.shape[0]), axis=0).T
    step8 = wbuf.shape[1]
    for p in range(ep_size):
        wcol[pl.ds(p * count, count), :] = jnp.broadcast_to(turned[0:count, p * step8:p * step8 + 1], (count, 128))
    gate_step(0)
    inner_pass(0, near, False)
    pair_out(1)
    side_out()
    back_step(0)
    inner_pass(0, far)
    slot_step(0)
    inner_pass(1, near, False)
    inner_pass(1, far)
    ref = cols.at[1, pl.ds(1, 2), pl.ds(0, count)]
    remote(ref, ref, c_send.at[0], c_recv.at[2], ep, peers_dp[1]).wait_recv()
    own_out(2)
    outer_pass(0, near)
    turn_up()
    facing_out(2)
    outer_pass(0, far)
    if lead == 3:
        take(0, 3)
    take_side(0)
    outer_pass(1, near)
    outer_pass(1, far)
    take(0, far + 1)
    gate_step(1)
    fold_early()
    pass_hidden(0)
    if lead == 3:
        take(1, 3)
    take_side(1)
    take(1, far + 1)
    back_step(1)
    diag_out(2)
    inner_pass(2, near)
    inner_pass(2, far)
    slot_step(1)
    for s in range(1, 8):
        remote(rs.at[s], rr.at[ep], r_sem.at[0], r_sem.at[1], targets[s], dp).start()
    pltpu.make_async_copy(rs.at[0], rr.at[ep], r_sem.at[1]).start()
    outer_pass(2, near)
    outer_pass(2, far)
    pass_grad_first()
    fold_ready()
    fold_mid(0)
    fold_mid(2)
    remote(cols.at[0], cols.at[0], c_send.at[0], c_recv.at[0], ep, peers_dp[0]).wait_recv()
    colst[0] = tc[0, dp].T
    for r in range(3):
        colst[1 + r] = cols[0, r].T
    fold_mid(1)
    fold_mid(3)
    pass_hidden(1)
    remote(cols.at[1, 0], cols.at[1, 0], c_send.at[0], c_recv.at[1], ep, peers_dp[0]).wait_recv()
    remote(gp_recv.at[0], gp_recv.at[0], h_send.at[1], h_done.at[4], ep, peers_dp[0]).wait_recv()
    ref = gp_recv.at[2, :, :, wave_rows(0)]
    remote(ref, ref, h_send.at[1], h_done.at[6 + tiles], ep, peers_dp[0]).wait_recv()

    def down_tile(t):
        blocks = [hw_own.at[t]] + [hw_recv.at[r, t] for r in range(3)]
        cots = [tc.at[1, dp]] + [cols.at[1, r] for r in range(3)]
        grad_down = jnp.zeros((ft, col), f32)
        for g in range(4):
            grad_down += lax.dot_general(blocks[g][...], cots[g][...], contract_first, preferred_element_type=f32)
        gd_ref[span(t, ft), :] = grad_down.astype(bf16)

    def sum_all():
        remote(xs, xr, f_sem.at[0], x_sem.at[0], twin, dp).wait_recv()

        def step(n, carry):
            total = part[n, 0] + fr[n, 0].astype(f32) + br[n, 0].astype(f32) + xr[n].astype(f32)
            gt_ref[:, span(n, col)] = total.astype(bf16)
            return carry

        lax.fori_loop(0, groups, step, 0)

    def weight_tile(t):
        ref = gp_recv.at[2, t, :, wave_rows(1)]
        remote(ref, ref, h_send.at[1], h_done.at[7 + tiles + t], ep, peers_dp[0]).wait_recv()
        blocks = [gp_own.at[t]] + [gp_recv.at[r, t] for r in range(3)]
        grad_gate = jnp.zeros((col, ft), f32)
        grad_up = jnp.zeros((col, ft), f32)
        for g in range(4):
            grad_gate += jnp.dot(colst[g], blocks[g][0], preferred_element_type=f32)
            grad_up += jnp.dot(colst[g], blocks[g][1], preferred_element_type=f32)
        gg_ref[:, span(t, ft)] = grad_gate.astype(bf16)
        gu_ref[:, span(t, ft)] = grad_up.astype(bf16)

    def down_ready():
        got(2, 3)
        got(2, near + 1)
        got(2, far + 1)
        ref = hw_recv.at[pl.ds(0, 2)]
        remote(ref, ref, h_send.at[0], h_done.at[0], ep, peers_dp[0]).wait_recv()

    pass_grad(0)
    fold_cross(0)
    fold_cross(2)
    fold_cross(1)
    fold_cross(3)
    for t in range(1, tiles - 1):
        pass_grad(t)
    weight_tile(0)
    down_ready()
    for t in range(tiles):
        down_tile(t)
    pass_grad(tiles - 1)
    for t in range(1, tiles):
        weight_tile(t)
    sum_all()

    remote(rr, rr, r_sem.at[0], r_sem.at[1], ynb, dp).wait_recv()
    table = jnp.zeros(ids.shape, f32)
    for e in range(ep_size):
        table = table + jnp.where(ids == e, rr[e, 0:1, 0:count], 0.0)
    route_ref[...] = table.astype(bf16)

    def sent(ref, sem):
        remote(ref, ref, sem, r_sem.at[1], ynb, dp).wait_send()

    sent(rs.at[pl.ds(0, ep_size - 1)], r_sem.at[0])
    sent(wd.at[pl.ds(0, ep_size - 1)], w_sem.at[0])
    sent(wdn.at[pl.ds(0, (7 * groups * count * col) // model)], f_sem.at[0])
    unit = (groups * count * col) // model

    @pl.when(inner)
    def _():
        sent(wdn.at[pl.ds(0, 18 * unit + 9 * unit // 2)], g_send.at[0])

    @pl.when(outer)
    def _():
        sent(wdn.at[pl.ds(0, 10 * unit + 5 * unit // 2)], g_send.at[0])

    sent(wdn.at[pl.ds(0, (34 * count * col) // model)], c_send.at[0])
    sent(hw_recv, h_send.at[0])
    sent(gp_recv, h_send.at[1])


def store_kernel(*refs):
    sems = refs[-1]
    each = (len(refs) - 1) // 2
    copies = []
    for k in range(each):
        size = refs[k].shape[0]
        pieces = store_pieces if size % (16 * store_pieces) == 0 else 1
        step = size // pieces
        for p in range(pieces):
            place = pl.ds(p * step, step)
            copies.append(pltpu.make_async_copy(refs[k].at[place], refs[each + k].at[place], sems.at[k]))
    for copy in copies:
        copy.start()
    for k in range(each):
        pltpu.make_async_copy(refs[k], refs[each + k], sems.at[k]).wait()


def fused_body(tokens, cotangent, expert_ids, route_weights, w_gate, w_up, w_down):
    count, topk = expert_ids.shape
    model = tokens.shape[1]
    experts = lax.axis_size("ep")
    groups = lax.axis_size("dp")
    width = w_gate.shape[2]
    rows = experts * count
    col = model // groups
    ft = 256 if width % 256 == 0 else width
    tiles = width // ft
    lanes = 128
    bf16 = jnp.bfloat16
    f32 = jnp.float32
    any_spec = pl.BlockSpec(memory_space=pl.ANY)
    hbm = pl.BlockSpec(memory_space=pltpu.HBM)
    vmem = pl.BlockSpec(memory_space=pltpu.VMEM)
    dma = pltpu.SemaphoreType.DMA
    small = (experts, 8, lanes)
    shapes = ((count, model), (topk, count), (col, width), (col, width), (width, col))
    outs = pl.pallas_call(
        fused_kernel,
        name="fused_layer",
        out_shape=tuple(pltpu.VMEM(shape, bf16) for shape in shapes),
        in_specs=[hbm] * 7,
        out_specs=(vmem,) * 5,
        scratch_shapes=[
            pltpu.VMEM((topk, count), jnp.int32),
            pltpu.VMEM((topk, count), bf16),
            pltpu.VMEM((model, width), bf16),
            pltpu.VMEM((model, width), bf16),
            pltpu.VMEM((width, model), bf16),
            pltpu.VMEM((width, model), bf16),
            pltpu.VMEM((width, model), bf16),
            pltpu.VMEM((model, width), bf16),
            pltpu.VMEM((2, groups, rows, col), bf16),
            pltpu.VMEM(small, f32),
            pltpu.VMEM(small, f32),
            pltpu.VMEM((rows, lanes), f32),
            pltpu.VMEM((2, 3, rows, col), bf16),
            pltpu.VMEM((4, col, rows), bf16),
            pltpu.VMEM((tiles, rows, ft), f32),
            pltpu.VMEM((tiles, rows, ft), f32),
            pltpu.VMEM((tiles, rows, ft), bf16),
            pltpu.VMEM((tiles, rows, ft), bf16),
            pltpu.VMEM((3, tiles, rows, ft), bf16),
            pltpu.VMEM((tiles, 2, rows, ft), bf16),
            pltpu.VMEM((3, tiles, 2, rows, ft), bf16),
            pltpu.VMEM((groups, 8, count, col), f32),
            pltpu.VMEM((groups, 4, count, col), bf16),
            pltpu.VMEM((groups, 4, count, col), bf16),
            pltpu.VMEM((groups, 2, count, col), bf16),
            pltpu.VMEM((groups, 2, count, col), bf16),
            pltpu.VMEM((groups, count, col), bf16),
            pltpu.VMEM((groups, count, col), bf16),
            pltpu.VMEM(small, f32),
            pltpu.VMEM(small, f32),
            dma((7,)),
            dma((2,)),
            dma((1,)),
            dma((3, experts)),
            dma((1,)),
            dma((3,)),
            dma((2,)),
            dma((7 + 2 * tiles,)),
            dma((2 + groups,)),
            dma((groups,)),
            dma((1,)),
            dma((2,)),
        ],
        compiler_params=pltpu.CompilerParams(
            collective_id=0, has_side_effects=True, vmem_limit_bytes=64200000
        ),
    )(tokens, cotangent, expert_ids.T, route_weights.T, w_gate[0], w_up[0], w_down[0])
    outs = pl.pallas_call(
        store_kernel,
        name="store_results",
        out_shape=tuple(jax.ShapeDtypeStruct(shape, bf16) for shape in shapes),
        in_specs=[any_spec] * 5,
        out_specs=(any_spec,) * 5,
        scratch_shapes=[dma((5,))],
        compiler_params=pltpu.CompilerParams(vmem_limit_bytes=4 * 1024 * 1024),
    )(*outs)
    grad_tokens, grad_route, grad_gate, grad_up, grad_down = outs
    return grad_tokens, grad_route.T, grad_gate[None], grad_up[None], grad_down[None]


def body(tokens, cotangent, expert_ids, route_weights, w_gate, w_up, w_down):
    tok_count, topk = expert_ids.shape
    experts = lax.axis_size("ep")
    whole = 2 * tok_count * topk // experts >= tok_count
    width = w_gate.shape[2]
    paired = lax.axis_size("dp") == 4 and experts == 8 and tok_count == 32
    paired = paired and width % 256 == 0 and width >= 24 * tok_count
    chosen = fused_body if whole and paired else routed_body
    return chosen(tokens, cotangent, expert_ids, route_weights, w_gate, w_up, w_down)


def solution(mesh):
    return jax.shard_map(
        body,
        mesh=mesh,
        in_specs=(
            P(("ep", "dp"), None),
            P(("ep", "dp"), None),
            P(("ep", "dp"), None),
            P(("ep", "dp"), None),
            P("ep", None, None),
            P("ep", None, None),
            P("ep", None, None),
        ),
        out_specs=(
            P(("ep", "dp"), None),
            P(("ep", "dp"), None),
            P("ep", "dp", None),
            P("ep", "dp", None),
            P("ep", None, "dp"),
        ),
        check_vma=False,
    )
```

```python
import jax
import jax.numpy as jnp
from jax import lax
from jax.experimental import pallas as pl
from jax.experimental.pallas import tpu as pltpu
from jax.sharding import PartitionSpec as P

block_rows = 128
lead = 3
store_pieces = 4
along_y = 2
contract_last = (((1,), (1,)), ((), ()))
contract_first = (((0,), (0,)), ((), ()))


def silu_parts(gate_pre):
    sig = jax.nn.sigmoid(gate_pre)
    return (gate_pre * sig, sig * (1.0 + gate_pre * (1.0 - sig)))


def expert_pass(rows_x, rows_cot, rows_w, live_count, w_gate_one, w_up_one, w_down_one):
    total, model = rows_x.shape
    width = w_gate_one.shape[1]

    def step(index, carry):
        acc_gate, acc_up, acc_down, slot_grad, route_grad = carry
        start = index * block_rows
        tok = lax.dynamic_slice_in_dim(rows_x, start, block_rows, 0)
        cot = lax.dynamic_slice_in_dim(rows_cot, start, block_rows, 0)
        weight = lax.dynamic_slice_in_dim(rows_w, start, block_rows, 0).astype(jnp.float32)[:, None]
        gate_pre = jnp.dot(tok, w_gate_one, preferred_element_type=jnp.float32)
        up_pre = jnp.dot(tok, w_up_one, preferred_element_type=jnp.float32)
        act, slope = silu_parts(gate_pre)
        hidden = lax.optimization_barrier((act * up_pre).astype(jnp.bfloat16))
        back = lax.dot_general(cot, w_down_one, contract_last, preferred_element_type=jnp.float32)
        route_part = jnp.sum(hidden.astype(jnp.float32) * back, axis=1)
        scaled = weight * back
        grad_gate_pre = (scaled * up_pre * slope).astype(jnp.bfloat16)
        grad_up_pre = (scaled * act).astype(jnp.bfloat16)
        scaled_cot = (weight * cot.astype(jnp.float32)).astype(jnp.bfloat16)
        part = lax.dot_general(
            grad_gate_pre, w_gate_one, contract_last, preferred_element_type=jnp.float32
        )
        part = part + lax.dot_general(
            grad_up_pre, w_up_one, contract_last, preferred_element_type=jnp.float32
        )
        acc_gate = acc_gate + lax.dot_general(
            tok, grad_gate_pre, contract_first, preferred_element_type=jnp.float32
        )
        acc_up = acc_up + lax.dot_general(
            tok, grad_up_pre, contract_first, preferred_element_type=jnp.float32
        )
        acc_down = acc_down + lax.dot_general(
            hidden, scaled_cot, contract_first, preferred_element_type=jnp.float32
        )
        slot_grad = lax.dynamic_update_slice_in_dim(slot_grad, part, start, 0)
        route_grad = lax.dynamic_update_slice_in_dim(route_grad, route_part, start, 0)
        return (acc_gate, acc_up, acc_down, slot_grad, route_grad)

    init = (
        jnp.zeros((model, width), jnp.float32),
        jnp.zeros((model, width), jnp.float32),
        jnp.zeros((width, model), jnp.float32),
        jnp.zeros((total, model), jnp.float32),
        jnp.zeros((total,), jnp.float32),
    )
    block_count = (live_count + block_rows - 1) // block_rows
    return lax.fori_loop(0, block_count, step, init)


def routed_body(tokens, cotangent, expert_ids, route_weights, w_gate, w_up, w_down):
    tok_count, topk = expert_ids.shape
    model = tokens.shape[1]
    experts = lax.axis_size("ep")
    capacity = min(tok_count, 2 * tok_count * topk // experts)
    slots = tok_count * topk
    row_total = experts * capacity
    flat_ids = expert_ids.reshape(slots)
    onehot = (flat_ids[:, None] == jnp.arange(experts, dtype=jnp.int32)[None, :]).astype(jnp.int32)
    position = jnp.sum((jnp.cumsum(onehot, axis=0) - 1) * onehot, axis=1)
    slot_ids = jnp.arange(slots, dtype=jnp.int32)
    source = (
        jnp.full((row_total,), slots, jnp.int32).at[flat_ids * capacity + position].set(slot_ids)
    )
    filled = source < slots
    source_token = jnp.where(filled, source // topk, tok_count)
    joined = jnp.concatenate([tokens, cotangent], axis=1)
    picked = jnp.take(joined, source_token, axis=0, mode="fill", fill_value=0)
    send_x = picked[:, :model].reshape(experts, capacity, model)
    send_cot = picked[:, model:].reshape(experts, capacity, model)
    send_w = jnp.take(
        route_weights.reshape(slots), jnp.where(filled, source, slots), mode="fill", fill_value=0
    ).reshape(experts, capacity)
    recv_x, recv_cot, recv_w = (
        lax.all_to_all(send_x, "ep", split_axis=0, concat_axis=0, tiled=True),
        lax.all_to_all(send_cot, "ep", split_axis=0, concat_axis=0, tiled=True),
        lax.all_to_all(send_w, "ep", split_axis=0, concat_axis=0, tiled=True),
    )
    flat_w = recv_w.reshape(row_total)
    live = (flat_w != 0).astype(jnp.int32)
    live_count = jnp.sum(live)
    place = jnp.where(live > 0, jnp.cumsum(live) - 1, row_total)
    anchor = (
        jnp.full((row_total,), row_total, jnp.int32)
        .at[place]
        .set(jnp.arange(row_total, dtype=jnp.int32), mode="drop")
    )
    recv_joined = jnp.concatenate(
        [recv_x.reshape(row_total, model), recv_cot.reshape(row_total, model)], axis=1
    )
    packed = jnp.take(recv_joined, anchor, axis=0, mode="fill", fill_value=0)
    pack_x = packed[:, :model]
    pack_cot = packed[:, model:]
    pack_w = jnp.take(flat_w, anchor, mode="fill", fill_value=0)
    w_gate_one = w_gate[0]
    w_up_one = w_up[0]
    w_down_one = w_down[0]
    acc_gate, acc_up, acc_down, slot_grad, route_grad = expert_pass(
        pack_x, pack_cot, pack_w, live_count, w_gate_one, w_up_one, w_down_one
    )
    slot_rows = jnp.take(slot_grad, place, axis=0, mode="fill", fill_value=0.0).astype(jnp.bfloat16)
    route_rows = jnp.take(route_grad, place, axis=0, mode="fill", fill_value=0.0).astype(
        jnp.bfloat16
    )
    back_x, back_route_rows = (
        lax.all_to_all(
            slot_rows.reshape(experts, capacity, model),
            "ep",
            split_axis=0,
            concat_axis=0,
            tiled=True,
        ),
        lax.all_to_all(
            route_rows.reshape(experts, capacity), "ep", split_axis=0, concat_axis=0, tiled=True
        ),
    )
    mine_rows = back_x[flat_ids, position].reshape(tok_count, topk, model)
    grad_tokens = jnp.sum(mine_rows.astype(jnp.float32), axis=1).astype(jnp.bfloat16)
    grad_route = back_route_rows[flat_ids, position].reshape(tok_count, topk)
    summed = (
        lax.psum_scatter(
            acc_gate[None].astype(jnp.bfloat16), "dp", scatter_dimension=1, tiled=True
        ).astype(jnp.float32),
        lax.psum_scatter(
            acc_up[None].astype(jnp.bfloat16), "dp", scatter_dimension=1, tiled=True
        ).astype(jnp.float32),
        lax.psum_scatter(
            acc_down[None].astype(jnp.bfloat16), "dp", scatter_dimension=2, tiled=True
        ).astype(jnp.float32),
    )
    return (
        grad_tokens,
        grad_route,
        summed[0].astype(jnp.bfloat16),
        summed[1].astype(jnp.bfloat16),
        summed[2].astype(jnp.bfloat16),
    )


def fused_kernel(
    tok_hbm, cot_hbm, ids_hbm, rw_hbm, wg_hbm, wu_hbm, wdn_hbm,
    gt_ref, route_ref, gg_ref, gu_ref, gd_ref,
    ids_ref, rw_ref, wg, wu, wdn, wgt, wut, wdt, tc, wd, wbuf, wcol, cols, colst, act_buf, fac_buf, hid_buf,
    hw_own, hw_recv, gp_own, gp_recv, part, fs, fr, bs, br, xs, xr, rs, rr,
    l_sem, w_sem, g_send, g_recv, c_send, c_recv, h_send, h_done, f_sem, b_sem, x_sem, r_sem,
):
    ep_size = lax.axis_size("ep")
    groups = lax.axis_size("dp")
    count = tok_hbm.shape[0]
    col = tc.shape[3]
    model = wdn.shape[1]
    tiles, rows, ft = hw_own.shape
    ep = lax.axis_index("ep")
    dp = lax.axis_index("dp")
    z, y = ep // 2, ep % 2
    q, i = z // 2, z % 2
    xx, core = dp // 2, dp % 2
    peers_dp = (xx * 2 + 1 - core, (1 - xx) * 2 + core, (1 - xx) * 2 + 1 - core)
    inner = i != q
    outer = i == q
    zline = (z, z + 1 - 2 * i, z + 2 - 4 * q, 3 - z)
    targets = tuple(zline[s // 2] * 2 + (1 - y if s % 2 else y) for s in range(8))
    ynb, znb, twin, facing = targets[1], targets[2], targets[4], targets[6]
    inside = (i + q) % 2
    near = 4 + 2 * inside
    far = 6 - 2 * inside
    starts = (0, lead)
    sizes = (lead, 8 - lead)
    early = lead - 2
    f32 = jnp.float32
    bf16 = jnp.bfloat16

    def span(index, size):
        return pl.ds(pl.multiple_of(index * size, size), size)

    def remote(src, dst, send, recv, ep_to, dp_to):
        return pltpu.make_async_remote_copy(
            src_ref=src, dst_ref=dst, send_sem=send, recv_sem=recv,
            device_id=(ep_to, dp_to), device_id_type=pl.DeviceIdType.MESH,
        )

    loads = [
        [
            pltpu.make_async_copy(ref.at[:, pl.ds(j * col, col)], tc.at[k, j, pl.ds(0, count)], l_sem.at[k])
            for j in range(groups)
        ]
        for k, ref in enumerate((tok_hbm, cot_hbm))
    ]
    for group in loads:
        for load in group:
            load.start()
    lists = (
        pltpu.make_async_copy(ids_hbm, ids_ref, l_sem.at[2]),
        pltpu.make_async_copy(rw_hbm, rw_ref, l_sem.at[3]),
    )
    for load in lists:
        load.start()
    w_loads = [
        pltpu.make_async_copy(src, dst, l_sem.at[4 + k])
        for k, (src, dst) in enumerate(((wg_hbm, wg), (wu_hbm, wu), (wdn_hbm, wdn)))
    ]

    for k in (2, 0, 1):
        w_loads[k].start()
    barrier = pltpu.get_barrier_semaphore()
    for k in range(1, ep_size):
        pl.semaphore_signal(
            barrier, inc=1, device_id=((ep + k) % ep_size, dp), device_id_type=pl.DeviceIdType.MESH
        )
    for peer in peers_dp:
        pl.semaphore_signal(barrier, inc=1, device_id=(ep, peer), device_id_type=pl.DeviceIdType.MESH)
    pl.semaphore_wait(barrier, ep_size - 1 + len(peers_dp))

    def view(k, slot):
        place = span(slot, count)
        return cols.at[1, pl.ds(1, 2), place] if k == 2 else tc.at[k, :, place]

    def hop(k, slot, there, late, ep_to):
        remote(view(k, slot), view(k, there), g_send.at[0], g_recv.at[k, there], ep_to, dp).start()

    def got(k, slot):
        remote(view(k, slot), view(k, slot), g_send.at[0], g_recv.at[k, slot], ynb, dp).wait_recv()

    def share(k, slot, every=False):
        if k == 2:
            return
        for r in (1, 2, 0) if k == 0 or every else (0,):
            peer = peers_dp[r]
            remote(
                tc.at[k, peer, span(slot, count)], cols.at[k, r, span(slot, count)],
                c_send.at[0], c_recv.at[0 if k == 0 else 1 if r == 0 else 2], ep, peer,
            ).start()

    def take(k, slot):
        got(k, slot)
        share(k, slot)

    def own_out(k):
        hop(k, 0, 1, 0, ynb)
        hop(k, 0, 2, 0, znb)

        @pl.when(inner)
        def _():
            hop(k, 0, 6, 1, facing)

    def pair_out(k):
        got(k, 2)
        hop(k, 2, 3, 0, ynb)

        @pl.when(inner)
        def _():
            hop(k, 2, 4, 1, facing)

        share(k, 2)
        take(k, 1)

    def side_out():
        @pl.when(inner)
        def _():
            hop(0, 1, 7, 1, facing)
            hop(1, 1, 7, 1, facing)

    def half(part, slot):
        return tc.at[1, pl.ds(part * (groups // 2), groups // 2), span(slot, count)]

    def half_copy(part, slot, there, mark, ep_to):
        return remote(half(part, slot), half(part, there), g_send.at[0], g_recv.at[1, mark], ep_to, dp)

    def last_pass():
        @pl.when(outer)
        def _():
            got(1, 6)
            half_copy(0, 6, 7, 7, ynb).start()
            share(1, 6)

    def last_take():
        @pl.when(inner)
        def _():
            got(1, 5)
            half_copy(1, 5, 7, 0, znb).start()

        @pl.when(outer)
        def _():
            half_copy(0, 7, 7, 7, ynb).wait_recv()
            half_copy(1, 7, 7, 0, znb).wait_recv()

        share(1, far + 1)

    def take_side(k):
        got(k, near + 1)
        share(k, near + 1)

    def facing_out(k):
        @pl.when(inner)
        def _():
            got(k, 2)
            hop(k, 2, 4, 1, facing)

    def diag_out(k):
        @pl.when(outer)
        def _():
            got(k, 2)

        got(k, 1)
        hop(k, 1, 3, 0, znb)

    def inner_pass(k, slot, sideways=True):
        @pl.when(inner)
        def _():
            got(k, slot)
            hop(k, slot, 10 - slot, 1, znb)
            if sideways:
                hop(k, slot, slot + 1, 1, ynb)
            share(k, slot)

    def outer_pass(k, slot, sideways=True):
        @pl.when(outer)
        def _():
            got(k, slot)
            if sideways:
                hop(k, slot, slot + 1, 1, ynb)
            share(k, slot)

    pltpu.make_async_copy(view(0, 0), view(0, 0), l_sem.at[0]).wait()
    own_out(0)
    share(0, 0, True)
    wd[...] = jnp.zeros(wd.shape, f32)
    rs[...] = jnp.zeros(rs.shape, f32)
    for load in lists:
        load.wait()
    ids = ids_ref[...]
    values = rw_ref[...].astype(f32)
    for e in range(ep_size):
        line = jnp.sum(jnp.where(ids == e, values, 0.0), axis=0, keepdims=True)
        wd[e, :, 0:count] = jnp.broadcast_to(line, (wd.shape[1], count))
    for s in range(1, 8):
        remote(wd.at[targets[s]], wbuf.at[s], w_sem.at[0], w_sem.at[1 if s < lead else 2], targets[s], dp).start()
    keep_w = pltpu.make_async_copy(wd.at[ep], wbuf.at[0], w_sem.at[1])
    keep_w.start()
    pltpu.make_async_copy(view(1, 0), view(1, 0), l_sem.at[1]).wait()
    own_out(1)
    share(1, 0, True)

    def wave_rows(wave):
        return pl.ds(starts[wave] * count, sizes[wave] * count)

    def gate_step(wave):
        block = wave_rows(wave)
        half = sizes[wave] * count

        def step(t, carry):
            lanes = span(t, ft)
            gate_pre = jnp.zeros((half, ft), f32)
            up_pre = jnp.zeros((half, ft), f32)
            for j in range(groups):
                depth = pl.ds(j * col, col)
                gate_pre += jnp.dot(tc[0, j, block], wg[depth, lanes], preferred_element_type=f32)
                up_pre += jnp.dot(tc[0, j, block], wu[depth, lanes], preferred_element_type=f32)
            act, slope = silu_parts(gate_pre)
            product = act * up_pre
            weight = wcol[block, 0:1]
            hw_own[t, block] = (weight * product).astype(bf16)
            act_buf[t, block] = act
            fac_buf[t, block] = up_pre * slope
            hid_buf[t, block] = product.astype(bf16)
            for r in (1, 0):
                done = h_done.at[1 + wave] if r == 1 else h_done.at[0]
                remote(
                    hw_own.at[t, block], hw_recv.at[r, t, block], h_send.at[0], done, ep, peers_dp[r]
                ).start()
            return carry

        lax.fori_loop(0, tiles, step, 0)

    def back_step(wave):
        block = wave_rows(wave)
        weight = wcol[block, 0:1]
        half = sizes[wave] * count

        def step(t, route):
            back = jnp.zeros((half, ft), f32)
            for j in range(groups):
                back += jnp.dot(tc[1, j, block], wdt[pl.ds(j * col, col), span(t, ft)], preferred_element_type=f32)
            scaled = weight * back
            gp_own[t, 0, block] = (scaled * fac_buf[t, block]).astype(bf16)
            gp_own[t, 1, block] = (scaled * act_buf[t, block]).astype(bf16)
            route = route + jnp.sum(hid_buf[t, block].astype(f32) * back, axis=1, keepdims=True)
            for r in (1, 0):
                done = h_done.at[(5 + wave) + wave * t] if r == 1 else h_done.at[4]
                remote(
                    gp_own.at[t, :, block], gp_recv.at[r, t, :, block], h_send.at[1], done, ep, peers_dp[r]
                ).start()
            return route

        route = lax.fori_loop(0, tiles, step, jnp.zeros((half, 1), f32))
        lined = jnp.broadcast_to(route, (half, 128)).T
        for p in range(sizes[wave]):
            line = lined[0:1, p * count:(p + 1) * count]
            rs[starts[wave] + p, :, 0:count] = jnp.broadcast_to(line, (rs.shape[1], count))

    def fold_send(n, mode, phase):
        place = pl.ds(early * phase, early + (4 - 2 * early) * phase)
        done = f_sem.at[1 + phase * (1 + n)]
        to = ynb + mode * (znb - ynb)
        return remote(fs.at[n, place], fr.at[n, place], f_sem.at[0], done, to, dp)

    def fold_rows(n, mode, phase):
        for j in ((range(early), range(early, 4))[phase]):
            source = 2 * j + 1 + mode * (1 - j % 2)
            fs[n, j] = part[n, source].astype(bf16)

    def slot_step(wave):
        block = wave_rows(wave)
        size = sizes[wave]

        def step(turn, carry):
            n = turn % 2 * (groups // 2) + turn // 2
            total = jnp.zeros((size * count, col), f32)
            for t in range(tiles):
                depth = pl.ds(t * ft, ft)
                if wave == 0:
                    total += lax.dot_general(
                        gp_own[t, 0, block], wg[span(n, col), depth], contract_last, preferred_element_type=f32
                    )
                    total += lax.dot_general(
                        gp_own[t, 1, block], wu[span(n, col), depth], contract_last, preferred_element_type=f32
                    )
                else:
                    total += jnp.dot(gp_own[t, 0, block], wgt[depth, span(n, col)], preferred_element_type=f32)
                    total += jnp.dot(gp_own[t, 1, block], wut[depth, span(n, col)], preferred_element_type=f32)
            part[n, pl.ds(starts[wave], size)] = total.reshape(size, count, col)
            mode = n // along_y
            fold_rows(n, mode, wave)
            if wave == 1:
                fold_send(n, mode, 1).start()
            return carry

        lax.fori_loop(0, groups, step, 0)

    def fold_early(where):
        @pl.when(where)
        def _():
            def step(n, carry):
                fold_send(n, n // along_y, 0).start()
                return carry

            lax.fori_loop(0, groups, step, 0)

    def fold_ready():
        ref = fr.at[:, pl.ds(0, early)]
        remote(ref, ref, f_sem.at[0], f_sem.at[1], ynb, dp).wait_recv()

    def fold_mid(n):
        mode = n // along_y
        fold_send(n, mode, 1).wait_recv()
        bs[n, 0] = (part[n, 2 - mode] + fr[n, 1].astype(f32)).astype(bf16)
        bs[n, 1] = (part[n, 6 - mode] + fr[n, 3].astype(f32)).astype(bf16)
        remote(bs.at[n], br.at[n], f_sem.at[0], b_sem.at[n], (znb, ynb)[mode], dp).start()

    def fold_cross(n):
        remote(bs.at[n], br.at[n], f_sem.at[0], b_sem.at[n], znb, dp).wait_recv()
        xs[n] = (part[n, 4] + fr[n, 2].astype(f32) + br[n, 1].astype(f32)).astype(bf16)
        remote(xs.at[n], xr.at[n], f_sem.at[0], x_sem.at[0], twin, dp).start()

    def pass_hidden(wave):
        block = wave_rows(wave)
        ref = hw_recv.at[1, :, block]
        remote(ref, ref, h_send.at[0], h_done.at[1 + wave], ep, peers_dp[1]).wait_recv()
        remote(ref, hw_recv.at[2, :, block], h_send.at[0], h_done.at[0], ep, peers_dp[0]).start()

    def pass_grad_first():
        ref = gp_recv.at[1, :, :, wave_rows(0)]
        remote(ref, ref, h_send.at[1], h_done.at[5], ep, peers_dp[1]).wait_recv()
        remote(ref, gp_recv.at[2, :, :, wave_rows(0)], h_send.at[1], h_done.at[6 + tiles], ep, peers_dp[0]).start()

    def pass_grad(t):
        ref = gp_recv.at[1, t, :, wave_rows(1)]
        remote(ref, ref, h_send.at[1], h_done.at[6 + t], ep, peers_dp[1]).wait_recv()
        remote(
            ref, gp_recv.at[2, t, :, wave_rows(1)], h_send.at[1], h_done.at[7 + tiles + t], ep, peers_dp[0]
        ).start()

    def take_weights(wave):
        start, size = starts[wave], sizes[wave]
        ref = wbuf.at[pl.ds(start, size)]
        remote(ref, ref, w_sem.at[0], w_sem.at[1 + wave], ynb, dp).wait_recv()
        step = wbuf.shape[1]
        flat = wbuf[start:start + size].reshape(size * step, wbuf.shape[2])
        turned = jnp.concatenate([flat, jnp.zeros((128 - size * step, wbuf.shape[2]), f32)], axis=0).T
        for p in range(size):
            line = turned[0:count, p * step:p * step + 1]
            wcol[pl.ds((start + p) * count, count), :] = jnp.broadcast_to(line, (count, 128))

    def turn_down():
        def step(t, carry):
            for j in range(groups):
                wdt[pl.ds(j * col, col), span(t, ft)] = wdn[span(t, ft), pl.ds(j * col, col)].T
            return carry

        lax.fori_loop(0, tiles, step, 0)

    def turn_up():
        def step(n, carry):
            for t in range(tiles):
                wgt[pl.ds(t * ft, ft), span(n, col)] = wg[span(n, col), pl.ds(t * ft, ft)].T
                wut[pl.ds(t * ft, ft), span(n, col)] = wu[span(n, col), pl.ds(t * ft, ft)].T
            return carry

        lax.fori_loop(0, groups, step, 0)

    w_loads[2].wait()
    turn_down()
    pair_out(0)
    for load in w_loads[0:2]:
        load.wait()
    take_weights(0)
    gate_step(0)
    inner_pass(0, near, False)
    pair_out(1)
    side_out()
    back_step(0)
    inner_pass(0, far)
    slot_step(0)
    inner_pass(1, near, False)
    inner_pass(1, far)
    ref = cols.at[1, pl.ds(1, 2), pl.ds(0, count)]
    remote(ref, ref, c_send.at[0], c_recv.at[2], ep, peers_dp[1]).wait_recv()
    own_out(2)
    outer_pass(0, near)
    turn_up()
    facing_out(2)
    outer_pass(0, far)
    if lead == 3:
        take(0, 3)
    take_side(0)
    outer_pass(1, near)
    last_pass()
    take(0, far + 1)
    take_weights(1)
    gate_step(1)
    fold_early(outer)
    pass_hidden(0)
    if lead == 3:
        take(1, 3)
    take_side(1)
    last_take()
    fold_early(inner)
    back_step(1)
    diag_out(2)
    inner_pass(2, near)
    inner_pass(2, far)
    slot_step(1)
    for s in range(1, 8):
        remote(rs.at[s], rr.at[ep], r_sem.at[0], r_sem.at[1], targets[s], dp).start()
    pltpu.make_async_copy(rs.at[0], rr.at[ep], r_sem.at[1]).start()
    outer_pass(2, near)
    outer_pass(2, far)
    pass_grad_first()
    fold_ready()
    fold_mid(0)
    fold_mid(2)
    remote(cols.at[0], cols.at[0], c_send.at[0], c_recv.at[0], ep, peers_dp[0]).wait_recv()
    colst[0] = tc[0, dp].T
    for r in range(3):
        colst[1 + r] = cols[0, r].T
    fold_mid(1)
    fold_mid(3)
    pass_hidden(1)
    remote(cols.at[1, 0], cols.at[1, 0], c_send.at[0], c_recv.at[1], ep, peers_dp[0]).wait_recv()
    remote(gp_recv.at[0], gp_recv.at[0], h_send.at[1], h_done.at[4], ep, peers_dp[0]).wait_recv()
    ref = gp_recv.at[2, :, :, wave_rows(0)]
    remote(ref, ref, h_send.at[1], h_done.at[6 + tiles], ep, peers_dp[0]).wait_recv()

    def down_tile(t):
        blocks = [hw_own.at[t]] + [hw_recv.at[r, t] for r in range(3)]
        cots = [tc.at[1, dp]] + [cols.at[1, r] for r in range(3)]
        grad_down = jnp.zeros((ft, col), f32)
        for g in range(4):
            grad_down += lax.dot_general(blocks[g][...], cots[g][...], contract_first, preferred_element_type=f32)
        gd_ref[span(t, ft), :] = grad_down.astype(bf16)

    def sum_all():
        remote(xs, xr, f_sem.at[0], x_sem.at[0], twin, dp).wait_recv()

        def step(n, carry):
            total = part[n, 0] + fr[n, 0].astype(f32) + br[n, 0].astype(f32) + xr[n].astype(f32)
            gt_ref[:, span(n, col)] = total.astype(bf16)
            return carry

        lax.fori_loop(0, groups, step, 0)

    def weight_tile(t):
        ref = gp_recv.at[2, t, :, wave_rows(1)]
        remote(ref, ref, h_send.at[1], h_done.at[7 + tiles + t], ep, peers_dp[0]).wait_recv()
        blocks = [gp_own.at[t]] + [gp_recv.at[r, t] for r in range(3)]
        grad_gate = jnp.zeros((col, ft), f32)
        grad_up = jnp.zeros((col, ft), f32)
        for g in range(4):
            grad_gate += jnp.dot(colst[g], blocks[g][0], preferred_element_type=f32)
            grad_up += jnp.dot(colst[g], blocks[g][1], preferred_element_type=f32)
        gg_ref[:, span(t, ft)] = grad_gate.astype(bf16)
        gu_ref[:, span(t, ft)] = grad_up.astype(bf16)

    def down_ready():
        got(2, 3)
        got(2, near + 1)
        got(2, far + 1)
        ref = hw_recv.at[pl.ds(0, 2)]
        remote(ref, ref, h_send.at[0], h_done.at[0], ep, peers_dp[0]).wait_recv()

    pass_grad(0)
    fold_cross(0)
    fold_cross(2)
    fold_cross(1)
    fold_cross(3)
    for t in range(1, tiles - 1):
        pass_grad(t)
    weight_tile(0)
    down_ready()
    for t in range(tiles):
        down_tile(t)
    pass_grad(tiles - 1)
    for t in range(1, tiles):
        weight_tile(t)
    sum_all()

    remote(rr, rr, r_sem.at[0], r_sem.at[1], ynb, dp).wait_recv()
    table = jnp.zeros(ids.shape, f32)
    for e in range(ep_size):
        table = table + jnp.where(ids == e, rr[e, 0:1, 0:count], 0.0)
    route_ref[...] = table.astype(bf16)

    def sent(ref, sem):
        remote(ref, ref, sem, r_sem.at[1], ynb, dp).wait_send()

    sent(rs.at[pl.ds(0, ep_size - 1)], r_sem.at[0])
    sent(wd.at[pl.ds(0, ep_size - 1)], w_sem.at[0])
    sent(wdn.at[pl.ds(0, (7 * groups * count * col) // model)], f_sem.at[0])
    unit = (groups * count * col) // model

    @pl.when(inner)
    def _():
        sent(wdn.at[pl.ds(0, 18 * unit + 10 * unit // 2)], g_send.at[0])

    @pl.when(outer)
    def _():
        sent(wdn.at[pl.ds(0, 10 * unit + 4 * unit // 2)], g_send.at[0])

    sent(wdn.at[pl.ds(0, (34 * count * col) // model)], c_send.at[0])
    sent(hw_recv, h_send.at[0])
    sent(gp_recv, h_send.at[1])


def store_kernel(*refs):
    sems = refs[-1]
    each = (len(refs) - 1) // 2
    copies = []
    for k in range(each):
        size = refs[k].shape[0]
        pieces = store_pieces if size % (16 * store_pieces) == 0 else 1
        step = size // pieces
        for p in range(pieces):
            place = pl.ds(p * step, step)
            copies.append(pltpu.make_async_copy(refs[k].at[place], refs[each + k].at[place], sems.at[k]))
    for copy in copies:
        copy.start()
    for k in range(each):
        pltpu.make_async_copy(refs[k], refs[each + k], sems.at[k]).wait()


def fused_body(tokens, cotangent, expert_ids, route_weights, w_gate, w_up, w_down):
    count, topk = expert_ids.shape
    model = tokens.shape[1]
    experts = lax.axis_size("ep")
    groups = lax.axis_size("dp")
    width = w_gate.shape[2]
    rows = experts * count
    col = model // groups
    ft = 256 if width % 256 == 0 else width
    tiles = width // ft
    lanes = 128
    bf16 = jnp.bfloat16
    f32 = jnp.float32
    any_spec = pl.BlockSpec(memory_space=pl.ANY)
    hbm = pl.BlockSpec(memory_space=pltpu.HBM)
    vmem = pl.BlockSpec(memory_space=pltpu.VMEM)
    dma = pltpu.SemaphoreType.DMA
    small = (experts, 8, lanes)
    shapes = ((count, model), (topk, count), (col, width), (col, width), (width, col))
    outs = pl.pallas_call(
        fused_kernel,
        name="fused_layer",
        out_shape=tuple(pltpu.VMEM(shape, bf16) for shape in shapes),
        in_specs=[hbm] * 7,
        out_specs=(vmem,) * 5,
        scratch_shapes=[
            pltpu.VMEM((topk, count), jnp.int32),
            pltpu.VMEM((topk, count), bf16),
            pltpu.VMEM((model, width), bf16),
            pltpu.VMEM((model, width), bf16),
            pltpu.VMEM((width, model), bf16),
            pltpu.VMEM((width, model), bf16),
            pltpu.VMEM((width, model), bf16),
            pltpu.VMEM((model, width), bf16),
            pltpu.VMEM((2, groups, rows, col), bf16),
            pltpu.VMEM(small, f32),
            pltpu.VMEM(small, f32),
            pltpu.VMEM((rows, lanes), f32),
            pltpu.VMEM((2, 3, rows, col), bf16),
            pltpu.VMEM((4, col, rows), bf16),
            pltpu.VMEM((tiles, rows, ft), f32),
            pltpu.VMEM((tiles, rows, ft), f32),
            pltpu.VMEM((tiles, rows, ft), bf16),
            pltpu.VMEM((tiles, rows, ft), bf16),
            pltpu.VMEM((3, tiles, rows, ft), bf16),
            pltpu.VMEM((tiles, 2, rows, ft), bf16),
            pltpu.VMEM((3, tiles, 2, rows, ft), bf16),
            pltpu.VMEM((groups, 8, count, col), f32),
            pltpu.VMEM((groups, 4, count, col), bf16),
            pltpu.VMEM((groups, 4, count, col), bf16),
            pltpu.VMEM((groups, 2, count, col), bf16),
            pltpu.VMEM((groups, 2, count, col), bf16),
            pltpu.VMEM((groups, count, col), bf16),
            pltpu.VMEM((groups, count, col), bf16),
            pltpu.VMEM(small, f32),
            pltpu.VMEM(small, f32),
            dma((7,)),
            dma((3,)),
            dma((1,)),
            dma((3, experts)),
            dma((1,)),
            dma((3,)),
            dma((2,)),
            dma((7 + 2 * tiles,)),
            dma((2 + groups,)),
            dma((groups,)),
            dma((1,)),
            dma((2,)),
        ],
        compiler_params=pltpu.CompilerParams(
            collective_id=0, has_side_effects=True, vmem_limit_bytes=64200000
        ),
    )(tokens, cotangent, expert_ids.T, route_weights.T, w_gate[0], w_up[0], w_down[0])
    outs = pl.pallas_call(
        store_kernel,
        name="store_results",
        out_shape=tuple(jax.ShapeDtypeStruct(shape, bf16) for shape in shapes),
        in_specs=[any_spec] * 5,
        out_specs=(any_spec,) * 5,
        scratch_shapes=[dma((5,))],
        compiler_params=pltpu.CompilerParams(vmem_limit_bytes=4 * 1024 * 1024),
    )(*outs)
    grad_tokens, grad_route, grad_gate, grad_up, grad_down = outs
    return grad_tokens, grad_route.T, grad_gate[None], grad_up[None], grad_down[None]


def body(tokens, cotangent, expert_ids, route_weights, w_gate, w_up, w_down):
    tok_count, topk = expert_ids.shape
    experts = lax.axis_size("ep")
    whole = 2 * tok_count * topk // experts >= tok_count
    width = w_gate.shape[2]
    paired = lax.axis_size("dp") == 4 and experts == 8 and tok_count == 32
    paired = paired and width % 256 == 0 and width >= 24 * tok_count
    chosen = fused_body if whole and paired else routed_body
    return chosen(tokens, cotangent, expert_ids, route_weights, w_gate, w_up, w_down)


def solution(mesh):
    return jax.shard_map(
        body,
        mesh=mesh,
        in_specs=(
            P(("ep", "dp"), None),
            P(("ep", "dp"), None),
            P(("ep", "dp"), None),
            P(("ep", "dp"), None),
            P("ep", None, None),
            P("ep", None, None),
            P("ep", None, None),
        ),
        out_specs=(
            P(("ep", "dp"), None),
            P(("ep", "dp"), None),
            P("ep", "dp", None),
            P("ep", "dp", None),
            P("ep", None, "dp"),
        ),
        check_vma=False,
    )
```

```python
import jax
import jax.numpy as jnp
from jax import lax
from jax.experimental import pallas as pl
from jax.experimental.pallas import tpu as pltpu
from jax.sharding import PartitionSpec as P

block_rows = 128
lead = 3
store_pieces = 4
along_y = 2
contract_last = (((1,), (1,)), ((), ()))
contract_first = (((0,), (0,)), ((), ()))


def silu_parts(gate_pre):
    sig = jax.nn.sigmoid(gate_pre)
    return (gate_pre * sig, sig * (1.0 + gate_pre * (1.0 - sig)))


def expert_pass(rows_x, rows_cot, rows_w, live_count, w_gate_one, w_up_one, w_down_one):
    total, model = rows_x.shape
    width = w_gate_one.shape[1]

    def step(index, carry):
        acc_gate, acc_up, acc_down, slot_grad, route_grad = carry
        start = index * block_rows
        tok = lax.dynamic_slice_in_dim(rows_x, start, block_rows, 0)
        cot = lax.dynamic_slice_in_dim(rows_cot, start, block_rows, 0)
        weight = lax.dynamic_slice_in_dim(rows_w, start, block_rows, 0).astype(jnp.float32)[:, None]
        gate_pre = jnp.dot(tok, w_gate_one, preferred_element_type=jnp.float32)
        up_pre = jnp.dot(tok, w_up_one, preferred_element_type=jnp.float32)
        act, slope = silu_parts(gate_pre)
        hidden = lax.optimization_barrier((act * up_pre).astype(jnp.bfloat16))
        back = lax.dot_general(cot, w_down_one, contract_last, preferred_element_type=jnp.float32)
        route_part = jnp.sum(hidden.astype(jnp.float32) * back, axis=1)
        scaled = weight * back
        grad_gate_pre = (scaled * up_pre * slope).astype(jnp.bfloat16)
        grad_up_pre = (scaled * act).astype(jnp.bfloat16)
        scaled_cot = (weight * cot.astype(jnp.float32)).astype(jnp.bfloat16)
        part = lax.dot_general(
            grad_gate_pre, w_gate_one, contract_last, preferred_element_type=jnp.float32
        )
        part = part + lax.dot_general(
            grad_up_pre, w_up_one, contract_last, preferred_element_type=jnp.float32
        )
        acc_gate = acc_gate + lax.dot_general(
            tok, grad_gate_pre, contract_first, preferred_element_type=jnp.float32
        )
        acc_up = acc_up + lax.dot_general(
            tok, grad_up_pre, contract_first, preferred_element_type=jnp.float32
        )
        acc_down = acc_down + lax.dot_general(
            hidden, scaled_cot, contract_first, preferred_element_type=jnp.float32
        )
        slot_grad = lax.dynamic_update_slice_in_dim(slot_grad, part, start, 0)
        route_grad = lax.dynamic_update_slice_in_dim(route_grad, route_part, start, 0)
        return (acc_gate, acc_up, acc_down, slot_grad, route_grad)

    init = (
        jnp.zeros((model, width), jnp.float32),
        jnp.zeros((model, width), jnp.float32),
        jnp.zeros((width, model), jnp.float32),
        jnp.zeros((total, model), jnp.float32),
        jnp.zeros((total,), jnp.float32),
    )
    block_count = (live_count + block_rows - 1) // block_rows
    return lax.fori_loop(0, block_count, step, init)


def routed_body(tokens, cotangent, expert_ids, route_weights, w_gate, w_up, w_down):
    tok_count, topk = expert_ids.shape
    model = tokens.shape[1]
    experts = lax.axis_size("ep")
    capacity = min(tok_count, 2 * tok_count * topk // experts)
    slots = tok_count * topk
    row_total = experts * capacity
    flat_ids = expert_ids.reshape(slots)
    onehot = (flat_ids[:, None] == jnp.arange(experts, dtype=jnp.int32)[None, :]).astype(jnp.int32)
    position = jnp.sum((jnp.cumsum(onehot, axis=0) - 1) * onehot, axis=1)
    slot_ids = jnp.arange(slots, dtype=jnp.int32)
    source = (
        jnp.full((row_total,), slots, jnp.int32).at[flat_ids * capacity + position].set(slot_ids)
    )
    filled = source < slots
    source_token = jnp.where(filled, source // topk, tok_count)
    joined = jnp.concatenate([tokens, cotangent], axis=1)
    picked = jnp.take(joined, source_token, axis=0, mode="fill", fill_value=0)
    send_x = picked[:, :model].reshape(experts, capacity, model)
    send_cot = picked[:, model:].reshape(experts, capacity, model)
    send_w = jnp.take(
        route_weights.reshape(slots), jnp.where(filled, source, slots), mode="fill", fill_value=0
    ).reshape(experts, capacity)
    recv_x, recv_cot, recv_w = (
        lax.all_to_all(send_x, "ep", split_axis=0, concat_axis=0, tiled=True),
        lax.all_to_all(send_cot, "ep", split_axis=0, concat_axis=0, tiled=True),
        lax.all_to_all(send_w, "ep", split_axis=0, concat_axis=0, tiled=True),
    )
    flat_w = recv_w.reshape(row_total)
    live = (flat_w != 0).astype(jnp.int32)
    live_count = jnp.sum(live)
    place = jnp.where(live > 0, jnp.cumsum(live) - 1, row_total)
    anchor = (
        jnp.full((row_total,), row_total, jnp.int32)
        .at[place]
        .set(jnp.arange(row_total, dtype=jnp.int32), mode="drop")
    )
    recv_joined = jnp.concatenate(
        [recv_x.reshape(row_total, model), recv_cot.reshape(row_total, model)], axis=1
    )
    packed = jnp.take(recv_joined, anchor, axis=0, mode="fill", fill_value=0)
    pack_x = packed[:, :model]
    pack_cot = packed[:, model:]
    pack_w = jnp.take(flat_w, anchor, mode="fill", fill_value=0)
    w_gate_one = w_gate[0]
    w_up_one = w_up[0]
    w_down_one = w_down[0]
    acc_gate, acc_up, acc_down, slot_grad, route_grad = expert_pass(
        pack_x, pack_cot, pack_w, live_count, w_gate_one, w_up_one, w_down_one
    )
    slot_rows = jnp.take(slot_grad, place, axis=0, mode="fill", fill_value=0.0).astype(jnp.bfloat16)
    route_rows = jnp.take(route_grad, place, axis=0, mode="fill", fill_value=0.0).astype(
        jnp.bfloat16
    )
    back_x, back_route_rows = (
        lax.all_to_all(
            slot_rows.reshape(experts, capacity, model),
            "ep",
            split_axis=0,
            concat_axis=0,
            tiled=True,
        ),
        lax.all_to_all(
            route_rows.reshape(experts, capacity), "ep", split_axis=0, concat_axis=0, tiled=True
        ),
    )
    mine_rows = back_x[flat_ids, position].reshape(tok_count, topk, model)
    grad_tokens = jnp.sum(mine_rows.astype(jnp.float32), axis=1).astype(jnp.bfloat16)
    grad_route = back_route_rows[flat_ids, position].reshape(tok_count, topk)
    summed = (
        lax.psum_scatter(
            acc_gate[None].astype(jnp.bfloat16), "dp", scatter_dimension=1, tiled=True
        ).astype(jnp.float32),
        lax.psum_scatter(
            acc_up[None].astype(jnp.bfloat16), "dp", scatter_dimension=1, tiled=True
        ).astype(jnp.float32),
        lax.psum_scatter(
            acc_down[None].astype(jnp.bfloat16), "dp", scatter_dimension=2, tiled=True
        ).astype(jnp.float32),
    )
    return (
        grad_tokens,
        grad_route,
        summed[0].astype(jnp.bfloat16),
        summed[1].astype(jnp.bfloat16),
        summed[2].astype(jnp.bfloat16),
    )


def fused_kernel(
    tok_hbm, cot_hbm, ids_hbm, rw_hbm, wg_hbm, wu_hbm, wdn_hbm,
    gt_ref, route_ref, gg_ref, gu_ref, gd_ref,
    ids_ref, rw_ref, wg, wu, wdn, wgt, wut, wdt, tc, wd, wbuf, wcol, cols, colst, act_buf, fac_buf, hid_buf,
    hw_own, hw_recv, gp_own, gp_recv, part, fs, fr, bs, br, xs, xr, rs, rr,
    l_sem, w_sem, g_send, g_recv, c_send, c_recv, h_send, h_done, f_sem, b_sem, x_sem, r_sem,
):
    ep_size = lax.axis_size("ep")
    groups = lax.axis_size("dp")
    count = tok_hbm.shape[0]
    col = tc.shape[3]
    model = wdn.shape[1]
    tiles, rows, ft = hw_own.shape
    ep = lax.axis_index("ep")
    dp = lax.axis_index("dp")
    z, y = ep // 2, ep % 2
    q, i = z // 2, z % 2
    xx, core = dp // 2, dp % 2
    peers_dp = (xx * 2 + 1 - core, (1 - xx) * 2 + core, (1 - xx) * 2 + 1 - core)
    inner = i != q
    outer = i == q
    zline = (z, z + 1 - 2 * i, z + 2 - 4 * q, 3 - z)
    targets = tuple(zline[s // 2] * 2 + (1 - y if s % 2 else y) for s in range(8))
    ynb, znb, twin, facing = targets[1], targets[2], targets[4], targets[6]
    inside = (i + q) % 2
    near = 4 + 2 * inside
    far = 6 - 2 * inside
    starts = (0, lead)
    sizes = (lead, 8 - lead)
    early = lead - 2
    f32 = jnp.float32
    bf16 = jnp.bfloat16

    def span(index, size):
        return pl.ds(pl.multiple_of(index * size, size), size)

    def remote(src, dst, send, recv, ep_to, dp_to):
        return pltpu.make_async_remote_copy(
            src_ref=src, dst_ref=dst, send_sem=send, recv_sem=recv,
            device_id=(ep_to, dp_to), device_id_type=pl.DeviceIdType.MESH,
        )

    loads = [
        [
            pltpu.make_async_copy(ref.at[:, pl.ds(j * col, col)], tc.at[k, j, pl.ds(0, count)], l_sem.at[k])
            for j in range(groups)
        ]
        for k, ref in enumerate((tok_hbm, cot_hbm))
    ]
    for group in loads:
        for load in group:
            load.start()
    lists = (
        pltpu.make_async_copy(ids_hbm, ids_ref, l_sem.at[2]),
        pltpu.make_async_copy(rw_hbm, rw_ref, l_sem.at[3]),
    )
    for load in lists:
        load.start()
    w_loads = [
        pltpu.make_async_copy(src, dst, l_sem.at[4 + k])
        for k, (src, dst) in enumerate(((wg_hbm, wg), (wu_hbm, wu), (wdn_hbm, wdn)))
    ]

    for k in (2, 0, 1):
        w_loads[k].start()
    barrier = pltpu.get_barrier_semaphore()
    for k in range(1, ep_size):
        pl.semaphore_signal(
            barrier, inc=1, device_id=((ep + k) % ep_size, dp), device_id_type=pl.DeviceIdType.MESH
        )
    for peer in peers_dp:
        pl.semaphore_signal(barrier, inc=1, device_id=(ep, peer), device_id_type=pl.DeviceIdType.MESH)
    pl.semaphore_wait(barrier, ep_size - 1 + len(peers_dp))

    def view(k, slot):
        place = span(slot, count)
        return cols.at[1, pl.ds(1, 2), place] if k == 2 else tc.at[k, :, place]

    def hop(k, slot, there, late, ep_to):
        remote(view(k, slot), view(k, there), g_send.at[0], g_recv.at[k, there], ep_to, dp).start()

    def got(k, slot):
        remote(view(k, slot), view(k, slot), g_send.at[0], g_recv.at[k, slot], ynb, dp).wait_recv()

    def share(k, slot, every=False):
        if k == 2:
            return
        for r in (1, 2, 0) if k == 0 or every else (0,):
            peer = peers_dp[r]
            remote(
                tc.at[k, peer, span(slot, count)], cols.at[k, r, span(slot, count)],
                c_send.at[0], c_recv.at[0 if k == 0 else 1 if r == 0 else 2], ep, peer,
            ).start()

    def take(k, slot):
        got(k, slot)
        share(k, slot)

    def own_out(k):
        hop(k, 0, 1, 0, ynb)
        hop(k, 0, 2, 0, znb)

        @pl.when(inner)
        def _():
            hop(k, 0, 6, 1, facing)

    def pair_out(k):
        got(k, 2)
        hop(k, 2, 3, 0, ynb)

        @pl.when(inner)
        def _():
            hop(k, 2, 4, 1, facing)

        share(k, 2)
        take(k, 1)

    def side_out():
        @pl.when(inner)
        def _():
            hop(0, 1, 7, 1, facing)
            hop(1, 1, 7, 1, facing)

    def half(part, slot):
        return tc.at[1, pl.ds(part * (groups // 2), groups // 2), span(slot, count)]

    def half_copy(part, slot, there, mark, ep_to):
        return remote(half(part, slot), half(part, there), g_send.at[0], g_recv.at[1, mark], ep_to, dp)

    def last_pass():
        @pl.when(outer)
        def _():
            got(1, 6)
            half_copy(0, 6, 7, 7, ynb).start()
            share(1, 6)

    def last_take():
        @pl.when(inner)
        def _():
            got(1, 5)
            half_copy(1, 5, 7, 0, znb).start()

        @pl.when(outer)
        def _():
            half_copy(0, 7, 7, 7, ynb).wait_recv()
            half_copy(1, 7, 7, 0, znb).wait_recv()

        share(1, far + 1)

    def take_side(k):
        got(k, near + 1)
        share(k, near + 1)

    def facing_out(k):
        @pl.when(inner)
        def _():
            got(k, 2)
            hop(k, 2, 4, 1, facing)

    def diag_out(k):
        @pl.when(outer)
        def _():
            got(k, 2)

        got(k, 1)
        hop(k, 1, 3, 0, znb)

    def inner_pass(k, slot, sideways=True):
        @pl.when(inner)
        def _():
            got(k, slot)
            hop(k, slot, 10 - slot, 1, znb)
            if sideways:
                hop(k, slot, slot + 1, 1, ynb)
            share(k, slot)

    def outer_pass(k, slot, sideways=True):
        @pl.when(outer)
        def _():
            got(k, slot)
            if sideways:
                hop(k, slot, slot + 1, 1, ynb)
            share(k, slot)

    pltpu.make_async_copy(view(0, 0), view(0, 0), l_sem.at[0]).wait()
    own_out(0)
    share(0, 0, True)
    wd[...] = jnp.zeros(wd.shape, f32)
    rs[...] = jnp.zeros(rs.shape, f32)
    for load in lists:
        load.wait()
    ids = ids_ref[...]
    values = rw_ref[...].astype(f32)
    for e in range(ep_size):
        line = jnp.sum(jnp.where(ids == e, values, 0.0), axis=0, keepdims=True)
        wd[e, :, 0:count] = jnp.broadcast_to(line, (wd.shape[1], count))
    for s in range(1, 8):
        remote(wd.at[targets[s]], wbuf.at[s], w_sem.at[0], w_sem.at[1 if s < lead else 2], targets[s], dp).start()
    keep_w = pltpu.make_async_copy(wd.at[ep], wbuf.at[0], w_sem.at[1])
    keep_w.start()
    pltpu.make_async_copy(view(1, 0), view(1, 0), l_sem.at[1]).wait()
    own_out(1)
    share(1, 0, True)

    def wave_rows(wave):
        return pl.ds(starts[wave] * count, sizes[wave] * count)

    def gate_step(wave):
        block = wave_rows(wave)
        half = sizes[wave] * count

        def step(t, carry):
            lanes = span(t, ft)
            gate_pre = jnp.zeros((half, ft), f32)
            up_pre = jnp.zeros((half, ft), f32)
            for j in range(groups):
                depth = pl.ds(j * col, col)
                gate_pre += jnp.dot(tc[0, j, block], wg[depth, lanes], preferred_element_type=f32)
                up_pre += jnp.dot(tc[0, j, block], wu[depth, lanes], preferred_element_type=f32)
            act, slope = silu_parts(gate_pre)
            product = act * up_pre
            weight = wcol[block, 0:1]
            hw_own[t, block] = (weight * product).astype(bf16)
            act_buf[t, block] = act
            fac_buf[t, block] = up_pre * slope
            hid_buf[t, block] = product.astype(bf16)
            for r in (1, 0):
                done = h_done.at[1 + wave] if r == 1 else h_done.at[0]
                remote(
                    hw_own.at[t, block], hw_recv.at[r, t, block], h_send.at[0], done, ep, peers_dp[r]
                ).start()
            return carry

        lax.fori_loop(0, tiles, step, 0)

    def back_step(wave):
        block = wave_rows(wave)
        weight = wcol[block, 0:1]
        half = sizes[wave] * count

        def step(t, route):
            back = jnp.zeros((half, ft), f32)
            for j in range(groups):
                back += jnp.dot(tc[1, j, block], wdt[pl.ds(j * col, col), span(t, ft)], preferred_element_type=f32)
            scaled = weight * back
            gp_own[t, 0, block] = (scaled * fac_buf[t, block]).astype(bf16)
            gp_own[t, 1, block] = (scaled * act_buf[t, block]).astype(bf16)
            route = route + jnp.sum(hid_buf[t, block].astype(f32) * back, axis=1, keepdims=True)
            for r in (1, 0):
                done = h_done.at[(5 + wave) + wave * t] if r == 1 else h_done.at[4]
                remote(
                    gp_own.at[t, :, block], gp_recv.at[r, t, :, block], h_send.at[1], done, ep, peers_dp[r]
                ).start()
            return route

        route = lax.fori_loop(0, tiles, step, jnp.zeros((half, 1), f32))
        lined = jnp.broadcast_to(route, (half, 128)).T
        for p in range(sizes[wave]):
            line = lined[0:1, p * count:(p + 1) * count]
            rs[starts[wave] + p, :, 0:count] = jnp.broadcast_to(line, (rs.shape[1], count))

    def fold_send(n, mode, phase):
        place = pl.ds(early * phase, early + (4 - 2 * early) * phase)
        done = f_sem.at[1 + phase * (1 + n)]
        to = ynb + mode * (znb - ynb)
        return remote(fs.at[n, place], fr.at[n, place], f_sem.at[0], done, to, dp)

    def fold_rows(n, mode, phase):
        for j in ((range(early), range(early, 4))[phase]):
            source = 2 * j + 1 + mode * (1 - j % 2)
            fs[n, j] = part[n, source].astype(bf16)

    def slot_step(wave):
        block = wave_rows(wave)
        size = sizes[wave]

        def step(turn, carry):
            n = turn % 2 * (groups // 2) + turn // 2
            total = jnp.zeros((size * count, col), f32)
            for t in range(tiles):
                depth = pl.ds(t * ft, ft)
                if wave == 0:
                    total += lax.dot_general(
                        gp_own[t, 0, block], wg[span(n, col), depth], contract_last, preferred_element_type=f32
                    )
                    total += lax.dot_general(
                        gp_own[t, 1, block], wu[span(n, col), depth], contract_last, preferred_element_type=f32
                    )
                else:
                    total += jnp.dot(gp_own[t, 0, block], wgt[depth, span(n, col)], preferred_element_type=f32)
                    total += jnp.dot(gp_own[t, 1, block], wut[depth, span(n, col)], preferred_element_type=f32)
            part[n, pl.ds(starts[wave], size)] = total.reshape(size, count, col)
            mode = n // along_y
            fold_rows(n, mode, wave)
            if wave == 1:
                fold_send(n, mode, 1).start()
            return carry

        lax.fori_loop(0, groups, step, 0)

    def fold_early(where):
        @pl.when(where)
        def _():
            def step(n, carry):
                fold_send(n, n // along_y, 0).start()
                return carry

            lax.fori_loop(0, groups, step, 0)

    def fold_ready():
        ref = fr.at[:, pl.ds(0, early)]
        remote(ref, ref, f_sem.at[0], f_sem.at[1], ynb, dp).wait_recv()

    def fold_mid(n):
        mode = n // along_y
        fold_send(n, mode, 1).wait_recv()
        bs[n, 0] = (part[n, 2 - mode] + fr[n, 1].astype(f32)).astype(bf16)
        bs[n, 1] = (part[n, 6 - mode] + fr[n, 3].astype(f32)).astype(bf16)
        remote(bs.at[n], br.at[n], f_sem.at[0], b_sem.at[n], (znb, ynb)[mode], dp).start()

    def fold_cross(n):
        remote(bs.at[n], br.at[n], f_sem.at[0], b_sem.at[n], znb, dp).wait_recv()
        xs[n] = (part[n, 4] + fr[n, 2].astype(f32) + br[n, 1].astype(f32)).astype(bf16)
        remote(xs.at[n], xr.at[n], f_sem.at[0], x_sem.at[0], twin, dp).start()

    def pass_hidden(wave):
        block = wave_rows(wave)
        ref = hw_recv.at[1, :, block]
        remote(ref, ref, h_send.at[0], h_done.at[1 + wave], ep, peers_dp[1]).wait_recv()
        remote(ref, hw_recv.at[2, :, block], h_send.at[0], h_done.at[0], ep, peers_dp[0]).start()

    def pass_grad_first():
        ref = gp_recv.at[1, :, :, wave_rows(0)]
        remote(ref, ref, h_send.at[1], h_done.at[5], ep, peers_dp[1]).wait_recv()
        remote(ref, gp_recv.at[2, :, :, wave_rows(0)], h_send.at[1], h_done.at[6 + tiles], ep, peers_dp[0]).start()

    def pass_grad(t):
        ref = gp_recv.at[1, t, :, wave_rows(1)]
        remote(ref, ref, h_send.at[1], h_done.at[6 + t], ep, peers_dp[1]).wait_recv()
        remote(
            ref, gp_recv.at[2, t, :, wave_rows(1)], h_send.at[1], h_done.at[7 + tiles + t], ep, peers_dp[0]
        ).start()

    def take_weights(wave):
        start, size = starts[wave], sizes[wave]
        ref = wbuf.at[pl.ds(start, size)]
        remote(ref, ref, w_sem.at[0], w_sem.at[1 + wave], ynb, dp).wait_recv()
        step = wbuf.shape[1]
        flat = wbuf[start:start + size].reshape(size * step, wbuf.shape[2])
        turned = jnp.concatenate([flat, jnp.zeros((128 - size * step, wbuf.shape[2]), f32)], axis=0).T
        for p in range(size):
            line = turned[0:count, p * step:p * step + 1]
            wcol[pl.ds((start + p) * count, count), :] = jnp.broadcast_to(line, (count, 128))

    def turn_down():
        def step(t, carry):
            for j in range(groups):
                wdt[pl.ds(j * col, col), span(t, ft)] = wdn[span(t, ft), pl.ds(j * col, col)].T
            return carry

        lax.fori_loop(0, tiles, step, 0)

    def turn_up():
        def step(n, carry):
            for t in range(tiles):
                wgt[pl.ds(t * ft, ft), span(n, col)] = wg[span(n, col), pl.ds(t * ft, ft)].T
                wut[pl.ds(t * ft, ft), span(n, col)] = wu[span(n, col), pl.ds(t * ft, ft)].T
            return carry

        lax.fori_loop(0, groups, step, 0)

    w_loads[2].wait()
    turn_down()
    pair_out(0)
    for load in w_loads[0:2]:
        load.wait()
    take_weights(0)
    gate_step(0)
    inner_pass(0, near, False)
    pair_out(1)
    side_out()
    back_step(0)
    inner_pass(0, far)
    slot_step(0)
    inner_pass(1, near, False)
    inner_pass(1, far)
    ref = cols.at[1, pl.ds(1, 2), pl.ds(0, count)]
    remote(ref, ref, c_send.at[0], c_recv.at[2], ep, peers_dp[1]).wait_recv()
    @pl.when(outer)
    def _():
        own_out(2)

    outer_pass(0, near)
    turn_up()
    facing_out(2)
    outer_pass(0, far)
    if lead == 3:
        take(0, 3)
    take_side(0)
    outer_pass(1, near)
    last_pass()
    take(0, far + 1)
    take_weights(1)
    gate_step(1)
    fold_early(outer)
    pass_hidden(0)
    if lead == 3:
        take(1, 3)
    take_side(1)
    last_take()

    @pl.when(inner)
    def _():
        own_out(2)

    fold_early(inner)
    back_step(1)
    diag_out(2)
    inner_pass(2, near)
    inner_pass(2, far)
    slot_step(1)
    for s in range(1, 8):
        remote(rs.at[s], rr.at[ep], r_sem.at[0], r_sem.at[1], targets[s], dp).start()
    pltpu.make_async_copy(rs.at[0], rr.at[ep], r_sem.at[1]).start()
    outer_pass(2, near)
    outer_pass(2, far)
    pass_grad_first()
    fold_ready()
    fold_mid(0)
    fold_mid(2)
    remote(cols.at[0], cols.at[0], c_send.at[0], c_recv.at[0], ep, peers_dp[0]).wait_recv()
    colst[0] = tc[0, dp].T
    for r in range(3):
        colst[1 + r] = cols[0, r].T
    fold_mid(1)
    fold_mid(3)
    pass_hidden(1)
    remote(cols.at[1, 0], cols.at[1, 0], c_send.at[0], c_recv.at[1], ep, peers_dp[0]).wait_recv()
    remote(gp_recv.at[0], gp_recv.at[0], h_send.at[1], h_done.at[4], ep, peers_dp[0]).wait_recv()
    ref = gp_recv.at[2, :, :, wave_rows(0)]
    remote(ref, ref, h_send.at[1], h_done.at[6 + tiles], ep, peers_dp[0]).wait_recv()

    def down_tile(t):
        blocks = [hw_own.at[t]] + [hw_recv.at[r, t] for r in range(3)]
        cots = [tc.at[1, dp]] + [cols.at[1, r] for r in range(3)]
        grad_down = jnp.zeros((ft, col), f32)
        for g in range(4):
            grad_down += lax.dot_general(blocks[g][...], cots[g][...], contract_first, preferred_element_type=f32)
        gd_ref[span(t, ft), :] = grad_down.astype(bf16)

    def sum_all():
        remote(xs, xr, f_sem.at[0], x_sem.at[0], twin, dp).wait_recv()

        def step(n, carry):
            total = part[n, 0] + fr[n, 0].astype(f32) + br[n, 0].astype(f32) + xr[n].astype(f32)
            gt_ref[:, span(n, col)] = total.astype(bf16)
            return carry

        lax.fori_loop(0, groups, step, 0)

    def weight_tile(t):
        ref = gp_recv.at[2, t, :, wave_rows(1)]
        remote(ref, ref, h_send.at[1], h_done.at[7 + tiles + t], ep, peers_dp[0]).wait_recv()
        blocks = [gp_own.at[t]] + [gp_recv.at[r, t] for r in range(3)]
        grad_gate = jnp.zeros((col, ft), f32)
        grad_up = jnp.zeros((col, ft), f32)
        for g in range(4):
            grad_gate += jnp.dot(colst[g], blocks[g][0], preferred_element_type=f32)
            grad_up += jnp.dot(colst[g], blocks[g][1], preferred_element_type=f32)
        gg_ref[:, span(t, ft)] = grad_gate.astype(bf16)
        gu_ref[:, span(t, ft)] = grad_up.astype(bf16)

    def down_ready():
        got(2, 3)
        got(2, near + 1)
        got(2, far + 1)
        ref = hw_recv.at[pl.ds(0, 2)]
        remote(ref, ref, h_send.at[0], h_done.at[0], ep, peers_dp[0]).wait_recv()

    pass_grad(0)
    fold_cross(0)
    fold_cross(2)
    fold_cross(1)
    fold_cross(3)
    for t in range(1, tiles - 1):
        pass_grad(t)
    weight_tile(0)
    down_ready()
    for t in range(tiles):
        down_tile(t)
    pass_grad(tiles - 1)
    for t in range(1, tiles):
        weight_tile(t)
    sum_all()

    remote(rr, rr, r_sem.at[0], r_sem.at[1], ynb, dp).wait_recv()
    table = jnp.zeros(ids.shape, f32)
    for e in range(ep_size):
        table = table + jnp.where(ids == e, rr[e, 0:1, 0:count], 0.0)
    route_ref[...] = table.astype(bf16)

    def sent(ref, sem):
        remote(ref, ref, sem, r_sem.at[1], ynb, dp).wait_send()

    sent(rs.at[pl.ds(0, ep_size - 1)], r_sem.at[0])
    sent(wd.at[pl.ds(0, ep_size - 1)], w_sem.at[0])
    sent(wdn.at[pl.ds(0, (7 * groups * count * col) // model)], f_sem.at[0])
    unit = (groups * count * col) // model

    @pl.when(inner)
    def _():
        sent(wdn.at[pl.ds(0, 18 * unit + 10 * unit // 2)], g_send.at[0])

    @pl.when(outer)
    def _():
        sent(wdn.at[pl.ds(0, 10 * unit + 4 * unit // 2)], g_send.at[0])

    sent(wdn.at[pl.ds(0, (34 * count * col) // model)], c_send.at[0])
    sent(hw_recv, h_send.at[0])
    sent(gp_recv, h_send.at[1])


def store_kernel(*refs):
    sems = refs[-1]
    each = (len(refs) - 1) // 2
    copies = []
    for k in range(each):
        size = refs[k].shape[0]
        pieces = store_pieces if size % (16 * store_pieces) == 0 else 1
        step = size // pieces
        for p in range(pieces):
            place = pl.ds(p * step, step)
            copies.append(pltpu.make_async_copy(refs[k].at[place], refs[each + k].at[place], sems.at[k]))
    for copy in copies:
        copy.start()
    for k in range(each):
        pltpu.make_async_copy(refs[k], refs[each + k], sems.at[k]).wait()


def fused_body(tokens, cotangent, expert_ids, route_weights, w_gate, w_up, w_down):
    count, topk = expert_ids.shape
    model = tokens.shape[1]
    experts = lax.axis_size("ep")
    groups = lax.axis_size("dp")
    width = w_gate.shape[2]
    rows = experts * count
    col = model // groups
    ft = 256 if width % 256 == 0 else width
    tiles = width // ft
    lanes = 128
    bf16 = jnp.bfloat16
    f32 = jnp.float32
    any_spec = pl.BlockSpec(memory_space=pl.ANY)
    hbm = pl.BlockSpec(memory_space=pltpu.HBM)
    vmem = pl.BlockSpec(memory_space=pltpu.VMEM)
    dma = pltpu.SemaphoreType.DMA
    small = (experts, 8, lanes)
    shapes = ((count, model), (topk, count), (col, width), (col, width), (width, col))
    outs = pl.pallas_call(
        fused_kernel,
        name="fused_layer",
        out_shape=tuple(pltpu.VMEM(shape, bf16) for shape in shapes),
        in_specs=[hbm] * 7,
        out_specs=(vmem,) * 5,
        scratch_shapes=[
            pltpu.VMEM((topk, count), jnp.int32),
            pltpu.VMEM((topk, count), bf16),
            pltpu.VMEM((model, width), bf16),
            pltpu.VMEM((model, width), bf16),
            pltpu.VMEM((width, model), bf16),
            pltpu.VMEM((width, model), bf16),
            pltpu.VMEM((width, model), bf16),
            pltpu.VMEM((model, width), bf16),
            pltpu.VMEM((2, groups, rows, col), bf16),
            pltpu.VMEM(small, f32),
            pltpu.VMEM(small, f32),
            pltpu.VMEM((rows, lanes), f32),
            pltpu.VMEM((2, 3, rows, col), bf16),
            pltpu.VMEM((4, col, rows), bf16),
            pltpu.VMEM((tiles, rows, ft), f32),
            pltpu.VMEM((tiles, rows, ft), f32),
            pltpu.VMEM((tiles, rows, ft), bf16),
            pltpu.VMEM((tiles, rows, ft), bf16),
            pltpu.VMEM((3, tiles, rows, ft), bf16),
            pltpu.VMEM((tiles, 2, rows, ft), bf16),
            pltpu.VMEM((3, tiles, 2, rows, ft), bf16),
            pltpu.VMEM((groups, 8, count, col), f32),
            pltpu.VMEM((groups, 4, count, col), bf16),
            pltpu.VMEM((groups, 4, count, col), bf16),
            pltpu.VMEM((groups, 2, count, col), bf16),
            pltpu.VMEM((groups, 2, count, col), bf16),
            pltpu.VMEM((groups, count, col), bf16),
            pltpu.VMEM((groups, count, col), bf16),
            pltpu.VMEM(small, f32),
            pltpu.VMEM(small, f32),
            dma((7,)),
            dma((3,)),
            dma((1,)),
            dma((3, experts)),
            dma((1,)),
            dma((3,)),
            dma((2,)),
            dma((7 + 2 * tiles,)),
            dma((2 + groups,)),
            dma((groups,)),
            dma((1,)),
            dma((2,)),
        ],
        compiler_params=pltpu.CompilerParams(
            collective_id=0, has_side_effects=True, vmem_limit_bytes=64200000
        ),
    )(tokens, cotangent, expert_ids.T, route_weights.T, w_gate[0], w_up[0], w_down[0])
    outs = pl.pallas_call(
        store_kernel,
        name="store_results",
        out_shape=tuple(jax.ShapeDtypeStruct(shape, bf16) for shape in shapes),
        in_specs=[any_spec] * 5,
        out_specs=(any_spec,) * 5,
        scratch_shapes=[dma((5,))],
        compiler_params=pltpu.CompilerParams(vmem_limit_bytes=4 * 1024 * 1024),
    )(*outs)
    grad_tokens, grad_route, grad_gate, grad_up, grad_down = outs
    return grad_tokens, grad_route.T, grad_gate[None], grad_up[None], grad_down[None]


def body(tokens, cotangent, expert_ids, route_weights, w_gate, w_up, w_down):
    tok_count, topk = expert_ids.shape
    experts = lax.axis_size("ep")
    whole = 2 * tok_count * topk // experts >= tok_count
    width = w_gate.shape[2]
    paired = lax.axis_size("dp") == 4 and experts == 8 and tok_count == 32
    paired = paired and width % 256 == 0 and width >= 24 * tok_count
    chosen = fused_body if whole and paired else routed_body
    return chosen(tokens, cotangent, expert_ids, route_weights, w_gate, w_up, w_down)


def solution(mesh):
    return jax.shard_map(
        body,
        mesh=mesh,
        in_specs=(
            P(("ep", "dp"), None),
            P(("ep", "dp"), None),
            P(("ep", "dp"), None),
            P(("ep", "dp"), None),
            P("ep", None, None),
            P("ep", None, None),
            P("ep", None, None),
        ),
        out_specs=(
            P(("ep", "dp"), None),
            P(("ep", "dp"), None),
            P("ep", "dp", None),
            P("ep", "dp", None),
            P("ep", None, "dp"),
        ),
        check_vma=False,
    )
```
